32 devices in a mesh: ctx: 8 (over y, x, core), wsh: 4 (over z).
Axes of the slice: x: 2, y: 2, z: 4, core: 2. Of those that a mesh axis runs over, the one named last changes fastest.
Arguments:
- layer_input: bfloat16 [12, 1024, 1472], P('wsh', 'ctx'), may hold values from -6 to 6
- segments: int32 [12, 1024], P('wsh', 'ctx'), may hold values from 0 to 3, never falling along the last dimension, each value on 1 to 512 neighbouring positions
- cotangent: bfloat16 [12, 1024, 1472], P('wsh', 'ctx'), may hold values from -6 to 6
- query_weight: bfloat16 [1472, 384], P('wsh'), may hold values from -0.15625 to 0.15625
- key_weight: bfloat16 [1472, 384], P('wsh'), may hold values from -0.0390625 to 0.0390625
- value_weight: bfloat16 [1472, 384], P('wsh'), may hold values from -0.15625 to 0.15625
- projection: bfloat16 [384, 1472], P('wsh'), may hold values from -1.25 to 1.25
- gate_weight: bfloat16 [1472, 3584], P('wsh'), may hold values from -0.15625 to 0.15625
- up_weight: bfloat16 [1472, 3584], P('wsh'), may hold values from -0.15625 to 0.15625
- down_weight: bfloat16 [3584, 1472], P('wsh'), may hold values from -0.09375 to 0.09375
- gain_early: bfloat16 [1472], P('wsh'), may hold values from 0.099609375 to 1.8984375
- gain_late: bfloat16 [1472], P('wsh'), may hold values from 0.099609375 to 1.8984375
- bias_table: bfloat16 [32, 6], P('wsh'), may hold values from -4 to 4
Outputs:
- layer_output: bfloat16 [12, 1024, 1472], P('wsh', 'ctx')
- input_grad: bfloat16 [12, 1024, 1472], P('wsh', 'ctx')
- query_grad: float32 [1472, 384], P('wsh')
- key_grad: float32 [1472, 384], P('wsh')
- value_grad: float32 [1472, 384], P('wsh')
- projection_grad: float32 [384, 1472], P('wsh')
- gate_grad: float32 [1472, 3584], P('wsh')
- up_grad: float32 [1472, 3584], P('wsh')
- down_grad: float32 [3584, 1472], P('wsh')
- early_grad: float32 [1472], P('wsh')
- late_grad: float32 [1472], P('wsh')
- table_grad: float32 [32, 6], P('wsh')
The draws below stay inside these ranges and needn't reach their ends.
Inputs may be any that keep to these rules, and one draw needn't show every extreme that they name: `segments`: document numbers never fall along a sequence; no document has more than 512 tokens, and some document has exactly that many.
All inputs are finite; a program needn't handle non-finite values.
Results may differ from the reference program's by a relative error of at most 0.02.
Values may be sent and summed in bfloat16 or wider, within the bound.
No kernel may reach another device: no remote copies, remote signals or barrier semaphores. Data moves between devices by JAX's collectives and lax.ppermute only.
A program may use at most 256 MiB of HBM per device.

```python
import math
import jax
import jax.numpy as jnp
import numpy as np
from jax import lax

D = 1472
HEADS = 6
DKV = 64
FF = 3584
BUCKETS = 32
INNER = 384
LEN = 1024
SEQS = 12
NSEG = 4
DOC_MOST = 512


def shard_levels(key, extent, cuts, least, high):
    level = 1.0
    for dim, parts in cuts:
        draws = jax.random.uniform(jax.random.fold_in(jax.random.fold_in(key, 6), dim), (parts,), jnp.float32, least / len(cuts), high / len(cuts))
        level = level * jnp.repeat(jnp.exp(draws), extent[dim] // parts).reshape((-1,) + (1,) * (len(extent) - 1 - dim))
    return level


def profile(number_of, total, limit, lean):
    weights = [(1 << 20) // math.isqrt(standing ** lean) + 1 for standing in range(2, number_of + 1)]
    surplus, counts = total - limit - (number_of - 1), [1] * (number_of - 1)
    while surplus > 0:
        movable = [i for i in range(number_of - 1) if counts[i] < limit]
        whole, remaining = sum([weights[i] for i in movable]), surplus
        for i in movable:
            extra = min(limit - counts[i], max(1, remaining * weights[i] // whole), surplus)
            counts[i] = counts[i] + extra
            surplus = surplus - extra
    return np.array([limit] + counts)


def uneven(rng, count, total, reach, skew):
    if count == 2:
        one = jax.random.randint(rng, (), max(1, total - reach), min(reach, total - 1) + 1)
        return jnp.stack([one, total - one])
    lengths = jnp.asarray(profile(count, total, reach, skew), jnp.int32)
    pairs = (count - 1) // 2
    giver, receiver = lengths[1:1 + 2 * pairs:2], lengths[2:2 + 2 * pairs:2]
    slack = jnp.minimum(giver - 1, reach - receiver)
    shifted = jax.random.randint(jax.random.fold_in(rng, 1), (pairs,), 0, 1 << 20) % (slack + 1)
    lengths = lengths.at[1:1 + 2 * pairs:2].set(giver - shifted).at[2:2 + 2 * pairs:2].set(receiver + shifted)
    return lengths[jax.random.permutation(jax.random.fold_in(rng, 2), count)]


def centred(key, extent, width, reach, cuts=(), held_as=jnp.bfloat16):
    entries = jax.random.normal(key, extent, jnp.float32) * width
    if len(cuts) > 0:
        entries = shard_levels(key, extent, cuts, -0.22, 0.18) * entries
    return jnp.clip(entries, min=-reach, max=reach).astype(held_as)


def setup_inputs(seed: int = 0) -> dict:
    keys = jax.random.split(jax.random.key(seed), 14)
    return {
        "layer_input": centred(keys[0], (SEQS, LEN, D), 1.0, 6.0, ((0, 4), (1, 8))),
        "segments": jax.vmap(lambda own: jnp.searchsorted(jnp.cumsum(uneven(own, NSEG, LEN, DOC_MOST, 2)), jnp.arange(LEN), side="right"))(jax.random.split(keys[1], SEQS)).reshape((SEQS, LEN)).astype(jnp.int32),
        "cotangent": centred(keys[2], (SEQS, LEN, D), 1.0, 6.0, ((0, 4), (1, 8))),
        "query_weight": centred(keys[3], (D, INNER), D ** -0.5, 0.15625, ((0, 4),)),
        "key_weight": centred(keys[4], (D, INNER), (16 * D) ** -0.5, 0.0390625, ((0, 4),)),
        "value_weight": centred(keys[5], (D, INNER), D ** -0.5, 0.15625, ((0, 4),)),
        "projection": centred(keys[6], (INNER, D), (INNER // 16) ** -0.5, 1.25, ((0, 4),)),
        "gate_weight": centred(keys[7], (D, FF), D ** -0.5, 0.15625, ((0, 4),)),
        "up_weight": centred(keys[8], (D, FF), D ** -0.5, 0.15625, ((0, 4),)),
        "down_weight": centred(keys[9], (FF, D), FF ** -0.5, 0.09375, ((0, 4),)),
        "gain_early": jnp.clip(1.0 + 0.18 * jax.random.normal(keys[10], (D,), jnp.float32), 0.099609375, 1.8984375).astype(jnp.bfloat16),
        "gain_late": jnp.clip(1.0 + 0.18 * jax.random.normal(keys[11], (D,), jnp.float32), 0.099609375, 1.8984375).astype(jnp.bfloat16),
        "bias_table": centred(keys[12], (BUCKETS, HEADS), 1.0, 4.0, ((0, 4),)),
    }


@jax.custom_vjp
def low(v):
    return lax.optimization_barrier(v.astype(jnp.bfloat16)).astype(jnp.float32)

@jax.custom_vjp
def low_back(v):
    return v

def low_keep(v):
    return (low(v), None)

def low_pass(kept, grad):
    return (grad,)

def back_keep(v):
    return (v, None)

def back_low(kept, grad):
    return (low(grad),)
low.defvjp(low_keep, low_pass)
low_back.defvjp(back_keep, back_low)
EPSILON = 1e-06
NEGATIVE = -1e+30
PRECISE = lax.Precision.HIGHEST
BUCKET_EDGES = (12, 16, 23, 32, 46, 64, 91)

def bucket_of(offsets):
    distance = jnp.abs(offsets)
    coarse = 8 + sum(((distance >= boundary).astype(jnp.int32) for boundary in BUCKET_EDGES))
    bucket_level = jnp.where(distance < 8, distance, coarse)
    return bucket_level + jnp.where(offsets > 0, 16, 0)

def rms_scale(hidden, gain_vector):
    return hidden * lax.rsqrt(lax.optimization_barrier(jnp.mean(hidden * hidden, axis=-1, keepdims=True)) + EPSILON) * gain_vector

def product(left_side, right_side):
    return jnp.dot(left_side, right_side, precision=PRECISE, preferred_element_type=jnp.float32)

def gated(gate_values, up_values):
    return jax.nn.gelu(gate_values, approximate=True) * up_values

def encoder_layer(hidden_in, query_weight, key_weight, value_weight, projection, gate_weight, up_weight, down_weight, gain_early, gain_late, bias_table, segment_ids):
    normed = low(rms_scale(hidden_in, gain_early))
    queries = low(low_back(product(normed, query_weight))).reshape(LEN, HEADS, DKV)
    key_rows = low(low_back(product(normed, key_weight))).reshape(LEN, HEADS, DKV)
    value_rows = low(low_back(product(normed, value_weight))).reshape(LEN, HEADS, DKV)
    places = jnp.arange(LEN, dtype=jnp.int32)
    rows_block = min(512, LEN)

    def attend(block_index):
        first_row = block_index * rows_block
        query_block = lax.dynamic_slice_in_dim(queries, first_row, rows_block, 0)
        query_segs = lax.dynamic_slice_in_dim(segment_ids, first_row, rows_block, 0)
        offsets = places[None, :] - (first_row + jnp.arange(rows_block, dtype=jnp.int32))[:, None]
        bias_terms = jnp.transpose(jnp.take(bias_table, bucket_of(offsets), axis=0), (2, 0, 1))
        raw_scores = low_back(jnp.einsum('ihd,jhd->hij', query_block, key_rows, precision=PRECISE))
        allowed = (query_segs[:, None] == segment_ids[None, :])[None]
        scores = jnp.where(allowed, raw_scores + bias_terms, NEGATIVE)
        soft_probs = jax.nn.softmax(scores, axis=-1)
        return jnp.einsum('hij,jhd->ihd', low(soft_probs), value_rows, precision=PRECISE)
    blocks = lax.map(jax.checkpoint(attend), jnp.arange(LEN // rows_block, dtype=jnp.int32))
    attention = low(low_back(blocks.reshape(LEN, HEADS * DKV)))
    after_attn = hidden_in + low_back(product(attention, projection))
    normed_late = low(rms_scale(after_attn, gain_late))
    gate_pre = low_back(product(normed_late, gate_weight))
    up_pre = low_back(product(normed_late, up_weight))
    activation = low(gated(gate_pre, up_pre))
    return after_attn + low_back(product(activation, down_weight))

def reference(layer_input, segments, cotangent, query_weight, key_weight, value_weight, projection, gate_weight, up_weight, down_weight, gain_early, gain_late, bias_table):
    weights = tuple((weight.astype(jnp.float32) for weight in (query_weight, key_weight, value_weight, projection, gate_weight, up_weight, down_weight, gain_early, gain_late, bias_table)))

    def per_sequence(totals, sequence_item):
        inputs_one, segs_one, grads_one = sequence_item

        def apply_layer(hidden_in, *params):
            return encoder_layer(hidden_in, *params, segs_one)
        result, pullback = jax.vjp(apply_layer, inputs_one.astype(jnp.float32), *weights)
        grad_parts = pullback(grads_one.astype(jnp.float32))
        new_totals = tuple((total + part for total, part in zip(totals, grad_parts[1:])))
        return (new_totals, (result.astype(jnp.bfloat16), grad_parts[0].astype(jnp.bfloat16)))
    zero_grads = tuple((jnp.zeros(weight.shape, jnp.float32) for weight in weights))
    totals, stacked = lax.scan(per_sequence, zero_grads, (layer_input, segments, cotangent))
    return (stacked[0], stacked[1], totals[0], totals[1], totals[2], totals[3], totals[4], totals[5], totals[6], totals[7], totals[8], totals[9])
```

```python
import functools

import jax
import jax.numpy as jnp
import numpy as np
from jax import lax
from jax.experimental import pallas as pl
from jax.experimental.pallas import tpu as pltpu
from jax.sharding import PartitionSpec as P

BUCKETS = 32
GROUP = 8
EPSILON = 1e-06
NEGATIVE = -1e30
PRECISE = lax.Precision.HIGHEST
BUCKET_EDGES = (12, 16, 23, 32, 46, 64, 91)
FLOAT = jnp.float32
BFLOAT = jnp.bfloat16


def bucket_number(offset):
    distance = abs(offset)
    level = distance if distance < 8 else 8 + sum(distance >= edge for edge in BUCKET_EDGES)
    return level + (16 if offset > 0 else 0)


def bucket_of(offsets):
    distance = jnp.abs(offsets)
    coarse = 8 + sum(((distance >= boundary).astype(jnp.int32) for boundary in BUCKET_EDGES))
    level = jnp.where(distance < 8, distance, coarse)
    return level + jnp.where(offsets > 0, 16, 0)


def near_radius(rows):
    return -(-(BUCKET_EDGES[-1] - 1) // rows)


def tile_offsets(block_gap, rows):
    keys = lax.broadcasted_iota(jnp.int32, (rows, rows), 0)
    queries = lax.broadcasted_iota(jnp.int32, (rows, rows), 1)
    return block_gap * rows + keys - queries


def tile_buckets(block_gap, rows):
    low, high = block_gap * rows - (rows - 1), block_gap * rows + (rows - 1)
    return sorted({bucket_number(offset) for offset in range(low, high + 1)})


def nt(left, right):
    return lax.dot_general(left, right, (((1,), (1,)), ((), ())), preferred_element_type=FLOAT)


def tn(left, right):
    return lax.dot_general(left, right, (((0,), (0,)), ((), ())), preferred_element_type=FLOAT)


def block_number(meta, half, position):
    low = lax.rem(meta, GROUP)
    return (position // 4) * GROUP + lax.bitwise_xor(low, jnp.int32(2 * (position % 4) + half))


def tile_index(meta, half, position, radius):
    gap = block_number(meta, half, position) - meta
    return jnp.clip(gap, -(radius + 1), radius + 1) + radius + 1


def build_bias(bias_ref, table_ref, pair, rows, radius):
    for side, bucket in ((0, 15), (2 * radius + 2, 31)):
        for head in range(2):
            bias_ref[head, side] = jnp.full((rows, rows), table_ref[bucket, 2 * pair + head], FLOAT)
    for gap in range(-radius, radius + 1):
        buckets = bucket_of(tile_offsets(gap, rows))
        present = tile_buckets(gap, rows)
        tiles = [jnp.full((rows, rows), table_ref[present[0], 2 * pair + head], FLOAT) for head in range(2)]
        for bucket in present[1:]:
            hit = buckets == bucket
            tiles = [jnp.where(hit, table_ref[bucket, 2 * pair + head], tiles[head]) for head in range(2)]
        for head in range(2):
            bias_ref[head, gap + radius + 1] = tiles[head]


def build_mask(mask_ref, segs_ref, meta, seq, rows, count):
    own = segs_ref[seq, pl.ds(meta, 1), :]
    for half in range(2):
        for position in range(count):
            row = segs_ref[seq, pl.ds(block_number(meta, half, position), 1), :]
            keys = jnp.transpose(jnp.broadcast_to(row, (rows, rows)))
            mask_ref[seq, half * count + position] = jnp.where(keys == own, 0.0, NEGATIVE)


def half_scores(keys, query, meta, head, half, seq, bias_ref, mask_ref, rows, count, radius):
    raw = nt(keys, query)
    parts = []
    for position in range(count):
        extra = bias_ref[head, tile_index(meta, half, position, radius)]
        masked = mask_ref[seq, half * count + position]
        parts.append(raw[position * rows : (position + 1) * rows] + (extra + masked))
    return jnp.concatenate(parts, axis=0)


def head_rows(value, head, lane):
    return jnp.where((lane < 64) == (head == 0), value, jnp.zeros_like(value))


def forward_kernel(
    meta_ref, table_ref, segs_ref, q_ref, ko_ref, ks_ref, vo_ref, vs_ref, out_ref, lse_ref, bias_ref, mask_ref,
    *, rows, count, radius,
):
    pair, seq = pl.program_id(0), pl.program_id(1)
    meta = meta_ref[0]

    @pl.when(seq == 0)
    def _():
        build_bias(bias_ref, table_ref, pair, rows, radius)

    @pl.when(pair == 0)
    def _():
        build_mask(mask_ref, segs_ref, meta, seq, rows, count)

    query = q_ref[0]
    lane = lax.broadcasted_iota(jnp.int32, query.shape, 1)
    keys = [ref[...].reshape(count * rows, 128) for ref in (ko_ref, ks_ref)]
    values = [ref[...].reshape(count * rows, 128) for ref in (vo_ref, vs_ref)]
    pieces = []
    for head in range(2):
        one = head_rows(query, head, lane)
        scores = [
            half_scores(keys[half], one, meta, head, half, seq, bias_ref, mask_ref, rows, count, radius)
            for half in range(2)
        ]
        top = jnp.maximum(jnp.max(scores[0], axis=0, keepdims=True), jnp.max(scores[1], axis=0, keepdims=True))
        raised = [jnp.exp(part - top) for part in scores]
        total = jnp.sum(raised[0], axis=0, keepdims=True) + jnp.sum(raised[1], axis=0, keepdims=True)
        scale = 1.0 / total
        mixed = sum(tn(values[half], (raised[half] * scale).astype(BFLOAT)) for half in range(2))
        pieces.append(mixed[64 * head : 64 * head + 64])
        lse_ref[0, 0, head : head + 1] = top + jnp.log(total)
    out_ref[0] = jnp.transpose(jnp.concatenate(pieces, axis=0))


def backward_kernel(
    meta_ref, table_ref, segs_ref, q_ref, ko_ref, ks_ref, vo_ref, vs_ref, do_ref, out_ref, lse_ref,
    dq_ref, dko_ref, dks_ref, dvo_ref, dvs_ref, tab_ref, bias_ref, mask_ref, sum_ref,
    *, rows, count, radius,
):
    pair, seq = pl.program_id(0), pl.program_id(1)
    meta = meta_ref[0]

    @pl.when(seq == 0)
    def _():
        build_bias(bias_ref, table_ref, pair, rows, radius)
        sum_ref[...] = jnp.zeros_like(sum_ref)

    @pl.when(pair == 0)
    def _():
        build_mask(mask_ref, segs_ref, meta, seq, rows, count)

    query, grad = q_ref[0], do_ref[0]
    lane = lax.broadcasted_iota(jnp.int32, query.shape, 1)
    keys = [ref[...].reshape(count * rows, 128) for ref in (ko_ref, ks_ref)]
    values = [ref[...].reshape(count * rows, 128) for ref in (vo_ref, vs_ref)]
    picks = (
        lax.broadcasted_iota(jnp.int32, (8, 128), 1) // 64 == lax.broadcasted_iota(jnp.int32, (8, 128), 0)
    ).astype(FLOAT)
    deltas = lax.dot_general(
        picks, grad.astype(FLOAT) * out_ref[0], (((1,), (1,)), ((), ())), precision=PRECISE, preferred_element_type=FLOAT
    )
    query_heads = [head_rows(query, head, lane) for head in range(2)]
    grad_heads = [head_rows(grad, head, lane) for head in range(2)]
    probs, slopes = [[], []], [[], []]
    pieces = []
    for head in range(2):
        logsum = lse_ref[0, 0, head : head + 1]
        delta = deltas[head : head + 1]
        flow = None
        for half in range(2):
            scores = half_scores(
                keys[half], query_heads[head], meta, head, half, seq, bias_ref, mask_ref, rows, count, radius
            )
            prob = jnp.exp(scores - logsum)
            slope = prob * (nt(values[half], grad_heads[head]) - delta)
            for position in range(count):
                index = tile_index(meta, half, position, radius)
                sum_ref[head, index] = sum_ref[head, index] + slope[position * rows : (position + 1) * rows]
            slope_low = slope.astype(BFLOAT)
            probs[half].append(prob.astype(BFLOAT))
            slopes[half].append(slope_low)
            term = tn(keys[half], slope_low)
            flow = term if flow is None else flow + term
        pieces.append(flow[64 * head : 64 * head + 64])
    dq_ref[0] = jnp.transpose(jnp.concatenate(pieces, axis=0)).astype(BFLOAT)
    query_stack = jnp.concatenate(query_heads, axis=0)
    grad_stack = jnp.concatenate(grad_heads, axis=0)
    for half, (dk_ref, dv_ref) in enumerate(((dko_ref, dvo_ref), (dks_ref, dvs_ref))):
        dk = jnp.dot(jnp.concatenate(slopes[half], axis=1), query_stack, preferred_element_type=FLOAT)
        dv = jnp.dot(jnp.concatenate(probs[half], axis=1), grad_stack, preferred_element_type=FLOAT)
        dk_ref[...] = dk.astype(BFLOAT).reshape(dk_ref.shape)
        dv_ref[...] = dv.astype(BFLOAT).reshape(dv_ref.shape)

    @pl.when(seq == pl.num_programs(1) - 1)
    def _():
        for head in range(2):
            sums = {}
            for side, bucket in ((0, 15), (2 * radius + 2, 31)):
                sums[bucket] = jnp.sum(sum_ref[head, side], axis=0, keepdims=True)
            for gap in range(-radius, radius + 1):
                buckets = bucket_of(tile_offsets(gap, rows))
                tile = sum_ref[head, gap + radius + 1]
                for bucket in tile_buckets(gap, rows):
                    part = jnp.sum(jnp.where(buckets == bucket, tile, 0.0), axis=0, keepdims=True)
                    sums[bucket] = sums[bucket] + part if bucket in sums else part
            for bucket in range(BUCKETS):
                tab_ref[0, head, bucket : bucket + 1] = sums.get(bucket, jnp.zeros((1, rows), FLOAT))


def attention_specs(seqs, rows, count, blocks, pairs):
    small = [
        pl.BlockSpec(memory_space=pltpu.SMEM),
        pl.BlockSpec(memory_space=pltpu.SMEM),
        pl.BlockSpec((seqs, blocks, rows), lambda p, s: (0, 0, 0)),
    ]
    query = pl.BlockSpec((1, rows, 128), lambda p, s: (s, 0, p))
    key = pl.BlockSpec((count, 1, rows, 128), lambda p, s: (0, s, 0, p))
    value = pl.BlockSpec((count, 1, rows, 128), lambda p, s: (0, s, 0, pairs + p))
    stat = pl.BlockSpec((1, 1, 8, rows), lambda p, s: (p, s, 0, 0))
    return small, query, key, value, stat


def attention_scratch(seqs, rows, count, radius):
    return [
        pltpu.VMEM((2, 2 * radius + 3, rows, rows), FLOAT),
        pltpu.VMEM((seqs, 2 * count, rows, rows), FLOAT),
    ]


def attention_cost(seqs, rows, keys, width, products):
    return pl.CostEstimate(
        flops=2 * products * seqs * rows * keys * width,
        bytes_accessed=4 * seqs * keys * width * products,
        transcendentals=seqs * rows * keys * width // 64,
    )


def attention_forward(meta, table, segs, queries, kv_own, kv_sib):
    seqs, rows, inner = queries.shape
    count, blocks, pairs = kv_own.shape[0], segs.shape[1], inner // 128
    radius = near_radius(rows)
    small, query, key, value, stat = attention_specs(seqs, rows, count, blocks, pairs)
    return pl.pallas_call(
        functools.partial(forward_kernel, rows=rows, count=count, radius=radius),
        grid=(pairs, seqs),
        in_specs=[*small, query, key, key, value, value],
        out_specs=[query, stat],
        out_shape=[
            jax.ShapeDtypeStruct((seqs, rows, inner), FLOAT),
            jax.ShapeDtypeStruct((pairs, seqs, 8, rows), FLOAT),
        ],
        scratch_shapes=attention_scratch(seqs, rows, count, radius),
        cost_estimate=attention_cost(seqs, rows, blocks * rows, inner, 2),
        name="attention_forward",
    )(meta, table, segs, queries, kv_own, kv_sib, kv_own, kv_sib)


def attention_backward(meta, table, segs, queries, kv_own, kv_sib, grad, out, lse):
    seqs, rows, inner = queries.shape
    count, blocks, pairs = kv_own.shape[0], segs.shape[1], inner // 128
    radius = near_radius(rows)
    small, query, key, value, stat = attention_specs(seqs, rows, count, blocks, pairs)
    side = jax.ShapeDtypeStruct((count, seqs, rows, inner), BFLOAT)
    return pl.pallas_call(
        functools.partial(backward_kernel, rows=rows, count=count, radius=radius),
        grid=(pairs, seqs),
        in_specs=[*small, query, key, key, value, value, query, query, stat],
        out_specs=[query, key, key, key, key, pl.BlockSpec((1, 2, BUCKETS, rows), lambda p, s: (p, 0, 0, 0))],
        out_shape=[
            jax.ShapeDtypeStruct((seqs, rows, inner), BFLOAT), side, side, side, side,
            jax.ShapeDtypeStruct((pairs, 2, BUCKETS, rows), FLOAT),
        ],
        scratch_shapes=[
            *attention_scratch(seqs, rows, count, radius),
            pltpu.VMEM((2, 2 * radius + 3, rows, rows), FLOAT),
        ],
        cost_estimate=attention_cost(seqs, rows, blocks * rows, inner, 5),
        name="attention_backward",
    )(meta, table, segs, queries, kv_own, kv_sib, kv_own, kv_sib, grad, out, lse)


def swap(value, bit):
    count = lax.axis_size("ctx")
    return lax.ppermute(value, "ctx", [(source, source ^ bit) for source in range(count)])


def gather_four(own):
    cut = own.shape[0] // 2
    first, second = swap(own, 2), swap(own, 4)
    last = jnp.concatenate((swap(first[:cut], 4), swap(second[cut:], 2)), axis=0)
    return [own, first, second, last]


def scatter_four(blocks):
    own, first, second, last = blocks
    cut = own.shape[0] // 2
    low, high = swap(last[:cut], 4), swap(last[cut:], 2)
    first = jnp.concatenate(((first[:cut].astype(FLOAT) + low.astype(FLOAT)).astype(BFLOAT), first[cut:]), axis=0)
    second = jnp.concatenate((second[:cut], (second[cut:].astype(FLOAT) + high.astype(FLOAT)).astype(BFLOAT)), axis=0)
    got_first, got_second = swap(first, 2), swap(second, 4)
    return own.astype(FLOAT) + got_first.astype(FLOAT) + got_second.astype(FLOAT)


def rms_rows(hidden, gain):
    return hidden * lax.rsqrt(jnp.mean(hidden * hidden, axis=-1, keepdims=True) + EPSILON) * gain


def rms_back(hidden, gain, back):
    scale = lax.rsqrt(jnp.mean(hidden * hidden, axis=-1, keepdims=True) + EPSILON)
    lifted = back * gain
    return scale * lifted - hidden * (scale * scale * scale) * jnp.mean(lifted * hidden, axis=-1, keepdims=True)


def ordered(blocks, low):
    stacked = jnp.stack(blocks)
    return [lax.dynamic_index_in_dim(stacked, lax.bitwise_xor(low, jnp.int32(index)), 0, keepdims=False) for index in range(GROUP)]


def gather_eight(own, low):
    four = gather_four(own)
    other = swap(jnp.stack(four), 1)
    listed = [four[index // 2] if index % 2 == 0 else other[index // 2] for index in range(GROUP)]
    return ordered(listed, low)


def slice_rows(weight, low):
    total = weight.shape[0]
    size = -(-total // (GROUP * 16)) * 16
    start = jnp.minimum(low * size, total - size)
    return lax.dynamic_slice_in_dim(weight, start, size, 0)


def join_rows(pieces, depth, total):
    size = pieces[0].shape[0] // depth
    cut = [piece.reshape(depth, size, -1) for piece in pieces]
    rows = []
    covered = 0
    for index, piece in enumerate(cut):
        start = min(index * size, total - size)
        if start + size > covered:
            rows.append(piece[:, covered - start :])
            covered = start + size
    return jnp.concatenate(rows, axis=1).reshape(depth * total, -1)


def on_device(
    layer_input,
    segments,
    cotangent,
    query_weight,
    key_weight,
    value_weight,
    projection,
    gate_weight,
    up_weight,
    down_weight,
    gain_early,
    gain_late,
    bias_table,
):
    ring = lax.axis_size("ctx")
    depth = lax.axis_size("wsh")
    groups = ring // GROUP
    mine = lax.axis_index("ctx")
    low = lax.rem(mine, GROUP)
    chip, core = low // 2, lax.rem(low, 2)
    zed = lax.axis_index("wsh")
    seqs, rows, width = layer_input.shape
    inner = query_weight.shape[1]
    heads = bias_table.shape[1]
    hidden = gate_weight.shape[1]
    shard = width // depth
    slab = hidden // depth
    part = slab // 4
    piece = part // 2
    upper = [[group * GROUP + index for group in range(groups)] for index in range(GROUP)]
    is_zero = core == 0

    qkv_shard = jnp.concatenate((query_weight, key_weight, value_weight), axis=1)
    qkv_z = lax.all_gather(slice_rows(qkv_shard, low), "wsh", axis=0, tiled=True)
    proj_z = lax.all_gather(slice_rows(projection, low), "wsh", axis=0, tiled=True)
    qkv_full = join_rows(gather_eight(qkv_z, low), depth, shard)
    proj_full = join_rows(gather_eight(proj_z, low), depth, inner // depth)
    vectors = jnp.stack((gain_early, gain_late))
    vectors = lax.all_gather(vectors, "wsh", axis=1, tiled=True).astype(FLOAT)
    early_gain, late_gain = vectors[0], vectors[1]
    table = lax.all_gather(bias_table, "wsh", axis=0, tiled=True).astype(FLOAT)
    segs = lax.all_gather(segments, "ctx", axis=1, tiled=True).reshape(seqs, ring, rows).astype(FLOAT)
    meta = mine.astype(jnp.int32).reshape(1)

    def columns(weight):
        return jnp.concatenate(
            [lax.dynamic_slice_in_dim(weight, index * slab + chip * part, part, 1) for index in range(depth)], axis=1
        )

    pair_mine = lax.all_gather(jnp.where(is_zero, columns(gate_weight), columns(up_weight)), "wsh", axis=0, tiled=True)
    pair_other = swap(pair_mine, 1)
    down_slice = lax.dynamic_slice_in_dim(down_weight, chip * part + core * piece, piece, 0)
    down_mine = lax.all_gather(down_slice, "wsh", axis=0, tiled=True).reshape(depth, piece, width)
    down_other = swap(down_mine, 1)
    down_full = jnp.where(
        is_zero, jnp.stack((down_mine, down_other), axis=1), jnp.stack((down_other, down_mine), axis=1)
    ).reshape(depth * part, width)

    four_inputs = jnp.stack(gather_four(layer_input.reshape(seqs * rows, width)))
    four_cots = jnp.stack(gather_four(cotangent.reshape(seqs * rows, width)))
    hidden_in = layer_input.reshape(seqs * rows, width).astype(FLOAT)
    four_normed = rms_rows(four_inputs.astype(FLOAT), early_gain).astype(BFLOAT).reshape(-1, width)
    kv_own = jnp.dot(four_normed, qkv_full[:, inner:], preferred_element_type=FLOAT).astype(BFLOAT)
    own_normed = four_normed[: seqs * rows]
    queries = jnp.dot(own_normed, qkv_full[:, :inner], preferred_element_type=FLOAT).astype(BFLOAT)
    queries = queries.reshape(seqs, rows, inner)
    kv_own = kv_own.reshape(4, seqs, rows, 2 * inner)
    kv_sib = swap(kv_own, 1)

    def whole(value):
        if groups == 1:
            return value
        return lax.all_gather(value, "ctx", axis=0, tiled=True, axis_index_groups=upper)

    kv_all, kv_sib_all = whole(kv_own), whole(kv_sib)
    attention, lse = attention_forward(meta, table, segs, queries, kv_all, kv_sib_all)
    attn_low = attention.astype(BFLOAT).reshape(seqs * rows, inner)
    four_attn = jnp.stack(gather_four(attn_low)).reshape(-1, inner)
    four_after = four_inputs.reshape(-1, width).astype(FLOAT) + jnp.dot(
        four_attn, proj_full, preferred_element_type=FLOAT
    )
    after_attn = four_after[: seqs * rows]
    normed_late = rms_rows(four_after, late_gain).astype(BFLOAT)

    pre_mine = jnp.dot(normed_late, pair_mine, preferred_element_type=FLOAT)
    pre_other = jnp.dot(normed_late, pair_other, preferred_element_type=FLOAT)
    gate_pre = jnp.where(is_zero, pre_mine, pre_other)
    up_pre = jnp.where(is_zero, pre_other, pre_mine)

    def gated(gate_values, up_values):
        return jax.nn.gelu(gate_values, approximate=True) * up_values

    activation = gated(gate_pre, up_pre).astype(BFLOAT)
    cots = four_cots.reshape(-1, width)
    act_grad = lax.dot_general(cots, down_full, (((1,), (1,)), ((), ())), preferred_element_type=FLOAT)
    gate_back, up_back = jax.vjp(gated, gate_pre, up_pre)[1](act_grad)
    back_mine = jnp.where(is_zero, gate_back, up_back).astype(BFLOAT)
    back_other = jnp.where(is_zero, up_back, gate_back).astype(BFLOAT)
    late_part = lax.dot_general(
        back_mine, pair_mine, (((1,), (1,)), ((), ())), preferred_element_type=FLOAT
    ) + lax.dot_general(back_other, pair_other, (((1,), (1,)), ((), ())), preferred_element_type=FLOAT)
    late_part = late_part.astype(BFLOAT).reshape(4, seqs * rows, width)
    late_back = scatter_four([late_part[index] for index in range(4)])
    out_part = jnp.dot(activation, down_full, preferred_element_type=FLOAT).astype(BFLOAT)
    out_part = out_part.reshape(4, seqs * rows, width)
    result = (after_attn + scatter_four([out_part[index] for index in range(4)])).astype(BFLOAT)

    down_grad = tn(activation, cots).astype(BFLOAT).reshape(depth, 2, piece, width)
    mine_grad = tn(normed_late, back_mine).astype(BFLOAT)
    other_grad = tn(normed_late, back_other).astype(BFLOAT)

    def join(kept, sent):
        return (kept.astype(FLOAT) + swap(sent, 1).astype(FLOAT)).astype(BFLOAT)

    down_keep = jnp.where(is_zero, down_grad[:, 0], down_grad[:, 1]).reshape(depth * piece, width)
    down_send = jnp.where(is_zero, down_grad[:, 1], down_grad[:, 0]).reshape(depth * piece, width)
    down_sum = join(down_keep, down_send)
    pair_sum = join(mine_grad, other_grad)

    def over_groups(value):
        return lax.psum(value, "ctx", axis_index_groups=upper) if groups > 1 else value

    down_own = over_groups(lax.psum_scatter(down_sum, "wsh", scatter_dimension=0, tiled=True))
    pair_own = over_groups(lax.psum_scatter(pair_sum, "wsh", scatter_dimension=0, tiled=True))
    down_out = jnp.concatenate(gather_eight(down_own, low), axis=0).astype(FLOAT)
    four_pair = gather_four(pair_own)
    stacked_pair = jnp.stack(four_pair)
    stacked_other = swap(stacked_pair, 1)

    def spread(stack):
        chips = [
            lax.dynamic_index_in_dim(stack, lax.bitwise_xor(chip, jnp.int32(index)), 0, keepdims=False) for index in range(4)
        ]
        return jnp.concatenate(
            [chips[index][:, level * part : (level + 1) * part] for level in range(depth) for index in range(4)], axis=1
        )

    gate_out = spread(jnp.where(is_zero, stacked_pair, stacked_other)).astype(FLOAT)
    up_out = spread(jnp.where(is_zero, stacked_other, stacked_pair)).astype(FLOAT)

    cot_own = cotangent.reshape(seqs * rows, width).astype(FLOAT)
    residual_grad = cot_own + rms_back(after_attn, late_gain, late_back)
    mix_low = residual_grad.astype(BFLOAT)
    proj_grad = tn(attn_low, mix_low).astype(BFLOAT)
    attn_grad = lax.dot_general(mix_low, proj_full, (((1,), (1,)), ((), ())), preferred_element_type=FLOAT)
    attn_grad = attn_grad.astype(BFLOAT).reshape(seqs, rows, inner)
    dq, dk_own, dk_sib, dv_own, dv_sib, table_part = attention_backward(
        meta, table, segs, queries, kv_all, kv_sib_all, attn_grad, attention, lse
    )

    def owned(value):
        if groups == 1:
            return value
        return lax.psum_scatter(value, "ctx", scatter_dimension=0, tiled=True, axis_index_groups=upper)

    dkv_own = owned(jnp.concatenate((dk_own, dv_own), axis=-1))
    dkv_sib = owned(jnp.concatenate((dk_sib, dv_sib), axis=-1))
    dkv_four = (dkv_own.astype(FLOAT) + swap(dkv_sib, 1).astype(FLOAT)).astype(BFLOAT)
    dkv_four = dkv_four.reshape(4, seqs * rows, 2 * inner)
    dkv = scatter_four([dkv_four[index] for index in range(4)]).astype(BFLOAT)
    dq = dq.reshape(seqs * rows, inner)
    kv_grad = tn(four_normed, dkv_four.reshape(-1, 2 * inner)).astype(BFLOAT)
    q_grad = tn(own_normed, dq).astype(BFLOAT)
    dqkv = jnp.concatenate((dq, dkv), axis=1)
    early_back = lax.dot_general(dqkv, qkv_full, (((1,), (1,)), ((), ())), preferred_element_type=FLOAT)
    input_grad = (residual_grad + rms_back(hidden_in, early_gain, early_back)).astype(BFLOAT)

    qkv_grad = jnp.concatenate((q_grad, kv_grad), axis=1)
    qkv_out = lax.psum(lax.psum_scatter(qkv_grad, "wsh", scatter_dimension=0, tiled=True), "ctx").astype(FLOAT)
    proj_out = lax.psum(lax.psum_scatter(proj_grad, "wsh", scatter_dimension=0, tiled=True), "ctx").astype(FLOAT)
    table_sum = jnp.sum(table_part, axis=-1).reshape(heads, BUCKETS)
    table_sum = lax.psum(table_sum, ("ctx", "wsh"))
    table_rows = BUCKETS // depth
    table_out = jnp.transpose(lax.dynamic_slice_in_dim(table_sum, zed * table_rows, table_rows, 1))
    early_out = jnp.sum(qkv_out * qkv_shard.astype(FLOAT), axis=1) / gain_early.astype(FLOAT)
    late_out = (
        jnp.sum(gate_out * gate_weight.astype(FLOAT), axis=1) + jnp.sum(up_out * up_weight.astype(FLOAT), axis=1)
    ) / gain_late.astype(FLOAT)
    return (
        result.reshape(seqs, rows, width),
        input_grad.reshape(seqs, rows, width),
        qkv_out[:, :inner],
        qkv_out[:, inner : 2 * inner],
        qkv_out[:, 2 * inner :],
        proj_out,
        gate_out,
        up_out,
        down_out,
        early_out,
        late_out,
        table_out,
    )


def solution(mesh):
    rows = P("wsh", "ctx", None)
    split = P("wsh", None)
    vector = P("wsh")
    return jax.shard_map(
        on_device,
        mesh=mesh,
        in_specs=(rows, P("wsh", "ctx"), rows, split, split, split, split, split, split, split, vector, vector, split),
        out_specs=(rows, rows, split, split, split, split, split, split, split, vector, vector, split),
        check_vma=False,
    )
```

```python
import functools

import jax
import jax.numpy as jnp
import numpy as np
from jax import lax
from jax.experimental import pallas as pl
from jax.experimental.pallas import tpu as pltpu
from jax.sharding import PartitionSpec as P

BUCKETS = 32
GROUP = 8
EPSILON = 1e-06
NEGATIVE = -1e30
PRECISE = lax.Precision.HIGHEST
BUCKET_EDGES = (12, 16, 23, 32, 46, 64, 91)
FLOAT = jnp.float32
BFLOAT = jnp.bfloat16


def bucket_number(offset):
    distance = abs(offset)
    level = distance if distance < 8 else 8 + sum(distance >= edge for edge in BUCKET_EDGES)
    return level + (16 if offset > 0 else 0)


def bucket_of(offsets):
    distance = jnp.abs(offsets)
    coarse = 8 + sum(((distance >= boundary).astype(jnp.int32) for boundary in BUCKET_EDGES))
    level = jnp.where(distance < 8, distance, coarse)
    return level + jnp.where(offsets > 0, 16, 0)


def near_radius(rows):
    return -(-(BUCKET_EDGES[-1] - 1) // rows)


def tile_offsets(block_gap, rows):
    keys = lax.broadcasted_iota(jnp.int32, (rows, rows), 0)
    queries = lax.broadcasted_iota(jnp.int32, (rows, rows), 1)
    return block_gap * rows + keys - queries


def tile_buckets(block_gap, rows):
    low, high = block_gap * rows - (rows - 1), block_gap * rows + (rows - 1)
    return sorted({bucket_number(offset) for offset in range(low, high + 1)})


def nt(left, right):
    return lax.dot_general(left, right, (((1,), (1,)), ((), ())), preferred_element_type=FLOAT)


def tn(left, right):
    return lax.dot_general(left, right, (((0,), (0,)), ((), ())), preferred_element_type=FLOAT)


def block_number(meta, half, position):
    low = lax.rem(meta, GROUP)
    return (position // 4) * GROUP + lax.bitwise_xor(low, jnp.int32(2 * (position % 4) + half))


def tile_index(meta, half, position, radius):
    gap = block_number(meta, half, position) - meta
    return jnp.clip(gap, -(radius + 1), radius + 1) + radius + 1


def build_bias(bias_ref, table_ref, pair, rows, radius):
    for side, bucket in ((0, 15), (2 * radius + 2, 31)):
        for head in range(2):
            bias_ref[head, side] = jnp.full((rows, rows), table_ref[bucket, 2 * pair + head], FLOAT)
    for gap in range(-radius, radius + 1):
        buckets = bucket_of(tile_offsets(gap, rows))
        present = tile_buckets(gap, rows)
        tiles = [jnp.full((rows, rows), table_ref[present[0], 2 * pair + head], FLOAT) for head in range(2)]
        for bucket in present[1:]:
            hit = buckets == bucket
            tiles = [jnp.where(hit, table_ref[bucket, 2 * pair + head], tiles[head]) for head in range(2)]
        for head in range(2):
            bias_ref[head, gap + radius + 1] = tiles[head]


def build_mask(mask_ref, segs_ref, meta, seq, rows, count):
    own = segs_ref[seq, pl.ds(meta, 1), :]
    for half in range(2):
        for position in range(count):
            row = segs_ref[seq, pl.ds(block_number(meta, half, position), 1), :]
            keys = jnp.transpose(jnp.broadcast_to(row, (rows, rows)))
            mask_ref[seq, half * count + position] = jnp.where(keys == own, 0.0, NEGATIVE)


def half_scores(keys, query, meta, head, half, seq, bias_ref, mask_ref, rows, count, radius):
    raw = nt(keys, query)
    parts = []
    for position in range(count):
        extra = bias_ref[head, tile_index(meta, half, position, radius)]
        masked = mask_ref[seq, half * count + position]
        parts.append(raw[position * rows : (position + 1) * rows] + (extra + masked))
    return jnp.concatenate(parts, axis=0)


def head_rows(value, head, lane):
    return jnp.where((lane < 64) == (head == 0), value, jnp.zeros_like(value))


def forward_kernel(
    meta_ref, table_ref, segs_ref, q_ref, ko_ref, ks_ref, vo_ref, vs_ref, out_ref, lse_ref, bias_ref, mask_ref,
    *, rows, count, radius,
):
    pair, seq = pl.program_id(0), pl.program_id(1)
    meta = meta_ref[0]

    @pl.when(seq == 0)
    def _():
        build_bias(bias_ref, table_ref, pair, rows, radius)

    @pl.when(pair == 0)
    def _():
        build_mask(mask_ref, segs_ref, meta, seq, rows, count)

    query = q_ref[0]
    lane = lax.broadcasted_iota(jnp.int32, query.shape, 1)
    keys = [ref[...].reshape(count * rows, 128) for ref in (ko_ref, ks_ref)]
    values = [ref[...].reshape(count * rows, 128) for ref in (vo_ref, vs_ref)]
    pieces = []
    for head in range(2):
        one = head_rows(query, head, lane)
        scores = [
            half_scores(keys[half], one, meta, head, half, seq, bias_ref, mask_ref, rows, count, radius)
            for half in range(2)
        ]
        top = jnp.maximum(jnp.max(scores[0], axis=0, keepdims=True), jnp.max(scores[1], axis=0, keepdims=True))
        raised = [jnp.exp(part - top) for part in scores]
        total = jnp.sum(raised[0], axis=0, keepdims=True) + jnp.sum(raised[1], axis=0, keepdims=True)
        scale = 1.0 / total
        mixed = sum(tn(values[half], (raised[half] * scale).astype(BFLOAT)) for half in range(2))
        pieces.append(mixed[64 * head : 64 * head + 64])
        lse_ref[0, 0, head : head + 1] = top + jnp.log(total)
    out_ref[0] = jnp.transpose(jnp.concatenate(pieces, axis=0))


def backward_kernel(
    meta_ref, table_ref, segs_ref, q_ref, ko_ref, ks_ref, vo_ref, vs_ref, do_ref, out_ref, lse_ref,
    dq_ref, dko_ref, dks_ref, dvo_ref, dvs_ref, tab_ref, bias_ref, mask_ref, sum_ref,
    *, rows, count, radius,
):
    pair, seq = pl.program_id(0), pl.program_id(1)
    meta = meta_ref[0]

    @pl.when(seq == 0)
    def _():
        build_bias(bias_ref, table_ref, pair, rows, radius)
        sum_ref[...] = jnp.zeros_like(sum_ref)

    @pl.when(pair == 0)
    def _():
        build_mask(mask_ref, segs_ref, meta, seq, rows, count)

    query, grad = q_ref[0], do_ref[0]
    lane = lax.broadcasted_iota(jnp.int32, query.shape, 1)
    keys = [ref[...].reshape(count * rows, 128) for ref in (ko_ref, ks_ref)]
    values = [ref[...].reshape(count * rows, 128) for ref in (vo_ref, vs_ref)]
    picks = (
        lax.broadcasted_iota(jnp.int32, (8, 128), 1) // 64 == lax.broadcasted_iota(jnp.int32, (8, 128), 0)
    ).astype(FLOAT)
    deltas = lax.dot_general(
        picks, grad.astype(FLOAT) * out_ref[0], (((1,), (1,)), ((), ())), precision=PRECISE, preferred_element_type=FLOAT
    )
    query_heads = [head_rows(query, head, lane) for head in range(2)]
    grad_heads = [head_rows(grad, head, lane) for head in range(2)]
    probs, slopes = [[], []], [[], []]
    pieces = []
    for head in range(2):
        logsum = lse_ref[0, 0, head : head + 1]
        delta = deltas[head : head + 1]
        flow = None
        for half in range(2):
            scores = half_scores(
                keys[half], query_heads[head], meta, head, half, seq, bias_ref, mask_ref, rows, count, radius
            )
            prob = jnp.exp(scores - logsum)
            slope = prob * (nt(values[half], grad_heads[head]) - delta)
            for position in range(count):
                index = tile_index(meta, half, position, radius)
                sum_ref[head, index] = sum_ref[head, index] + slope[position * rows : (position + 1) * rows]
            slope_low = slope.astype(BFLOAT)
            probs[half].append(prob.astype(BFLOAT))
            slopes[half].append(slope_low)
            term = tn(keys[half], slope_low)
            flow = term if flow is None else flow + term
        pieces.append(flow[64 * head : 64 * head + 64])
    dq_ref[0] = jnp.transpose(jnp.concatenate(pieces, axis=0)).astype(BFLOAT)
    query_stack = jnp.concatenate(query_heads, axis=0)
    grad_stack = jnp.concatenate(grad_heads, axis=0)
    for half, (dk_ref, dv_ref) in enumerate(((dko_ref, dvo_ref), (dks_ref, dvs_ref))):
        dk = jnp.dot(jnp.concatenate(slopes[half], axis=1), query_stack, preferred_element_type=FLOAT)
        dv = jnp.dot(jnp.concatenate(probs[half], axis=1), grad_stack, preferred_element_type=FLOAT)
        dk_ref[...] = dk.astype(BFLOAT).reshape(dk_ref.shape)
        dv_ref[...] = dv.astype(BFLOAT).reshape(dv_ref.shape)

    @pl.when(seq == pl.num_programs(1) - 1)
    def _():
        for head in range(2):
            sums = {}
            for side, bucket in ((0, 15), (2 * radius + 2, 31)):
                sums[bucket] = jnp.sum(sum_ref[head, side], axis=0, keepdims=True)
            for gap in range(-radius, radius + 1):
                buckets = bucket_of(tile_offsets(gap, rows))
                tile = sum_ref[head, gap + radius + 1]
                for bucket in tile_buckets(gap, rows):
                    part = jnp.sum(jnp.where(buckets == bucket, tile, 0.0), axis=0, keepdims=True)
                    sums[bucket] = sums[bucket] + part if bucket in sums else part
            for bucket in range(BUCKETS):
                tab_ref[0, head, bucket : bucket + 1] = sums.get(bucket, jnp.zeros((1, rows), FLOAT))


def attention_specs(seqs, rows, count, blocks, pairs):
    small = [
        pl.BlockSpec(memory_space=pltpu.SMEM),
        pl.BlockSpec(memory_space=pltpu.SMEM),
        pl.BlockSpec((seqs, blocks, rows), lambda p, s: (0, 0, 0)),
    ]
    query = pl.BlockSpec((1, rows, 128), lambda p, s: (s, 0, p))
    key = pl.BlockSpec((count, 1, rows, 128), lambda p, s: (0, s, 0, p))
    value = pl.BlockSpec((count, 1, rows, 128), lambda p, s: (0, s, 0, pairs + p))
    stat = pl.BlockSpec((1, 1, 8, rows), lambda p, s: (p, s, 0, 0))
    return small, query, key, value, stat


def attention_scratch(seqs, rows, count, radius):
    return [
        pltpu.VMEM((2, 2 * radius + 3, rows, rows), FLOAT),
        pltpu.VMEM((seqs, 2 * count, rows, rows), FLOAT),
    ]


def attention_cost(seqs, rows, keys, width, products):
    return pl.CostEstimate(
        flops=2 * products * seqs * rows * keys * width,
        bytes_accessed=4 * seqs * keys * width * products,
        transcendentals=seqs * rows * keys * width // 64,
    )


def attention_forward(meta, table, segs, queries, kv_own, kv_sib):
    seqs, rows, inner = queries.shape
    count, blocks, pairs = kv_own.shape[0], segs.shape[1], inner // 128
    radius = near_radius(rows)
    small, query, key, value, stat = attention_specs(seqs, rows, count, blocks, pairs)
    return pl.pallas_call(
        functools.partial(forward_kernel, rows=rows, count=count, radius=radius),
        grid=(pairs, seqs),
        in_specs=[*small, query, key, key, value, value],
        out_specs=[query, stat],
        out_shape=[
            jax.ShapeDtypeStruct((seqs, rows, inner), FLOAT),
            jax.ShapeDtypeStruct((pairs, seqs, 8, rows), FLOAT),
        ],
        scratch_shapes=attention_scratch(seqs, rows, count, radius),
        cost_estimate=attention_cost(seqs, rows, blocks * rows, inner, 2),
        name="attention_forward",
    )(meta, table, segs, queries, kv_own, kv_sib, kv_own, kv_sib)


def attention_backward(meta, table, segs, queries, kv_own, kv_sib, grad, out, lse):
    seqs, rows, inner = queries.shape
    count, blocks, pairs = kv_own.shape[0], segs.shape[1], inner // 128
    radius = near_radius(rows)
    small, query, key, value, stat = attention_specs(seqs, rows, count, blocks, pairs)
    side = jax.ShapeDtypeStruct((count, seqs, rows, inner), BFLOAT)
    return pl.pallas_call(
        functools.partial(backward_kernel, rows=rows, count=count, radius=radius),
        grid=(pairs, seqs),
        in_specs=[*small, query, key, key, value, value, query, query, stat],
        out_specs=[query, key, key, key, key, pl.BlockSpec((1, 2, BUCKETS, rows), lambda p, s: (p, 0, 0, 0))],
        out_shape=[
            jax.ShapeDtypeStruct((seqs, rows, inner), BFLOAT), side, side, side, side,
            jax.ShapeDtypeStruct((pairs, 2, BUCKETS, rows), FLOAT),
        ],
        scratch_shapes=[
            *attention_scratch(seqs, rows, count, radius),
            pltpu.VMEM((2, 2 * radius + 3, rows, rows), FLOAT),
        ],
        cost_estimate=attention_cost(seqs, rows, blocks * rows, inner, 5),
        name="attention_backward",
    )(meta, table, segs, queries, kv_own, kv_sib, kv_own, kv_sib, grad, out, lse)


def swap(value, bit):
    count = lax.axis_size("ctx")
    return lax.ppermute(value, "ctx", [(source, source ^ bit) for source in range(count)])


def swap_depth(value, bit):
    count = lax.axis_size("wsh")
    return lax.ppermute(value, "wsh", [(source, source ^ bit) for source in range(count)])


def halves_four(own, cut):
    first, second = swap(own, 2), swap(own, 4)
    return own, first, second, swap(first[:cut], 4), swap(second[cut:], 2)


def gather_four(own, cut):
    own, first, second, upper, lower = halves_four(own, cut)
    return jnp.stack((own, first, second, jnp.concatenate((upper, lower), axis=0)))


def scatter_four(blocks, cut):
    own, first, second, last = (blocks[index] for index in range(4))
    low, high = swap(last[:cut], 4), swap(last[cut:], 2)
    first = jnp.concatenate(((first[:cut].astype(FLOAT) + low.astype(FLOAT)).astype(BFLOAT), first[cut:]), axis=0)
    second = jnp.concatenate((second[:cut], (second[cut:].astype(FLOAT) + high.astype(FLOAT)).astype(BFLOAT)), axis=0)
    got_first, got_second = swap(first, 2), swap(second, 4)
    return own.astype(FLOAT) + got_first.astype(FLOAT) + got_second.astype(FLOAT)


def rms_back(hidden, gain, back):
    scale = lax.rsqrt(jnp.mean(hidden * hidden, axis=-1, keepdims=True) + EPSILON)
    lifted = back * gain
    return scale * lifted - hidden * (scale * scale * scale) * jnp.mean(lifted * hidden, axis=-1, keepdims=True)


VMEM_WHOLE = pl.BlockSpec(memory_space=pltpu.VMEM)
SMEM_WHOLE = pl.BlockSpec(memory_space=pltpu.SMEM)
BIG = pltpu.CompilerParams(vmem_limit_bytes=60 * 1024 * 1024)


def slice_size(total):
    return -(-total // (GROUP * 16)) * 16


def slice_start(index, total, size):
    return jnp.minimum(index * size, total - size)


def join_kernel(place_ref, near_ref, far_ref, *out_refs, depth, total, size):
    low, zed = place_ref[0], place_ref[1]
    for index in range(GROUP):
        gap = lax.bitwise_xor(low, jnp.int32(index))
        slot, odd = gap // 2, lax.rem(gap, 2)
        for level in range(depth):
            step = lax.bitwise_xor(zed, jnp.int32(level)) if depth > 1 else 0
            start = pl.multiple_of(step * size, 16)
            near = near_ref[slot, pl.ds(start, size), :]
            far = far_ref[slot, pl.ds(start, size), :]
            rows = jnp.where(odd == 0, near, far)
            base = level * total + min(index * size, total - size)
            column = 0
            for out_ref in out_refs:
                wide = out_ref.shape[1]
                out_ref[base : base + size, :] = rows[:, column : column + wide].astype(out_ref.dtype)
                column += wide


def join(place, near, far, depth, total, size, widths, dtype):
    return pl.pallas_call(
        functools.partial(join_kernel, depth=depth, total=total, size=size),
        in_specs=[SMEM_WHOLE, VMEM_WHOLE, VMEM_WHOLE],
        out_specs=[VMEM_WHOLE] * len(widths),
        out_shape=[jax.ShapeDtypeStruct((depth * total, wide), dtype) for wide in widths],
        compiler_params=BIG,
        cost_estimate=pl.CostEstimate(flops=0, bytes_accessed=6 * depth * total * sum(widths), transcendentals=0),
        name="join_rows",
    )(place, near, far)


def deal_kernel(place_ref, *refs, depth, total, size):
    in_refs, (keep_ref, send_ref) = refs[:-2], refs[-2:]
    low, zed = place_ref[0], place_ref[1]
    for index in range(GROUP):
        target = lax.bitwise_xor(low, jnp.int32(index))
        out_ref = keep_ref if index % 2 == 0 else send_ref
        for step in range(depth):
            level = lax.bitwise_xor(zed, jnp.int32(step))
            start = pl.multiple_of(level * total + slice_start(target, total, size), 16)
            column = 0
            for in_ref in in_refs:
                wide = in_ref.shape[1]
                out_ref[index // 2, step, :, column : column + wide] = in_ref[pl.ds(start, size), :]
                column += wide


def deal(place, parts, depth, total, size):
    width = sum(part.shape[1] for part in parts)
    shape = jax.ShapeDtypeStruct((4, depth, size, width), BFLOAT)
    return pl.pallas_call(
        functools.partial(deal_kernel, depth=depth, total=total, size=size),
        in_specs=[SMEM_WHOLE] + [VMEM_WHOLE] * len(parts),
        out_specs=[VMEM_WHOLE] * 2,
        out_shape=[shape, shape],
        compiler_params=BIG,
        cost_estimate=pl.CostEstimate(flops=0, bytes_accessed=4 * depth * total * width, transcendentals=0),
        name="deal_rows",
    )(place, *parts)


def misc_kernel(place_ref, misc_ref, near_ref, far_ref, gains_ref, table_ref, segs_ref, *, depth, shard, buckets, base):
    low, zed = place_ref[0], place_ref[1]
    for level in range(depth):
        rows = misc_ref[lax.bitwise_xor(zed, jnp.int32(level))].astype(FLOAT)
        gains_ref[:, level * shard : (level + 1) * shard] = rows[:8, :shard]
        table_ref[level * buckets : (level + 1) * buckets, :] = rows[8 : 8 + buckets, :128]
    seqs, _, rows = segs_ref.shape
    for index in range(GROUP):
        gap = lax.bitwise_xor(low, jnp.int32(index))
        slot, odd = gap // 2, lax.rem(gap, 2)
        own = jnp.where(odd == 0, near_ref[slot, base : base + 16, :128], far_ref[slot, base : base + 16, :128])
        own = own.astype(FLOAT)
        for seq in range(seqs):
            segs_ref[seq, index : index + 1, :] = own[seq : seq + 1, :rows]


def unpack_misc(place, misc, near, far, depth, shard, buckets, base, seqs, rows):
    return pl.pallas_call(
        functools.partial(misc_kernel, depth=depth, shard=shard, buckets=buckets, base=base),
        in_specs=[SMEM_WHOLE, VMEM_WHOLE, VMEM_WHOLE, VMEM_WHOLE],
        out_specs=[VMEM_WHOLE] * 3,
        out_shape=[
            jax.ShapeDtypeStruct((8, depth * shard), FLOAT),
            jax.ShapeDtypeStruct((depth * buckets, 128), FLOAT),
            jax.ShapeDtypeStruct((seqs, GROUP, rows), FLOAT),
        ],
        name="unpack_misc",
    )(place, misc, near, far)


def pick_block(refs, step, scratch_ref, cut):
    for index in range(3):

        @pl.when(step == index)
        def _(index=index):
            scratch_ref[...] = refs[index][...]

    @pl.when(step == 3)
    def _():
        scratch_ref[:cut] = refs[3][...]
        scratch_ref[cut:] = refs[4][...]


def once(shape):
    return pl.BlockSpec(shape, lambda g: (0,) * len(shape), pipeline_mode=pl.Buffered(1))


def norm_kernel(x0, x1, x2, x3, x4, gain_ref, weight_ref, normed_ref, kv_ref, q_ref, x_scr, *, inner):
    step = pl.program_id(0)
    pick_block((x0, x1, x2, x3, x4), step, x_scr, x3.shape[0])
    hidden = x_scr[...].astype(FLOAT)
    scale = lax.rsqrt(jnp.mean(hidden * hidden, axis=-1, keepdims=True) + EPSILON)
    normed = (hidden * scale * gain_ref[...]).astype(BFLOAT)
    normed_ref[0] = normed
    kv_ref[0] = jnp.dot(normed, weight_ref[:, inner:], preferred_element_type=FLOAT).astype(BFLOAT)

    @pl.when(step == 0)
    def _():
        q_ref[...] = jnp.dot(normed, weight_ref[:, :inner], preferred_element_type=FLOAT).astype(BFLOAT)


def norm_project(pieces, gain, weight, inner):
    tokens, width = pieces[0].shape
    return pl.pallas_call(
        functools.partial(norm_kernel, inner=inner),
        grid=(4,),
        in_specs=[*[once(piece.shape) for piece in pieces], once(gain.shape), once(weight.shape)],
        out_specs=[
            pl.BlockSpec((1, tokens, width), lambda g: (g, 0, 0)),
            pl.BlockSpec((1, tokens, 2 * inner), lambda g: (g, 0, 0)),
            pl.BlockSpec((tokens, inner), lambda g: (0, 0)),
        ],
        out_shape=[
            jax.ShapeDtypeStruct((4, tokens, width), BFLOAT),
            jax.ShapeDtypeStruct((4, tokens, 2 * inner), BFLOAT),
            jax.ShapeDtypeStruct((tokens, inner), BFLOAT),
        ],
        scratch_shapes=[pltpu.VMEM((tokens, width), BFLOAT)],
        compiler_params=BIG,
        cost_estimate=pl.CostEstimate(
            flops=18 * tokens * width * inner, bytes_accessed=18 * tokens * width, transcendentals=0
        ),
        name="norm_project",
    )(*pieces, gain, weight)


GELU_SCALE = float(np.sqrt(2.0 / np.pi))


def feed_kernel(
    core_ref, a0, a1, a2, a3, a4, x0, x1, x2, x3, x4, c0, c1, c2, c3, c4, proj_ref, gain_ref, mine_ref, other_ref, down_ref,
    after_ref, normed_ref, act_ref, dmine_ref, dother_ref, out_ref, late_ref, a_scr, x_scr, c_scr,
):
    step = pl.program_id(0)
    cut = x3.shape[0]
    pick_block((a0, a1, a2, a3, a4), step, a_scr, cut)
    pick_block((x0, x1, x2, x3, x4), step, x_scr, cut)
    pick_block((c0, c1, c2, c3, c4), step, c_scr, cut)
    is_zero = core_ref[0] == 0
    after = x_scr[...].astype(FLOAT) + jnp.dot(a_scr[...], proj_ref[...], preferred_element_type=FLOAT)

    @pl.when(step == 0)
    def _():
        after_ref[...] = after

    scale = lax.rsqrt(jnp.mean(after * after, axis=-1, keepdims=True) + EPSILON)
    normed = (after * scale * gain_ref[...]).astype(BFLOAT)
    normed_ref[0] = normed
    pre_mine = jnp.dot(normed, mine_ref[...], preferred_element_type=FLOAT)
    pre_other = jnp.dot(normed, other_ref[...], preferred_element_type=FLOAT)
    gate = jnp.where(is_zero, pre_mine, pre_other)
    up = jnp.where(is_zero, pre_other, pre_mine)
    square = gate * gate
    lifted = jnp.tanh(GELU_SCALE * (gate + 0.044715 * gate * square))
    half = 0.5 * (1.0 + lifted)
    smooth = gate * half
    act = (smooth * up).astype(BFLOAT)
    act_ref[0] = act
    out_ref[0] = jnp.dot(act, down_ref[...], preferred_element_type=FLOAT).astype(BFLOAT)
    act_back = nt(c_scr[...], down_ref[...])
    slope = half + 0.5 * gate * (1.0 - lifted * lifted) * (GELU_SCALE * (1.0 + 3 * 0.044715 * square))
    gate_back = act_back * up * slope
    up_back = act_back * smooth
    dmine = jnp.where(is_zero, gate_back, up_back).astype(BFLOAT)
    dother = jnp.where(is_zero, up_back, gate_back).astype(BFLOAT)
    dmine_ref[0] = dmine
    dother_ref[0] = dother
    late_ref[0] = (nt(dmine, mine_ref[...]) + nt(dother, other_ref[...])).astype(BFLOAT)


def feed_forward(core, attn, inputs, cots, proj, gain, mine, other, down):
    tokens, width = inputs[0].shape
    inner, wide = attn[0].shape[1], mine.shape[1]

    def block(size):
        return pl.BlockSpec((1, tokens, size), lambda g: (g, 0, 0))

    def shape(size):
        return jax.ShapeDtypeStruct((4, tokens, size), BFLOAT)

    return pl.pallas_call(
        feed_kernel,
        grid=(4,),
        in_specs=[
            SMEM_WHOLE,
            *[once(piece.shape) for piece in (*attn, *inputs, *cots)],
            *[once(value.shape) for value in (proj, gain, mine, other, down)],
        ],
        out_specs=[
            pl.BlockSpec((tokens, width), lambda g: (0, 0)),
            block(width), block(wide), block(wide), block(wide), block(width), block(width),
        ],
        out_shape=[
            jax.ShapeDtypeStruct((tokens, width), FLOAT),
            shape(width), shape(wide), shape(wide), shape(wide), shape(width), shape(width),
        ],
        scratch_shapes=[
            pltpu.VMEM((tokens, inner), BFLOAT), pltpu.VMEM((tokens, width), BFLOAT), pltpu.VMEM((tokens, width), BFLOAT),
        ],
        compiler_params=BIG,
        cost_estimate=pl.CostEstimate(
            flops=8 * tokens * width * (6 * wide + inner), bytes_accessed=30 * tokens * width, transcendentals=4 * tokens * wide
        ),
        name="feed_forward",
    )(core, *attn, *inputs, *cots, proj, gain, mine, other, down)


def spread_kernel(place_ref, near_ref, far_ref, gate_ref, up_ref, gate_out, up_out, late_ref, *, depth, part):
    low = place_ref[0]
    chip, core = low // 2, lax.rem(low, 2)
    for index in range(4):
        slot = lax.bitwise_xor(chip, jnp.int32(index))
        near, far = near_ref[slot].astype(FLOAT), far_ref[slot].astype(FLOAT)
        gate = jnp.where(core == 0, near, far)
        up = jnp.where(core == 0, far, near)
        for level in range(depth):
            base = (level * 4 + index) * part
            gate_out[:, base : base + part] = gate[:, level * part : (level + 1) * part]
            up_out[:, base : base + part] = up[:, level * part : (level + 1) * part]
    total = gate_out[...] * gate_ref[...].astype(FLOAT) + up_out[...] * up_ref[...].astype(FLOAT)
    late_ref[...] = jnp.broadcast_to(jnp.sum(total, axis=1, keepdims=True), late_ref.shape)


def spread(place, near, far, gate, up, depth, part):
    shard, hidden = gate.shape
    tile = shard // 2 if shard % 32 == 0 else shard
    tile = 184 if shard % 184 == 0 else shard
    pieces = pl.BlockSpec((4, tile, near.shape[2]), lambda g: (0, g, 0))
    rows = pl.BlockSpec((tile, hidden), lambda g: (g, 0))
    return pl.pallas_call(
        functools.partial(spread_kernel, depth=depth, part=part),
        grid=(shard // tile,),
        in_specs=[SMEM_WHOLE, pieces, pieces, rows, rows],
        out_specs=[rows, rows, pl.BlockSpec((tile, 128), lambda g: (g, 0))],
        out_shape=[
            jax.ShapeDtypeStruct((shard, hidden), FLOAT),
            jax.ShapeDtypeStruct((shard, hidden), FLOAT),
            jax.ShapeDtypeStruct((shard, 128), FLOAT),
        ],
        compiler_params=BIG,
        cost_estimate=pl.CostEstimate(flops=4 * shard * hidden, bytes_accessed=16 * shard * hidden, transcendentals=0),
        name="spread_columns",
    )(place, near, far, gate, up)


def after(value, *others):
    return lax.optimization_barrier((value, *others))[0]


def on_device(
    layer_input, segments, cotangent, query_weight, key_weight, value_weight, projection, gate_weight, up_weight,
    down_weight, gain_early, gain_late, bias_table,
):
    ring = lax.axis_size("ctx")
    depth = lax.axis_size("wsh")
    groups = ring // GROUP
    mine = lax.axis_index("ctx")
    low = lax.rem(mine, GROUP)
    chip, core = low // 2, lax.rem(low, 2)
    zed = lax.axis_index("wsh")
    seqs, rows, width = layer_input.shape
    inner = query_weight.shape[1]
    heads = bias_table.shape[1]
    shard = width // depth
    slab = gate_weight.shape[1] // depth
    part = slab // 4
    piece = part // 2
    tokens = seqs * rows
    cut = tokens // 2
    buckets = BUCKETS // depth
    upper = [[group * GROUP + index for group in range(groups)] for index in range(GROUP)]
    is_zero = core == 0
    place = jnp.stack((low, zed)).astype(jnp.int32)
    meta = mine.astype(jnp.int32).reshape(1)
    core_flag = core.astype(jnp.int32).reshape(1)

    def columns(weight):
        return jnp.concatenate(
            [lax.dynamic_slice_in_dim(weight, index * slab + chip * part, part, 1) for index in range(depth)], axis=1
        )

    pair_mine = lax.all_gather(jnp.where(is_zero, columns(gate_weight), columns(up_weight)), "wsh", axis=0, tiled=True)
    down_slice = lax.dynamic_slice_in_dim(down_weight, chip * part + core * piece, piece, 0)
    down_mine = lax.all_gather(down_slice, "wsh", axis=0, tiled=True).reshape(depth, piece, width)

    own_x = layer_input.reshape(tokens, width)
    own_cot = cotangent.reshape(tokens, width)
    inputs = halves_four(own_x, cut)

    size, proj_rows = slice_size(shard), inner // depth
    proj_size = slice_size(proj_rows)
    start = slice_start(low, shard, size)
    qkv_slice = jnp.concatenate(
        [lax.dynamic_slice_in_dim(weight, start, size, 0) for weight in (query_weight, key_weight, value_weight)], axis=1
    )
    proj_slice = lax.dynamic_slice_in_dim(projection, slice_start(low, proj_rows, proj_size), proj_size, 0)
    vectors = jnp.pad(jnp.stack((gain_early, gain_late)), ((0, 6), (0, width - shard)))
    table_rows = jnp.pad(bias_table, ((0, 8 - buckets), (0, width - heads)))
    proj_slice = jnp.concatenate((proj_slice, vectors, table_rows), axis=0)
    qkv_levels = [qkv_slice] + [swap_depth(qkv_slice, step) for step in range(1, depth)]
    proj_levels = jnp.stack([proj_slice] + [swap_depth(proj_slice, step) for step in range(1, depth)])
    seg_rows = jnp.pad(segments.astype(BFLOAT), ((0, 16 - seqs), (0, 3 * inner - rows)))
    qkv_near = gather_four(jnp.concatenate((*qkv_levels, seg_rows), axis=0), (depth * size + 16) // 32 * 16)
    qkv_far = swap(qkv_near, 1)
    proj_near = gather_four(proj_levels[:, :proj_size].reshape(depth * proj_size, width), depth * proj_size // 2)
    proj_far = swap(proj_near, 1)
    qkv_full = join(place, qkv_near, qkv_far, depth, shard, size, (3 * inner,), BFLOAT)[0]
    proj_full = join(place, proj_near, proj_far, depth, proj_rows, proj_size, (width,), BFLOAT)[0]
    gains, table, segs = unpack_misc(
        place, proj_levels[:, proj_size:], qkv_near, qkv_far, depth, shard, buckets, depth * size, seqs, rows
    )

    def whole(value, axis=0):
        if groups == 1:
            return value
        return lax.all_gather(value, "ctx", axis=axis, tiled=True, axis_index_groups=upper)

    segs = whole(segs, 1)

    normed, kv_own, queries = norm_project(inputs, gains[0:1], qkv_full, inner)
    kv_own = kv_own.reshape(4, seqs, rows, 2 * inner)
    queries = queries.reshape(seqs, rows, inner)
    kv_sib = swap(kv_own, 1)
    kv_all, kv_sib_all = whole(kv_own), whole(kv_sib)
    attention, lse = attention_forward(meta, table, segs, queries, kv_all, kv_sib_all)
    attn_low = attention.astype(BFLOAT).reshape(tokens, inner)
    attn = halves_four(attn_low, cut)
    cots = halves_four(own_cot, cut)

    pair_other = swap(pair_mine, 1)
    down_other = swap(down_mine, 1)
    down_full = jnp.where(
        is_zero, jnp.stack((down_mine, down_other), axis=1), jnp.stack((down_other, down_mine), axis=1)
    ).reshape(depth * part, width)
    after_attn, normed_late, activation, back_mine, back_other, out_part, late_part = feed_forward(
        core_flag, attn, inputs, cots, proj_full, gains[1:2], pair_mine, pair_other, down_full
    )
    late_back = scatter_four(late_part, cut)
    out_sum = scatter_four(out_part, cut)
    result = (after_attn + out_sum).astype(BFLOAT)

    def flat(value):
        return value.reshape(4 * tokens, value.shape[2])

    all_cots = jnp.concatenate(cots, axis=0)
    down_grad = tn(flat(activation), all_cots).astype(BFLOAT).reshape(depth, 2, piece, width)
    mine_grad = tn(flat(normed_late), flat(back_mine)).astype(BFLOAT)
    other_grad = tn(flat(normed_late), flat(back_other)).astype(BFLOAT)

    def add(kept, got):
        return (kept.astype(FLOAT) + got.astype(FLOAT)).astype(BFLOAT)

    def over_groups(value):
        return lax.psum(value, "ctx", axis_index_groups=upper) if groups > 1 else value

    down_keep = jnp.where(is_zero, down_grad[:, 0], down_grad[:, 1]).reshape(depth * piece, width)
    down_send = jnp.where(is_zero, down_grad[:, 1], down_grad[:, 0]).reshape(depth * piece, width)
    down_sum = add(down_keep, swap(down_send, 1))
    pair_sum = add(mine_grad, swap(other_grad, 1))
    down_own = over_groups(lax.psum_scatter(down_sum, "wsh", scatter_dimension=0, tiled=True))
    pair_own = over_groups(lax.psum_scatter(pair_sum, "wsh", scatter_dimension=0, tiled=True))
    down_near = gather_four(down_own, piece // 32 * 16)
    pair_near = gather_four(pair_own, shard // 32 * 16)
    down_out = join(place, down_near, swap(down_near, 1), 1, slab, piece, (width,), FLOAT)[0]
    gate_out, up_out, late_sum = spread(place, pair_near, swap(pair_near, 1), gate_weight, up_weight, depth, part)

    residual_grad = own_cot.astype(FLOAT) + rms_back(after_attn, gains[1:2], late_back)
    mix_low = residual_grad.astype(BFLOAT)
    proj_grad = tn(attn_low, mix_low).astype(BFLOAT)
    attn_grad = nt(mix_low, proj_full).astype(BFLOAT).reshape(seqs, rows, inner)
    dq, dk_own, dk_sib, dv_own, dv_sib, table_part = attention_backward(
        meta, table, segs, queries, kv_all, kv_sib_all, attn_grad, attention, lse
    )

    def owned(value):
        if groups == 1:
            return value
        return lax.psum_scatter(value, "ctx", scatter_dimension=0, tiled=True, axis_index_groups=upper)

    def both(key_part, value_part):
        return owned(jnp.concatenate((key_part, value_part), axis=-1)).reshape(4, tokens, 2 * inner)

    dkv_four = add(both(dk_own, dv_own), swap(both(dk_sib, dv_sib), 1))
    dkv = scatter_four(dkv_four, cut).astype(BFLOAT)
    dq = dq.reshape(tokens, inner)
    kv_grad = tn(flat(normed), flat(dkv_four)).astype(BFLOAT)
    q_grad = tn(normed[0], dq).astype(BFLOAT)
    dqkv = jnp.concatenate((dq, dkv), axis=1)
    early_back = nt(dqkv, qkv_full)
    input_grad = (residual_grad + rms_back(own_x.astype(FLOAT), gains[0:1], early_back)).astype(BFLOAT)

    def reduce_small(parts, total, rows_each, widths):
        keep, send = deal(place, parts, depth, total, rows_each)
        levels = scatter_four(add(keep, swap(send, 1)), depth // 2).astype(BFLOAT)
        summed = levels[0].astype(FLOAT)
        for step in range(1, depth):
            summed = summed + swap_depth(levels[step], step).astype(FLOAT)
        near = gather_four(over_groups(summed.astype(BFLOAT)), rows_each // 32 * 16 or rows_each // 2)
        return join(place, near, swap(near, 1), 1, total, rows_each, widths, FLOAT)

    proj_out = reduce_small((proj_grad,), proj_rows, proj_size, (width,))[0]
    query_out, key_out, value_out = reduce_small((q_grad, kv_grad), shard, size, (inner,) * 3)
    table_sum = jnp.pad(jnp.sum(table_part, axis=-1).reshape(heads, BUCKETS), ((0, 8 - heads), (0, 128 - BUCKETS)))
    for bit in (1, 2, 4):
        table_sum = table_sum + swap(table_sum, bit)
    for bit in (1, 2):
        table_sum = table_sum + swap_depth(table_sum, bit)
    table_sum = over_groups(table_sum)
    table_out = jnp.transpose(lax.dynamic_slice(table_sum, (0, zed * buckets), (heads, buckets)))
    early_out = (
        jnp.sum(query_out * query_weight.astype(FLOAT), axis=1)
        + jnp.sum(key_out * key_weight.astype(FLOAT), axis=1)
        + jnp.sum(value_out * value_weight.astype(FLOAT), axis=1)
    ) / gain_early.astype(FLOAT)
    late_out = late_sum[:, 0] / gain_late.astype(FLOAT)
    return (
        result.reshape(seqs, rows, width),
        input_grad.reshape(seqs, rows, width),
        query_out,
        key_out,
        value_out,
        proj_out,
        gate_out,
        up_out,
        down_out,
        early_out,
        late_out,
        table_out,
    )


def solution(mesh):
    rows = P("wsh", "ctx", None)
    split = P("wsh", None)
    vector = P("wsh")
    return jax.shard_map(
        on_device,
        mesh=mesh,
        in_specs=(rows, P("wsh", "ctx"), rows, split, split, split, split, split, split, split, vector, vector, split),
        out_specs=(rows, rows, split, split, split, split, split, split, split, vector, vector, split),
        check_vma=False,
    )
```

```python
import functools

import jax
import jax.numpy as jnp
import numpy as np
from jax import lax
from jax.experimental import pallas as pl
from jax.experimental.pallas import tpu as pltpu
from jax.sharding import PartitionSpec as P

BUCKETS = 32
GROUP = 8
EPSILON = 1e-06
NEGATIVE = -1e30
PRECISE = lax.Precision.HIGHEST
BUCKET_EDGES = (12, 16, 23, 32, 46, 64, 91)
FLOAT = jnp.float32
BFLOAT = jnp.bfloat16


SCALE = 0.2


def cost(flops, bytes_accessed, transcendentals):
    return pl.CostEstimate(
        flops=int(SCALE * flops), bytes_accessed=int(SCALE * bytes_accessed), transcendentals=int(SCALE * transcendentals)
    )


def bucket_number(offset):
    distance = abs(offset)
    level = distance if distance < 8 else 8 + sum(distance >= edge for edge in BUCKET_EDGES)
    return level + (16 if offset > 0 else 0)


def bucket_of(offsets):
    distance = jnp.abs(offsets)
    coarse = 8 + sum(((distance >= boundary).astype(jnp.int32) for boundary in BUCKET_EDGES))
    level = jnp.where(distance < 8, distance, coarse)
    return level + jnp.where(offsets > 0, 16, 0)


def near_radius(rows):
    return -(-(BUCKET_EDGES[-1] - 1) // rows)


def tile_offsets(block_gap, rows):
    keys = lax.broadcasted_iota(jnp.int32, (rows, rows), 0)
    queries = lax.broadcasted_iota(jnp.int32, (rows, rows), 1)
    return block_gap * rows + keys - queries


def tile_buckets(block_gap, rows):
    low, high = block_gap * rows - (rows - 1), block_gap * rows + (rows - 1)
    return sorted({bucket_number(offset) for offset in range(low, high + 1)})


def nt(left, right):
    return lax.dot_general(left, right, (((1,), (1,)), ((), ())), preferred_element_type=FLOAT)


def tn(left, right):
    return lax.dot_general(left, right, (((0,), (0,)), ((), ())), preferred_element_type=FLOAT)


def block_number(meta, half, position, count):
    low = lax.rem(meta, GROUP)
    part, group = divmod(position, count // 4)
    return group * GROUP + lax.bitwise_xor(low, jnp.int32(2 * part + half))


def tile_index(meta, half, position, count, radius):
    gap = block_number(meta, half, position, count) - meta
    return jnp.clip(gap, -(radius + 1), radius + 1) + radius + 1


def build_bias(bias_ref, table_ref, pair, rows, radius):
    for side, bucket in ((0, 15), (2 * radius + 2, 31)):
        for head in range(2):
            bias_ref[head, side] = jnp.full((rows, rows), table_ref[bucket, 2 * pair + head], FLOAT)
    for gap in range(-radius, radius + 1):
        buckets = bucket_of(tile_offsets(gap, rows))
        present = tile_buckets(gap, rows)
        tiles = [jnp.full((rows, rows), table_ref[present[0], 2 * pair + head], FLOAT) for head in range(2)]
        for bucket in present[1:]:
            hit = buckets == bucket
            tiles = [jnp.where(hit, table_ref[bucket, 2 * pair + head], tiles[head]) for head in range(2)]
        for head in range(2):
            bias_ref[head, gap + radius + 1] = tiles[head]


def build_mask(mask_ref, segs_ref, meta, seq, rows, count):
    own = segs_ref[seq, pl.ds(meta, 1), :]
    for half in range(2):
        for position in range(count):
            row = segs_ref[seq, pl.ds(block_number(meta, half, position, count), 1), :]
            keys = jnp.transpose(jnp.broadcast_to(row, (rows, rows)))
            mask_ref[seq, half * count + position] = jnp.where(keys == own, 0.0, NEGATIVE)


def half_scores(keys, query, meta, head, half, seq, bias_ref, mask_ref, rows, count, radius):
    raw = nt(keys, query)
    parts = []
    for position in range(count):
        extra = bias_ref[head, tile_index(meta, half, position, count, radius)]
        masked = mask_ref[seq, half * count + position]
        parts.append(raw[position * rows : (position + 1) * rows] + (extra + masked))
    return jnp.concatenate(parts, axis=0)


def joined(refs):
    return jnp.concatenate([ref[...].reshape(-1, ref.shape[-1]) for ref in refs], axis=0)


def head_rows(value, head, lane):
    return jnp.where((lane < 64) == (head == 0), value, jnp.zeros_like(value))


def forward_kernel(
    meta_ref, table_ref, segs_ref, q_ref, *refs, rows, count, radius,
):
    key_refs, value_refs, (out_ref, lse_ref, bias_ref, mask_ref) = refs[:8], refs[8:16], refs[16:]
    pair, seq = pl.program_id(0), pl.program_id(1)
    meta = meta_ref[0]

    @pl.when(seq == 0)
    def _():
        build_bias(bias_ref, table_ref, pair, rows, radius)

    @pl.when(pair == 0)
    def _():
        build_mask(mask_ref, segs_ref, meta, seq, rows, count)

    query = q_ref[0]
    lane = lax.broadcasted_iota(jnp.int32, query.shape, 1)
    keys = [joined(key_refs[:4]), joined(key_refs[4:])]
    values = [joined(value_refs[:4]), joined(value_refs[4:])]
    pieces = []
    for head in range(2):
        one = head_rows(query, head, lane)
        scores = [
            half_scores(keys[half], one, meta, head, half, seq, bias_ref, mask_ref, rows, count, radius)
            for half in range(2)
        ]
        top = jnp.maximum(jnp.max(scores[0], axis=0, keepdims=True), jnp.max(scores[1], axis=0, keepdims=True))
        raised = [jnp.exp(part - top) for part in scores]
        total = jnp.sum(raised[0], axis=0, keepdims=True) + jnp.sum(raised[1], axis=0, keepdims=True)
        scale = 1.0 / total
        mixed = sum(tn(values[half], (raised[half] * scale).astype(BFLOAT)) for half in range(2))
        pieces.append(mixed[64 * head : 64 * head + 64])
        lse_ref[0, 0, head : head + 1] = top + jnp.log(total)
    out_ref[0] = jnp.transpose(jnp.concatenate(pieces, axis=0))


def backward_kernel(
    meta_ref, table_ref, segs_ref, q_ref, *refs, rows, count, radius,
):
    key_refs, value_refs, (do_ref, out_ref, lse_ref, dq_ref) = refs[:8], refs[8:16], refs[16:20]
    both_refs, (tab_ref, bias_ref, mask_ref, sum_ref) = refs[20:28], refs[28:]
    pair, seq = pl.program_id(0), pl.program_id(1)
    meta = meta_ref[0]

    @pl.when(seq == 0)
    def _():
        build_bias(bias_ref, table_ref, pair, rows, radius)
        sum_ref[...] = jnp.zeros_like(sum_ref)

    @pl.when(pair == 0)
    def _():
        build_mask(mask_ref, segs_ref, meta, seq, rows, count)

    query, grad = q_ref[0], do_ref[0]
    lane = lax.broadcasted_iota(jnp.int32, query.shape, 1)
    keys = [joined(key_refs[:4]), joined(key_refs[4:])]
    values = [joined(value_refs[:4]), joined(value_refs[4:])]
    picks = (
        lax.broadcasted_iota(jnp.int32, (8, 128), 1) // 64 == lax.broadcasted_iota(jnp.int32, (8, 128), 0)
    ).astype(FLOAT)
    deltas = lax.dot_general(
        picks, grad.astype(FLOAT) * out_ref[0], (((1,), (1,)), ((), ())), precision=PRECISE, preferred_element_type=FLOAT
    )
    query_heads = [head_rows(query, head, lane) for head in range(2)]
    grad_heads = [head_rows(grad, head, lane) for head in range(2)]
    probs, slopes = [[], []], [[], []]
    pieces = []
    for head in range(2):
        logsum = lse_ref[0, 0, head : head + 1]
        delta = deltas[head : head + 1]
        flow = None
        for half in range(2):
            scores = half_scores(
                keys[half], query_heads[head], meta, head, half, seq, bias_ref, mask_ref, rows, count, radius
            )
            prob = jnp.exp(scores - logsum)
            slope = prob * (nt(values[half], grad_heads[head]) - delta)
            for position in range(count):
                index = tile_index(meta, half, position, count, radius)
                sum_ref[head, index] = sum_ref[head, index] + slope[position * rows : (position + 1) * rows]
            slope_low = slope.astype(BFLOAT)
            probs[half].append(prob.astype(BFLOAT))
            slopes[half].append(slope_low)
            term = tn(keys[half], slope_low)
            flow = term if flow is None else flow + term
        pieces.append(flow[64 * head : 64 * head + 64])
    dq_ref[0] = jnp.transpose(jnp.concatenate(pieces, axis=0)).astype(BFLOAT)
    query_stack = jnp.concatenate(query_heads, axis=0)
    grad_stack = jnp.concatenate(grad_heads, axis=0)
    for half in range(2):
        dk = jnp.dot(jnp.concatenate(slopes[half], axis=1), query_stack, preferred_element_type=FLOAT)
        dv = jnp.dot(jnp.concatenate(probs[half], axis=1), grad_stack, preferred_element_type=FLOAT)
        dk = dk.astype(BFLOAT).reshape(count, 1, rows, 128)
        dv = dv.astype(BFLOAT).reshape(count, 1, rows, 128)
        for part, both_ref in enumerate(both_refs[4 * half : 4 * half + 4]):
            side = slice(part * count // 4, (part + 1) * count // 4)
            both_ref[:, :, :, :128] = dk[side]
            both_ref[:, :, :, 128:] = dv[side]

    @pl.when(seq == pl.num_programs(1) - 1)
    def _():
        for head in range(2):
            sums = {}
            for side, bucket in ((0, 15), (2 * radius + 2, 31)):
                sums[bucket] = jnp.sum(sum_ref[head, side], axis=0, keepdims=True)
            for gap in range(-radius, radius + 1):
                buckets = bucket_of(tile_offsets(gap, rows))
                tile = sum_ref[head, gap + radius + 1]
                for bucket in tile_buckets(gap, rows):
                    part = jnp.sum(jnp.where(buckets == bucket, tile, 0.0), axis=0, keepdims=True)
                    sums[bucket] = sums[bucket] + part if bucket in sums else part
            for bucket in range(BUCKETS):
                tab_ref[0, head, bucket : bucket + 1] = sums.get(bucket, jnp.zeros((1, rows), FLOAT))


def attention_specs(seqs, rows, count, blocks, pairs):
    small = [
        pl.BlockSpec(memory_space=pltpu.SMEM),
        pl.BlockSpec(memory_space=pltpu.SMEM),
        pl.BlockSpec((seqs, blocks, rows), lambda p, s: (0, 0, 0)),
    ]
    query = pl.BlockSpec((1, rows, 128), lambda p, s: (s, 0, p))
    key = pl.BlockSpec((count // 4, 1, rows, 128), lambda p, s: (0, s, 0, 2 * p))
    value = pl.BlockSpec((count // 4, 1, rows, 128), lambda p, s: (0, s, 0, 2 * p + 1))
    stat = pl.BlockSpec((1, 1, 8, rows), lambda p, s: (p, s, 0, 0))
    return small, query, key, value, stat


def attention_scratch(seqs, rows, count, radius):
    return [
        pltpu.VMEM((2, 2 * radius + 3, rows, rows), FLOAT),
        pltpu.VMEM((seqs, 2 * count, rows, rows), FLOAT),
    ]


def attention_cost(seqs, rows, keys, width, products):
    return cost(
        flops=2 * products * seqs * rows * keys * width,
        bytes_accessed=4 * seqs * keys * width * products,
        transcendentals=seqs * rows * keys * width // 64,
    )


def attention_forward(meta, table, segs, queries, kv):
    seqs, rows, inner = queries.shape
    count, blocks, pairs = 4 * kv[0].shape[0], segs.shape[1], inner // 128
    radius = near_radius(rows)
    small, query, key, value, stat = attention_specs(seqs, rows, count, blocks, pairs)
    return pl.pallas_call(
        functools.partial(forward_kernel, rows=rows, count=count, radius=radius),
        grid=(pairs, seqs),
        in_specs=[*small, query, *[key] * 8, *[value] * 8],
        out_specs=[query, stat],
        out_shape=[
            jax.ShapeDtypeStruct((seqs, rows, inner), FLOAT),
            jax.ShapeDtypeStruct((pairs, seqs, 8, rows), FLOAT),
        ],
        scratch_shapes=attention_scratch(seqs, rows, count, radius),
        cost_estimate=attention_cost(seqs, rows, blocks * rows, inner, 2),
        name="attention_forward",
    )(meta, table, segs, queries, *kv, *kv)


def attention_backward(meta, table, segs, queries, kv, grad, out, lse, *deps):
    seqs, rows, inner = queries.shape
    count, blocks, pairs = 4 * kv[0].shape[0], segs.shape[1], inner // 128
    radius = near_radius(rows)
    small, query, key, value, stat = attention_specs(seqs, rows, count, blocks, pairs)
    side = jax.ShapeDtypeStruct((count // 4, seqs, rows, 2 * inner), BFLOAT)
    both = pl.BlockSpec((count // 4, 1, rows, 256), lambda p, s: (0, s, 0, p))
    return pl.pallas_call(
        skipping(functools.partial(backward_kernel, rows=rows, count=count, radius=radius), 23, len(deps)),
        grid=(pairs, seqs),
        in_specs=[*small, query, *[key] * 8, *[value] * 8, query, query, stat] + [UNREAD] * len(deps),
        out_specs=[query, *[both] * 8, pl.BlockSpec((1, 2, BUCKETS, rows), lambda p, s: (p, 0, 0, 0))],
        out_shape=[
            jax.ShapeDtypeStruct((seqs, rows, inner), BFLOAT), *[side] * 8,
            jax.ShapeDtypeStruct((pairs, 2, BUCKETS, rows), FLOAT),
        ],
        scratch_shapes=[
            *attention_scratch(seqs, rows, count, radius),
            pltpu.VMEM((2, 2 * radius + 3, rows, rows), FLOAT),
        ],
        cost_estimate=attention_cost(seqs, rows, blocks * rows, inner, 5),
        name="attention_backward",
    )(meta, table, segs, queries, *kv, *kv, grad, out, lse, *deps)


def swap(value, bit):
    count = lax.axis_size("ctx")
    return lax.ppermute(value, "ctx", [(source, source ^ bit) for source in range(count)])


def swap_depth(value, bit):
    count = lax.axis_size("wsh")
    return lax.ppermute(value, "wsh", [(source, source ^ bit) for source in range(count)])


def after(value, *others):
    return lax.optimization_barrier((value, *others))[0]


def gather_halves(own):
    near, far = own
    first_near, second_far = swap(near, 2), swap(far, 4)
    first_far, second_near = swap(far, 2), swap(near, 4)
    return [near, far, first_near, first_far, second_near, second_far, swap(first_near, 4), swap(second_far, 2)]


def gather_direct(own):
    return [own, swap(own, 2), swap(own, 4), swap(own, 6)]


def gather_relay(own, cut):
    first, second = swap(own, 2), swap(own, 4)
    return jnp.stack((own, first, second, jnp.concatenate((swap(first[:cut], 4), swap(second[cut:], 2)), axis=0)))


VMEM_WHOLE = pl.BlockSpec(memory_space=pltpu.VMEM)
UNREAD = pl.BlockSpec(memory_space=pl.ANY)


def skipping(kernel, inputs, count):
    return lambda *refs: kernel(*refs[:inputs], *refs[inputs + count :])


SMEM_WHOLE = pl.BlockSpec(memory_space=pltpu.SMEM)
BIG = pltpu.CompilerParams(vmem_limit_bytes=60 * 1024 * 1024)


def moved(*arrays):
    return cost(
        flops=0, bytes_accessed=sum(int(np.prod(array.shape)) * array.dtype.itemsize for array in arrays), transcendentals=0
    )


def slice_size(total):
    return -(-total // (GROUP * 16)) * 16


def slice_start(index, total, size):
    return jnp.minimum(index * size, total - size)


def column_cut(width):
    return -(-width // 512) * 128


def pack_kernel(place_ref, q_ref, k_ref, v_ref, proj_ref, early_ref, late_ref, table_ref, out_ref, *, size, wide):
    low = place_ref[0]
    chip, core = low // 2, lax.rem(low, 2)
    inner = q_ref.shape[1]
    shard = q_ref.shape[0]
    start = pl.multiple_of(slice_start(low, shard, size), 16)
    out_ref[:size, :inner] = q_ref[pl.ds(start, size), :]
    for index, ref in enumerate((k_ref, v_ref)):
        rows = ref[pl.ds(start, size), :]
        for pair in range(inner // 128):
            base = inner + 256 * pair + 128 * index
            out_ref[:size, base : base + 128] = rows[:, 128 * pair : 128 * pair + 128]
    part = proj_ref.shape[0] // 2
    each = part // 3
    out_ref[size:, :] = jnp.zeros((out_ref.shape[0] - size, out_ref.shape[1]), BFLOAT)
    for column in range(4):
        reach = min(wide, proj_ref.shape[1] - column * wide)

        @pl.when(chip == column)
        def _(column=column, reach=reach):
            for lane in range(3):
                row = pl.multiple_of(core * part + lane * each, 16)
                out_ref[size : size + each, lane * wide : lane * wide + reach] = proj_ref[
                    pl.ds(row, each), column * wide : column * wide + reach
                ]

    base = size + each
    out_ref[base : base + 1, :shard] = early_ref[...]
    out_ref[base + 1 : base + 2, :shard] = late_ref[...]
    out_ref[base + 8 : base + 16, :128] = table_ref[...]


def unpack_kernel(place_ref, misc_ref, near_ref, far_ref, qkv_ref, proj_ref, gains_ref, table_ref, segs_ref, *, depth, size, wide):
    low = place_ref[0]
    shard, part = qkv_ref.shape[0] // depth, proj_ref.shape[0] // depth // 2
    each = part // 3
    span = size + each
    buckets = table_ref.shape[0] // depth
    for level in range(depth):
        rows = misc_ref[level].astype(FLOAT)
        gains_ref[:, level * shard : (level + 1) * shard] = rows[:8, :shard]
        table_ref[level * buckets : (level + 1) * buckets, :] = rows[8 : 8 + buckets, :128]
    seqs, _, rows = segs_ref.shape
    for index in range(GROUP):
        gap = lax.bitwise_xor(low, jnp.int32(index))
        slot, odd = gap // 2, lax.rem(gap, 2)
        block = jnp.where(odd == 0, near_ref[slot], far_ref[slot])
        for level in range(depth):
            base = level * shard + min(index * size, shard - size)
            qkv_ref[base : base + size, :] = block[level * span : level * span + size]
            column = (index // 2) * wide
            reach = min(wide, proj_ref.shape[1] - column)
            for lane in range(3):
                base = (level * 2 + index % 2) * part + lane * each
                proj_ref[base : base + each, column : column + reach] = block[
                    level * span + size : level * span + span, lane * wide : lane * wide + reach
                ]
        own = block[depth * span : depth * span + 16, :128].astype(FLOAT)
        for seq in range(seqs):
            segs_ref[seq, index : index + 1, :] = own[seq : seq + 1, :rows]


def grad_kernel(
    place_ref, normed_ref, *refs, depth, size, wide
):
    owns, gots, (dq_ref, table_ref, proj_ref) = refs[:4], refs[4:8], refs[8:11]
    sums, (keep_ref, send_ref, kv_scr, q_scr, t_scr) = refs[11:15], refs[15:]
    step = pl.program_id(0)
    for index in range(4):

        @pl.when(step == index)
        def _(index=index):
            total = (owns[index][0].astype(FLOAT) + gots[index][0].astype(FLOAT)).astype(BFLOAT)
            t_scr[...] = total
            sums[index][...] = total

    part = tn(normed_ref[0], t_scr[...])

    @pl.when(step == 0)
    def _():
        kv_scr[...] = part
        q_scr[...] = tn(normed_ref[0], dq_ref[...]).astype(BFLOAT)

    @pl.when(step > 0)
    def _():
        kv_scr[...] = kv_scr[...] + part

    @pl.when(step == 3)
    def _():
        low = place_ref[0]
        zed = place_ref[1]
        inner = q_scr.shape[1]
        shard = q_scr.shape[0] // depth
        for index in range(GROUP):
            target = lax.bitwise_xor(low, jnp.int32(index))
            out_ref = keep_ref if index % 2 == 0 else send_ref
            for gap in range(depth):
                level = lax.bitwise_xor(zed, jnp.int32(gap))
                start = pl.multiple_of(level * shard + slice_start(target, shard, size), 16)
                out_ref[index // 2, gap, :size, :inner] = q_scr[pl.ds(start, size), :]
                out_ref[index // 2, gap, :size, inner:] = kv_scr[pl.ds(start, size), :].astype(BFLOAT)
                part = proj_ref.shape[0] // depth // 2
                each = part // 3
                column = pl.multiple_of((target // 2) * wide, 128)
                for lane in range(3):
                    row = pl.multiple_of((level * 2 + lax.rem(target, 2)) * part + lane * each, 16)
                    out_ref[index // 2, gap, size:, lane * wide : (lane + 1) * wide] = proj_ref[
                        pl.ds(row, each), pl.ds(column, wide)
                    ]
                last = target == GROUP - 1
                rows = table_ref[pl.ds(pl.multiple_of(level * 16, 16), 16), :]
                out_ref[index // 2, gap, :16, :128] = jnp.where(last, rows, out_ref[index // 2, gap, :16, :128])


def weight_grads(place, normed, own, got, dq, table, proj, depth, size, wide):
    _, tokens, width = normed.shape
    inner = dq.shape[1]
    block = once((1, tokens, 2 * inner))
    summed = pl.BlockSpec((tokens, 2 * inner), lambda g: (0, 0))
    span = size + proj.shape[0] // depth // 6
    piece = jax.ShapeDtypeStruct((4, depth, span, 3 * inner), BFLOAT)
    kept = pl.BlockSpec((4, depth, span, 3 * inner), lambda g: (0, 0, 0, 0))
    return pl.pallas_call(
        functools.partial(grad_kernel, depth=depth, size=size, wide=wide),
        grid=(4,),
        in_specs=[
            SMEM_WHOLE, pl.BlockSpec((1, tokens, width), lambda g: (g, 0, 0)), *[block] * 8, once(dq.shape), once(table.shape),
            once(proj.shape),
        ],
        out_specs=[*[summed] * 4, kept, kept],
        out_shape=[*[jax.ShapeDtypeStruct((tokens, 2 * inner), BFLOAT)] * 4, piece, piece],
        scratch_shapes=[
            pltpu.VMEM((width, 2 * inner), FLOAT), pltpu.VMEM((width, inner), BFLOAT), pltpu.VMEM((tokens, 2 * inner), BFLOAT),
        ],
        compiler_params=BIG,
        cost_estimate=cost(flops=18 * tokens * width * inner, bytes_accessed=12 * tokens * width, transcendentals=0),
        name="weight_grads",
    )(place, normed, *own, *got, dq, table, proj)


def pick_block(refs, step, scratch_ref):
    cut = refs[0].shape[0]
    for index in range(4):

        @pl.when(step == index)
        def _(index=index):
            scratch_ref[:cut] = refs[2 * index][...]
            scratch_ref[cut:] = refs[2 * index + 1][...]


def pick_whole(refs, step, scratch_ref):
    for index in range(4):

        @pl.when(step == index)
        def _(index=index):
            scratch_ref[...] = refs[index][...]


def once(shape):
    return pl.BlockSpec(shape, lambda g, *_: (0,) * len(shape), pipeline_mode=pl.Buffered(1))


def norm_kernel(*refs, inner):
    pieces, (gain_ref, weight_ref, normed_ref, k0, k1, k2, k3, q_ref, x_scr) = refs[:8], refs[8:]
    step = pl.program_id(0)
    pick_block(pieces, step, x_scr)
    hidden = x_scr[...].astype(FLOAT)
    scale = lax.rsqrt(jnp.mean(hidden * hidden, axis=-1, keepdims=True) + EPSILON)
    normed = (hidden * scale * gain_ref[...]).astype(BFLOAT)
    normed_ref[0] = normed
    both = jnp.dot(normed, weight_ref[:, inner:], preferred_element_type=FLOAT).astype(BFLOAT)

    for index, kv_ref in enumerate((k0, k1, k2, k3)):

        @pl.when(step == index)
        def _(kv_ref=kv_ref):
            kv_ref[0] = both

    @pl.when(step == 0)
    def _():
        q_ref[...] = jnp.dot(normed, weight_ref[:, :inner], preferred_element_type=FLOAT).astype(BFLOAT)


def norm_project(pieces, gain, weight, inner):
    tokens, width = 2 * pieces[0].shape[0], pieces[0].shape[1]
    return pl.pallas_call(
        functools.partial(norm_kernel, inner=inner),
        grid=(4,),
        in_specs=[*[once(piece.shape) for piece in pieces], once(gain.shape), once(weight.shape)],
        out_specs=[
            pl.BlockSpec((1, tokens, width), lambda g: (g, 0, 0)),
            *[pl.BlockSpec((1, tokens, 2 * inner), lambda g: (0, 0, 0))] * 4,
            pl.BlockSpec((tokens, inner), lambda g: (0, 0)),
        ],
        out_shape=[
            jax.ShapeDtypeStruct((4, tokens, width), BFLOAT),
            *[jax.ShapeDtypeStruct((1, tokens, 2 * inner), BFLOAT)] * 4,
            jax.ShapeDtypeStruct((tokens, inner), BFLOAT),
        ],
        scratch_shapes=[pltpu.VMEM((tokens, width), BFLOAT)],
        compiler_params=BIG,
        cost_estimate=cost(
            flops=18 * tokens * width * inner, bytes_accessed=18 * tokens * width, transcendentals=0
        ),
        name="norm_project",
    )(*pieces, gain, weight)


GELU_SCALE = float(np.sqrt(2.0 / np.pi))


def late_kernel(*refs):
    attn, inputs = refs[:4], refs[4:12]
    proj_ref, gain_ref, after_ref, normed_ref, a_scr, x_scr = refs[12:]
    step = pl.program_id(0)
    pick_whole(attn, step, a_scr)
    pick_block(inputs, step, x_scr)
    after_attn = x_scr[...].astype(FLOAT) + jnp.dot(a_scr[...], proj_ref[...], preferred_element_type=FLOAT)

    @pl.when(step == 0)
    def _():
        after_ref[...] = after_attn

    scale = lax.rsqrt(jnp.mean(after_attn * after_attn, axis=-1, keepdims=True) + EPSILON)
    normed_ref[0] = (after_attn * scale * gain_ref[...]).astype(BFLOAT)


def late_norm(attn, inputs, proj, gain):
    tokens, inner = attn[0].shape
    width = proj.shape[1]
    return pl.pallas_call(
        late_kernel,
        grid=(4,),
        in_specs=[once(value.shape) for value in (*attn, *inputs, proj, gain)],
        out_specs=[
            pl.BlockSpec((tokens, width), lambda g: (0, 0)), pl.BlockSpec((1, tokens, width), lambda g: (g, 0, 0)),
        ],
        out_shape=[
            jax.ShapeDtypeStruct((tokens, width), FLOAT), jax.ShapeDtypeStruct((4, tokens, width), BFLOAT),
        ],
        scratch_shapes=[pltpu.VMEM((tokens, inner), BFLOAT), pltpu.VMEM((tokens, width), BFLOAT)],
        compiler_params=BIG,
        cost_estimate=cost(flops=8 * tokens * width * inner, bytes_accessed=24 * tokens * width, transcendentals=0),
        name="late_norm",
    )(*attn, *inputs, proj, gain)


def feed_kernel(
    spot_ref, normed_ref, cots_ref, mine_ref, other_ref, down_ref,
    act_ref, dmine_ref, dother_ref, out_ref, l0, l1, l2, l3, cot_ref,
):
    is_zero = spot_ref[0] == 0
    tokens = normed_ref.shape[1]
    cot = cots_ref[...].reshape(tokens, cots_ref.shape[2])
    cot_ref[0] = cot
    normed = normed_ref[0]
    pre_mine = jnp.dot(normed, mine_ref[...], preferred_element_type=FLOAT)
    pre_other = jnp.dot(normed, other_ref[...], preferred_element_type=FLOAT)
    gate = jnp.where(is_zero, pre_mine, pre_other)
    up = jnp.where(is_zero, pre_other, pre_mine)
    square = gate * gate
    lifted = jnp.tanh(GELU_SCALE * (gate + 0.044715 * gate * square))
    half = 0.5 * (1.0 + lifted)
    smooth = gate * half
    act = (smooth * up).astype(BFLOAT)
    act_ref[0] = act
    out = jnp.dot(act, down_ref[...], preferred_element_type=FLOAT).astype(BFLOAT)
    out_ref[...] = out.reshape(out_ref.shape)
    act_back = nt(cot, down_ref[...])
    slope = half + 0.5 * gate * (1.0 - lifted * lifted) * (GELU_SCALE * (1.0 + 3 * 0.044715 * square))
    gate_back = act_back * up * slope
    up_back = act_back * smooth
    dmine = jnp.where(is_zero, gate_back, up_back).astype(BFLOAT)
    dother = jnp.where(is_zero, up_back, gate_back).astype(BFLOAT)
    dmine_ref[0] = dmine
    dother_ref[0] = dother
    late = (nt(dmine, mine_ref[...]) + nt(dother, other_ref[...])).astype(BFLOAT)
    for index, late_ref in enumerate((l0, l1, l2, l3)):

        @pl.when(pl.program_id(0) == index)
        def _(late_ref=late_ref):
            late_ref[...] = late.reshape(late_ref.shape)


def feed_forward(spot, normed, cots, mine, other, down):
    _, tokens, width = normed.shape
    wide = mine.shape[1]

    def block(size):
        return pl.BlockSpec((1, tokens, size), lambda g, spot: (g, 0, 0))

    def shape(size):
        return jax.ShapeDtypeStruct((4, tokens, size), BFLOAT)

    placed = pl.BlockSpec((2, tokens // 2, width), lambda g, spot: (lax.bitwise_xor(g, spot[1]), 0, 0))
    sent = jax.ShapeDtypeStruct((8, tokens // 2, width), BFLOAT)
    half = jax.ShapeDtypeStruct((2, tokens // 2, width), BFLOAT)
    piece = pl.BlockSpec((2, tokens // 2, width), lambda g, spot: (0, 0, 0))
    return pl.pallas_call(
        feed_kernel,
        grid_spec=pltpu.PrefetchScalarGridSpec(
            num_scalar_prefetch=1,
            grid=(4,),
            in_specs=[block(width), placed, *[once(value.shape) for value in (mine, other, down)]],
            out_specs=[block(wide), block(wide), block(wide), placed, *[piece] * 4, block(width)],
        ),
        out_shape=[shape(wide), shape(wide), shape(wide), sent, *[half] * 4, shape(width)],
        compiler_params=BIG,
        cost_estimate=cost(
            flops=48 * tokens * width * wide, bytes_accessed=30 * tokens * width, transcendentals=4 * tokens * wide
        ),
        name="feed_forward",
    )(spot, normed, cots, mine, other, down)


def outer_kernel(left_ref, *refs):
    rights, outs, scratch = refs[: len(refs) // 3], refs[len(refs) // 3 : 2 * len(refs) // 3], refs[2 * len(refs) // 3 :]
    step = pl.program_id(0)
    for right_ref, out_ref, acc_ref in zip(rights, outs, scratch):
        part = tn(left_ref[0], right_ref[0]).reshape(out_ref.shape)

        @pl.when(step == 0)
        def _(acc_ref=acc_ref, part=part):
            acc_ref[...] = part

        @pl.when((step > 0) & (step < 3))
        def _(acc_ref=acc_ref, part=part):
            acc_ref[...] = acc_ref[...] + part

        @pl.when(step == 3)
        def _(acc_ref=acc_ref, out_ref=out_ref, part=part):
            out_ref[...] = (acc_ref[...] + part).astype(BFLOAT)


def outer_sums(left, rights, *deps):
    _, tokens, width = left.shape
    shapes = [(2, width // 2, right.shape[2]) for right in rights]
    count = len(rights)
    return pl.pallas_call(
        skipping(outer_kernel, 1 + count, len(deps)),
        grid=(4,),
        in_specs=[pl.BlockSpec((1, tokens, value.shape[2]), lambda g: (g, 0, 0)) for value in (left, *rights)]
        + [UNREAD] * len(deps),
        out_specs=[pl.BlockSpec(shape, lambda g: (0, 0, 0)) for shape in shapes],
        out_shape=[jax.ShapeDtypeStruct(shape, BFLOAT) for shape in shapes],
        scratch_shapes=[pltpu.VMEM(shape, FLOAT) for shape in shapes],
        compiler_params=BIG,
        cost_estimate=cost(flops=8 * tokens * width * 2 * sum(shape[2] for shape in shapes), bytes_accessed=0, transcendentals=0),
        name="outer_sums",
    )(left, *rights, *deps)


def norm_back(hidden, gain, back):
    scale = lax.rsqrt(jnp.mean(hidden * hidden, axis=-1, keepdims=True) + EPSILON)
    lifted = back * gain
    return scale * lifted - hidden * (scale * scale * scale) * jnp.mean(lifted * hidden, axis=-1, keepdims=True)


def quarter_specs(tile, width):
    whole = pl.BlockSpec((tile, width), lambda g: (g, 0))
    near = pl.BlockSpec((tile, width), lambda g: (jnp.minimum(g, 1), 0))
    far = pl.BlockSpec((tile, width), lambda g: (jnp.maximum(g - 2, 0), 0))
    return whole, [near, near, far, far]


def summed(own_ref, parts):
    near = pl.program_id(0) < 2
    first = jnp.where(near, parts[0][...], parts[2][...]).astype(FLOAT)
    second = jnp.where(near, parts[1][...], parts[3][...]).astype(FLOAT)
    return own_ref[...].astype(FLOAT) + first + second


def middle_kernel(after_ref, p0, p1, p2, p3, cot_ref, gain_ref, proj_ref, residual_ref, mix_ref, attn_ref):
    back = sum(ref[0].astype(FLOAT) for ref in (p0, p1, p2, p3))
    residual = cot_ref[0].astype(FLOAT) + norm_back(after_ref[...], gain_ref[...], back)
    residual_ref[...] = residual
    mix = residual.astype(BFLOAT)
    mix_ref[...] = mix
    attn_ref[...] = nt(mix, proj_ref[...]).astype(BFLOAT)


def middle(after_attn, parts, cots, gain, proj):
    tokens, width = after_attn.shape
    inner = proj.shape[0]
    tile = tokens // 4
    whole = pl.BlockSpec((tile, width), lambda g: (g, 0))
    half = pl.BlockSpec((1, tile, width), lambda g: (g // 2, g % 2, 0))
    return pl.pallas_call(
        middle_kernel,
        grid=(4,),
        in_specs=[whole, half, half, half, half, half, once(gain.shape), once(proj.shape)],
        out_specs=[whole, whole, pl.BlockSpec((tile, inner), lambda g: (g, 0))],
        out_shape=[
            jax.ShapeDtypeStruct((tokens, width), FLOAT),
            jax.ShapeDtypeStruct((tokens, width), BFLOAT),
            jax.ShapeDtypeStruct((tokens, inner), BFLOAT),
        ],
        compiler_params=BIG,
        cost_estimate=pl.CostEstimate(flops=10**11, bytes_accessed=0, transcendentals=0),
        name="middle",
    )(after_attn, *parts, cots, gain, proj)


def plus_kernel(left_ref, *refs):
    rights, out_ref = refs[:-1], refs[-1]
    for index, right_ref in enumerate(rights):

        @pl.when(pl.program_id(0) * len(rights) // pl.num_programs(0) == index)
        def _(right_ref=right_ref):
            out_ref[0] = (left_ref[0].astype(FLOAT) + right_ref[0].astype(FLOAT)).astype(BFLOAT)


def plus(left, rights, *deps):
    shape = left.shape
    each = shape[0] // len(rights)
    spec = pl.BlockSpec((1, *shape[1:]), lambda g: (g,) + (0,) * (len(shape) - 1))

    def part(index):
        return pl.BlockSpec(
            (1, *shape[1:]), lambda g: (jnp.clip(g - index * each, 0, each - 1),) + (0,) * (len(shape) - 1)
        )

    return pl.pallas_call(
        skipping(plus_kernel, 1 + len(rights), len(deps)),
        grid=(shape[0],),
        in_specs=[spec, *[part(index) for index in range(len(rights))]] + [UNREAD] * len(deps),
        out_specs=spec,
        out_shape=jax.ShapeDtypeStruct(shape, BFLOAT),
        compiler_params=BIG,
        cost_estimate=moved(left, left, left),
        name="plus",
    )(left, *rights, *deps)


def last_kernel(dq_ref, own_ref, p1, p2, p3, x0, x1, residual_ref, gain_ref, weight_ref, out_ref):
    dkv = sum(ref[...].astype(FLOAT) for ref in (own_ref, p1, p2, p3)).astype(BFLOAT)
    inner = dq_ref.shape[1]
    back = nt(dq_ref[...], weight_ref[:, :inner]) + nt(dkv, weight_ref[:, inner:])
    hidden = jnp.where(pl.program_id(0) < 2, x0[...], x1[...]).astype(FLOAT)
    out_ref[...] = (residual_ref[...] + norm_back(hidden, gain_ref[...], back)).astype(BFLOAT)


def last(dq, own, parts, inputs, residual, gain, weight):
    tokens, width = residual.shape
    inner = dq.shape[1]
    tile = tokens // 4
    whole = pl.BlockSpec((tile, width), lambda g: (g, 0))
    near = pl.BlockSpec((tile, width), lambda g: (jnp.minimum(g, 1), 0))
    far = pl.BlockSpec((tile, width), lambda g: (jnp.maximum(g - 2, 0), 0))
    piece = pl.BlockSpec((tile, 2 * inner), lambda g: (g, 0))
    return pl.pallas_call(
        last_kernel,
        grid=(4,),
        in_specs=[
            pl.BlockSpec((tile, inner), lambda g: (g, 0)), piece, piece, piece, piece, near, far, whole,
            once(gain.shape), once(weight.shape),
        ],
        out_specs=whole,
        out_shape=jax.ShapeDtypeStruct((tokens, width), BFLOAT),
        compiler_params=BIG,
        cost_estimate=cost(flops=6 * tokens * width * inner, bytes_accessed=12 * tokens * width, transcendentals=0),
        name="input_gradient",
    )(dq, own, *parts, *inputs, residual, gain, weight)


def choose(refs, slot):
    value = refs[0][...]
    for index in range(1, len(refs)):
        value = jnp.where(slot == index, refs[index][...], value)
    return value


def spread_kernel(place_ref, *refs, depth, part):
    nears, fars, (gate_ref, up_ref, gate_out, up_out, late_ref) = refs[:4], refs[4:8], refs[8:]
    low = place_ref[0]
    chip, core = low // 2, lax.rem(low, 2)
    for index in range(4):
        slot = lax.bitwise_xor(chip, jnp.int32(index))
        near, far = choose(nears, slot), choose(fars, slot)
        gate = jnp.where(core == 0, near, far).astype(FLOAT)
        up = jnp.where(core == 0, far, near).astype(FLOAT)
        for level in range(depth):
            base = (level * 4 + index) * part
            gate_out[:, base : base + part] = gate[:, level * part : (level + 1) * part]
            up_out[:, base : base + part] = up[:, level * part : (level + 1) * part]
    total = gate_out[...] * gate_ref[...].astype(FLOAT) + up_out[...] * up_ref[...].astype(FLOAT)
    late_ref[...] = jnp.broadcast_to(jnp.sum(total, axis=1, keepdims=True), late_ref.shape)


def spread(place, nears, fars, gate, up, depth, part):
    shard, hidden = gate.shape
    tile = 184 if shard % 184 == 0 else shard
    pieces = pl.BlockSpec((tile, nears[0].shape[1]), lambda g: (g, 0))
    rows = pl.BlockSpec((tile, hidden), lambda g: (g, 0))
    return pl.pallas_call(
        functools.partial(spread_kernel, depth=depth, part=part),
        grid=(shard // tile,),
        in_specs=[SMEM_WHOLE, *[pieces] * 8, rows, rows],
        out_specs=[rows, rows, pl.BlockSpec((tile, 128), lambda g: (g, 0))],
        out_shape=[
            jax.ShapeDtypeStruct((shard, hidden), FLOAT),
            jax.ShapeDtypeStruct((shard, hidden), FLOAT),
            jax.ShapeDtypeStruct((shard, 128), FLOAT),
        ],
        compiler_params=BIG,
        cost_estimate=cost(flops=4 * shard * hidden, bytes_accessed=16 * shard * hidden, transcendentals=0),
        name="spread_columns",
    )(place, *nears, *fars, gate, up)


def rows_kernel(place_ref, *refs):
    nears, fars, out_ref = refs[:4], refs[4:8], refs[8]
    low = place_ref[0]
    size = nears[0].shape[0]
    for index in range(GROUP):
        gap = lax.bitwise_xor(low, jnp.int32(index))
        slot, odd = gap // 2, lax.rem(gap, 2)
        rows = jnp.where(odd == 0, choose(nears, slot), choose(fars, slot))
        out_ref[index * size : (index + 1) * size, :] = rows.astype(FLOAT)


def finish_kernel(
    place_ref, near_ref, far_ref, q_ref, k_ref, v_ref, q_out, k_out, v_out, proj_out, early_ref, table_ref, *, size, wide
):
    low = place_ref[0]
    shard, inner = q_ref.shape
    part = proj_out.shape[0] // 2
    each = part // 3
    for index in range(GROUP):
        gap = lax.bitwise_xor(low, jnp.int32(index))
        slot, odd = gap // 2, lax.rem(gap, 2)
        block = jnp.where(odd == 0, near_ref[slot], far_ref[slot]).astype(FLOAT)
        base = min(index * size, shard - size)
        skip = index * size - base
        q_out[base + skip : base + size, :] = block[skip:size, :inner]
        for pair in range(inner // 128):
            for offset, out_ref in enumerate((k_out, v_out)):
                column = inner + 256 * pair + 128 * offset
                out_ref[base + skip : base + size, 128 * pair : 128 * pair + 128] = block[skip:size, column : column + 128]
        if index == GROUP - 1:
            table_ref[...] = block[:16, :128]
        column = (index // 2) * wide
        reach = min(wide, proj_out.shape[1] - column)
        for lane in range(3):
            base = (index % 2) * part + lane * each
            proj_out[base : base + each, column : column + reach] = block[size:, lane * wide : lane * wide + reach]
    total = q_out[...] * q_ref[...].astype(FLOAT) + k_out[...] * k_ref[...].astype(FLOAT)
    total = total + v_out[...] * v_ref[...].astype(FLOAT)
    early_ref[...] = jnp.broadcast_to(jnp.sum(total, axis=1, keepdims=True), early_ref.shape)


def rows_of_kernel(x_ref, cot_ref, near_ref, far_ref, rows_ref):
    rows, cut = x_ref.shape[2], near_ref.shape[0]
    for seq in range(x_ref.shape[0]):
        turned = jnp.transpose(x_ref[seq])
        start = seq * rows
        split = min(max(cut - start, 0), rows)
        if split > 0:
            near_ref[start : start + split, :] = turned[:split]
        if split < rows:
            far_ref[start + split - cut : start + rows - cut, :] = turned[split:]
        turned = jnp.transpose(cot_ref[seq])
        for copy in range(4):
            if split > 0:
                rows_ref[2 * copy, start : start + split, :] = turned[:split]
            if split < rows:
                rows_ref[2 * copy + 1, start + split - cut : start + rows - cut, :] = turned[split:]


def on_device(
    layer_input, segments, cotangent, query_weight, key_weight, value_weight, projection, gate_weight, up_weight,
    down_weight, gain_early, gain_late, bias_table,
):
    ring = lax.axis_size("ctx")
    depth = lax.axis_size("wsh")
    groups = ring // GROUP
    mine = lax.axis_index("ctx")
    low = lax.rem(mine, GROUP)
    chip, core = low // 2, lax.rem(low, 2)
    zed = lax.axis_index("wsh")
    seqs, rows, width = layer_input.shape
    inner = query_weight.shape[1]
    heads = bias_table.shape[1]
    shard = width // depth
    slab = gate_weight.shape[1] // depth
    part = slab // 4
    piece = part // 2
    tokens = seqs * rows
    cut = tokens // 2
    buckets = BUCKETS // depth
    size, wide = slice_size(shard), column_cut(width)
    each = inner // depth // 6
    upper = [[group * GROUP + index for group in range(groups)] for index in range(GROUP)]
    is_zero = core == 0
    place = jnp.stack((low, zed)).astype(jnp.int32)
    meta = mine.astype(jnp.int32).reshape(1)
    spot = jnp.stack((core, chip)).astype(jnp.int32)

    half = jax.ShapeDtypeStruct((cut, width), BFLOAT)
    chips = [[group * GROUP + 2 * index + side for index in range(4)] for group in range(groups) for side in range(2)]

    def exchange(blocks):
        return lax.all_to_all(blocks, "ctx", split_axis=0, concat_axis=0, tiled=True, axis_index_groups=chips)

    x_near, x_far, own_cots = pl.pallas_call(
        rows_of_kernel,
        in_specs=[VMEM_WHOLE] * 2,
        out_specs=[VMEM_WHOLE] * 3,
        out_shape=[half, half, jax.ShapeDtypeStruct((8, cut, width), BFLOAT)],
        compiler_params=BIG,
        cost_estimate=moved(layer_input, layer_input, cotangent, cotangent),
        name="token_rows",
    )(jnp.swapaxes(layer_input, 1, 2), jnp.swapaxes(cotangent, 1, 2))
    inputs = gather_halves((x_near, x_far))

    def columns(weight):
        return jnp.concatenate(
            [lax.dynamic_slice_in_dim(weight, index * slab + chip * part, part, 1) for index in range(depth)], axis=1
        )

    pair_slice = jnp.where(is_zero, columns(gate_weight), columns(up_weight))
    down_slice = lax.dynamic_slice_in_dim(down_weight, chip * part + core * piece, piece, 0)

    packed = pl.pallas_call(
        functools.partial(pack_kernel, size=size, wide=wide),
        in_specs=[SMEM_WHOLE] + [VMEM_WHOLE] * 7,
        out_specs=VMEM_WHOLE,
        out_shape=jax.ShapeDtypeStruct((size + each + 16, 3 * inner), BFLOAT),
        cost_estimate=moved(query_weight, query_weight),
        name="pack",
    )(
        after(place, pair_slice, down_slice), query_weight, key_weight, value_weight, projection, gain_early.reshape(1, shard), gain_late.reshape(1, shard),
        jnp.pad(bias_table, ((0, 8 - buckets), (0, 128 - heads))),
    )
    packed = lax.all_gather(packed, "wsh", axis=0)
    pair_mine = lax.all_gather(after(pair_slice, packed), "wsh", axis=0, tiled=True)
    seg_rows = jnp.pad(segments.astype(BFLOAT), ((0, 16 - seqs), (0, 3 * inner - rows)))
    small = jnp.concatenate((packed[:, : size + each].reshape(-1, 3 * inner), seg_rows), axis=0)
    small = after(small, *inputs[2:6])
    near = gather_relay(small, small.shape[0] // 32 * 16)
    far = swap(near, 1)
    down_mine = lax.all_gather(after(down_slice, near), "wsh", axis=0, tiled=True).reshape(depth, piece, width)
    qkv_full, proj_full, gains, table, segs = pl.pallas_call(
        functools.partial(unpack_kernel, depth=depth, size=size, wide=wide),
        in_specs=[SMEM_WHOLE, VMEM_WHOLE, VMEM_WHOLE, VMEM_WHOLE],
        out_specs=[VMEM_WHOLE] * 5,
        out_shape=[
            jax.ShapeDtypeStruct((width, 3 * inner), BFLOAT),
            jax.ShapeDtypeStruct((inner, width), BFLOAT),
            jax.ShapeDtypeStruct((8, width), FLOAT),
            jax.ShapeDtypeStruct((BUCKETS, 128), FLOAT),
            jax.ShapeDtypeStruct((seqs, GROUP, rows), FLOAT),
        ],
        compiler_params=BIG,
        cost_estimate=moved(near, far, near),
        name="unpack",
    )(place, packed[:, size + each :], near, far)

    def whole(value, axis=0):
        if groups == 1:
            return value
        return lax.all_gather(value, "ctx", axis=axis, tiled=True, axis_index_groups=upper)

    segs = whole(segs, 1)

    normed, *kv, queries = norm_project(inputs, gains[0:1], qkv_full, inner)
    cots = exchange(own_cots)
    kv = [value.reshape(1, seqs, rows, 2 * inner) for value in kv]
    queries = queries.reshape(seqs, rows, inner)
    kv = [whole(value) for value in (*kv, *[swap(value, 1) for value in kv])]
    attention, lse = attention_forward(meta, table, segs, queries, kv)
    attn_low = attention.astype(BFLOAT).reshape(tokens, inner)
    attn = gather_direct(attn_low)

    after_attn, normed_late = late_norm(attn, inputs, proj_full, gains[1:2])
    pair_mine = after(pair_mine, attn_low)
    pair_other = swap(pair_mine, 1)
    down_mine = after(down_mine, attn_low)
    down_other = swap(down_mine, 1)
    down_full = jnp.where(
        is_zero, jnp.stack((down_mine, down_other), axis=1), jnp.stack((down_other, down_mine), axis=1)
    ).reshape(depth * part, width)
    activation, back_mine, back_other, out_part, *late_part, cot_all = feed_forward(
        spot, normed_late, cots, pair_mine, pair_other, down_full
    )

    def flat(value):
        return value.reshape(4 * tokens, value.shape[2])

    def over_groups(value):
        return lax.psum(value, "ctx", axis_index_groups=upper) if groups > 1 else value

    late_parts = [late_part[0]] + [swap(late_part[index], 2 * index) for index in range(1, 4)]
    other_grad, mine_grad = outer_sums(normed_late, (back_other, back_mine))
    other_got = [swap(other_grad[index : index + 1], 1) for index in range(2)]
    down_grad = outer_sums(activation, (cot_all,))[0].reshape(depth, 2, piece, width)
    down_keep = jnp.where(is_zero, down_grad[:, 0], down_grad[:, 1])
    down_send = jnp.where(is_zero, down_grad[:, 1], down_grad[:, 0])
    down_got = swap(down_send, 1)
    residual_grad, mix_low, attn_grad = middle(after_attn, late_parts, own_cots, gains[1:2], proj_full)
    pair_sum = plus(mine_grad, other_got, mix_low).reshape(width, 2 * piece * depth)
    down_sum = plus(down_keep, [down_got], pair_sum).reshape(depth * piece, width)
    pair_own = over_groups(lax.psum_scatter(pair_sum, "wsh", scatter_dimension=0, tiled=True))
    down_own = over_groups(lax.psum_scatter(down_sum, "wsh", scatter_dimension=0, tiled=True))
    attn_grad = attn_grad.reshape(seqs, rows, inner)
    proj_grad = tn(attn_low, jnp.pad(mix_low, ((0, 0), (0, 4 * wide - width)))).astype(BFLOAT)
    dq, *dkv, table_part = attention_backward(
        meta, table, segs, queries, kv, attn_grad, attention, lse, down_sum
    )

    def owned(value):
        if groups > 1:
            value = lax.psum_scatter(value, "ctx", scatter_dimension=0, tiled=True, axis_index_groups=upper)
        return value.reshape(1, tokens, 2 * inner)

    dkv = [owned(value) for value in dkv]
    dkv_got = [swap(value, 1) for value in dkv[4:]]
    dq = dq.reshape(tokens, inner)
    table_sum = jnp.transpose(jnp.sum(table_part, axis=-1).reshape(heads, BUCKETS)).reshape(depth, buckets, heads)
    table_sum = jnp.pad(table_sum, ((0, 0), (0, 16 - buckets), (0, 128 - heads))).reshape(depth * 16, 128).astype(BFLOAT)
    *dkv_four, keep, send = weight_grads(place, normed, dkv[:4], dkv_got, dq, table_sum, proj_grad, depth, size, wide)
    out_parts = exchange(out_part).astype(FLOAT).reshape(4, tokens, width)
    result = (after_attn + jnp.sum(out_parts, axis=0)).astype(BFLOAT)

    blocks = plus(keep, [swap(send, 1)], result)
    dkv_parts = [swap(dkv_four[index], 2 * index) for index in range(1, 4)]
    total = blocks[0].astype(FLOAT)
    for index in range(1, 4):
        total = total + swap(blocks[index], 2 * index).astype(FLOAT)
    levels = total.astype(BFLOAT)
    total = levels[0].astype(FLOAT)
    for gap in range(1, depth):
        total = total + swap_depth(levels[gap], gap).astype(FLOAT)
    input_grad = last(dq, dkv_four[0], dkv_parts, (x_near, x_far), residual_grad, gains[0:1], qkv_full)
    grads_near = jnp.stack(gather_direct(over_groups(total.astype(BFLOAT))))
    grads_far = swap(grads_near, 1)
    column = jax.ShapeDtypeStruct((shard, inner), FLOAT)
    query_out, key_out, value_out, proj_out, early_sum, table_rows = pl.pallas_call(
        functools.partial(finish_kernel, size=size, wide=wide),
        in_specs=[SMEM_WHOLE] + [VMEM_WHOLE] * 5,
        out_specs=[VMEM_WHOLE] * 6,
        out_shape=[
            column, column, column, jax.ShapeDtypeStruct((inner // depth, width), FLOAT),
            jax.ShapeDtypeStruct((shard, 128), FLOAT), jax.ShapeDtypeStruct((16, 128), FLOAT),
        ],
        compiler_params=BIG,
        cost_estimate=moved(grads_near, grads_far, grads_near),
        name="finish_small",
    )(place, grads_near, grads_far, query_weight, key_weight, value_weight)

    pair_own, down_own = after(pair_own, levels), after(down_own, levels)
    pair_near, down_near = gather_direct(pair_own), gather_direct(down_own)
    pair_far, down_far = [[swap(value, 1) for value in values] for values in (pair_near, down_near)]
    gate_out, up_out, late_sum = spread(place, pair_near, pair_far, gate_weight, up_weight, depth, part)
    down_out = pl.pallas_call(
        rows_kernel,
        in_specs=[SMEM_WHOLE] + [VMEM_WHOLE] * 8,
        out_specs=VMEM_WHOLE,
        out_shape=jax.ShapeDtypeStruct((slab, width), FLOAT),
        compiler_params=BIG,
        cost_estimate=moved(down_own, down_own, down_own),
        name="join_down",
    )(place, *down_near, *down_far)
    return (
        result.reshape(seqs, rows, width),
        input_grad.reshape(seqs, rows, width),
        query_out,
        key_out,
        value_out,
        proj_out,
        gate_out,
        up_out,
        down_out,
        early_sum[:, 0] / gain_early.astype(FLOAT),
        late_sum[:, 0] / gain_late.astype(FLOAT),
        table_rows[:buckets, :heads],
    )


def solution(mesh):
    rows = P("wsh", "ctx", None)
    split = P("wsh", None)
    vector = P("wsh")
    return jax.shard_map(
        on_device,
        mesh=mesh,
        in_specs=(rows, P("wsh", "ctx"), rows, split, split, split, split, split, split, split, vector, vector, split),
        out_specs=(rows, rows, split, split, split, split, split, split, split, vector, vector, split),
        check_vma=False,
    )
```

```python
import functools

import jax
import jax.numpy as jnp
import numpy as np
from jax import lax
from jax.experimental import pallas as pl
from jax.experimental.pallas import tpu as pltpu
from jax.sharding import PartitionSpec as P

BUCKETS = 32
GROUP = 8
EPSILON = 1e-06
NEGATIVE = -1e30
PRECISE = lax.Precision.HIGHEST
BUCKET_EDGES = (12, 16, 23, 32, 46, 64, 91)
FLOAT = jnp.float32
BFLOAT = jnp.bfloat16


SCALE = 0.2


def cost(flops, bytes_accessed, transcendentals):
    return pl.CostEstimate(
        flops=int(SCALE * flops), bytes_accessed=int(SCALE * bytes_accessed), transcendentals=int(SCALE * transcendentals)
    )


def bucket_number(offset):
    distance = abs(offset)
    level = distance if distance < 8 else 8 + sum(distance >= edge for edge in BUCKET_EDGES)
    return level + (16 if offset > 0 else 0)


def bucket_of(offsets):
    distance = jnp.abs(offsets)
    coarse = 8 + sum(((distance >= boundary).astype(jnp.int32) for boundary in BUCKET_EDGES))
    level = jnp.where(distance < 8, distance, coarse)
    return level + jnp.where(offsets > 0, 16, 0)


def near_radius(rows):
    return -(-(BUCKET_EDGES[-1] - 1) // rows)


def tile_offsets(block_gap, rows):
    keys = lax.broadcasted_iota(jnp.int32, (rows, rows), 0)
    queries = lax.broadcasted_iota(jnp.int32, (rows, rows), 1)
    return block_gap * rows + keys - queries


def tile_buckets(block_gap, rows):
    low, high = block_gap * rows - (rows - 1), block_gap * rows + (rows - 1)
    return sorted({bucket_number(offset) for offset in range(low, high + 1)})


def nt(left, right):
    return lax.dot_general(left, right, (((1,), (1,)), ((), ())), preferred_element_type=FLOAT)


def tn(left, right):
    return lax.dot_general(left, right, (((0,), (0,)), ((), ())), preferred_element_type=FLOAT)


def block_number(meta, half, position, count):
    low = lax.rem(meta, GROUP)
    part, group = divmod(position, count // 4)
    return group * GROUP + lax.bitwise_xor(low, jnp.int32(2 * part + half))


def tile_index(meta, half, position, count, radius):
    gap = block_number(meta, half, position, count) - meta
    return jnp.clip(gap, -(radius + 1), radius + 1) + radius + 1


def build_bias(bias_ref, table_ref, pair, rows, radius):
    for side, bucket in ((0, 15), (2 * radius + 2, 31)):
        for head in range(2):
            bias_ref[head, side] = jnp.full((rows, rows), table_ref[bucket, 2 * pair + head], FLOAT)
    for gap in range(-radius, radius + 1):
        buckets = bucket_of(tile_offsets(gap, rows))
        present = tile_buckets(gap, rows)
        tiles = [jnp.full((rows, rows), table_ref[present[0], 2 * pair + head], FLOAT) for head in range(2)]
        for bucket in present[1:]:
            hit = buckets == bucket
            tiles = [jnp.where(hit, table_ref[bucket, 2 * pair + head], tiles[head]) for head in range(2)]
        for head in range(2):
            bias_ref[head, gap + radius + 1] = tiles[head]


def build_mask(mask_ref, segs_ref, meta, seq, rows, count):
    own = segs_ref[seq, pl.ds(meta, 1), :]
    for half in range(2):
        for position in range(count):
            row = segs_ref[seq, pl.ds(block_number(meta, half, position, count), 1), :]
            keys = jnp.transpose(jnp.broadcast_to(row, (rows, rows)))
            mask_ref[seq, half * count + position] = jnp.where(keys == own, 0.0, NEGATIVE)


def half_scores(keys, query, meta, head, half, seq, bias_ref, mask_ref, rows, count, radius):
    raw = nt(keys, query)
    parts = []
    for position in range(count):
        extra = bias_ref[head, tile_index(meta, half, position, count, radius)]
        masked = mask_ref[seq, half * count + position]
        parts.append(raw[position * rows : (position + 1) * rows] + (extra + masked))
    return jnp.concatenate(parts, axis=0)


def joined(refs):
    return jnp.concatenate([ref[...].reshape(-1, ref.shape[-1]) for ref in refs], axis=0)


def head_rows(value, head, lane):
    return jnp.where((lane < 64) == (head == 0), value, jnp.zeros_like(value))


def forward_kernel(
    meta_ref, table_ref, segs_ref, q_ref, *refs, rows, count, radius,
):
    key_refs, value_refs, (out_ref, lse_ref, bias_ref, mask_ref) = refs[:8], refs[8:16], refs[16:]
    pair, seq = pl.program_id(0), pl.program_id(1)
    meta = meta_ref[0]

    @pl.when(seq == 0)
    def _():
        build_bias(bias_ref, table_ref, pair, rows, radius)

    @pl.when(pair == 0)
    def _():
        build_mask(mask_ref, segs_ref, meta, seq, rows, count)

    query = q_ref[0]
    lane = lax.broadcasted_iota(jnp.int32, query.shape, 1)
    keys = [joined(key_refs[:4]), joined(key_refs[4:])]
    values = [joined(value_refs[:4]), joined(value_refs[4:])]
    pieces = []
    for head in range(2):
        one = head_rows(query, head, lane)
        scores = [
            half_scores(keys[half], one, meta, head, half, seq, bias_ref, mask_ref, rows, count, radius)
            for half in range(2)
        ]
        top = jnp.maximum(jnp.max(scores[0], axis=0, keepdims=True), jnp.max(scores[1], axis=0, keepdims=True))
        raised = [jnp.exp(part - top) for part in scores]
        total = jnp.sum(raised[0], axis=0, keepdims=True) + jnp.sum(raised[1], axis=0, keepdims=True)
        scale = 1.0 / total
        mixed = sum(tn(values[half], (raised[half] * scale).astype(BFLOAT)) for half in range(2))
        pieces.append(mixed[64 * head : 64 * head + 64])
        lse_ref[0, 0, head : head + 1] = top + jnp.log(total)
    out_ref[0] = jnp.transpose(jnp.concatenate(pieces, axis=0))


def backward_kernel(
    meta_ref, table_ref, segs_ref, q_ref, *refs, rows, count, radius,
):
    key_refs, value_refs, (do_ref, out_ref, lse_ref, dq_ref) = refs[:8], refs[8:16], refs[16:20]
    both_refs, (tab_ref, bias_ref, mask_ref, sum_ref) = refs[20:28], refs[28:]
    pair, seq = pl.program_id(0), pl.program_id(1)
    meta = meta_ref[0]

    @pl.when(seq == 0)
    def _():
        build_bias(bias_ref, table_ref, pair, rows, radius)
        sum_ref[...] = jnp.zeros_like(sum_ref)

    @pl.when(pair == 0)
    def _():
        build_mask(mask_ref, segs_ref, meta, seq, rows, count)

    query, grad = q_ref[0], do_ref[0]
    lane = lax.broadcasted_iota(jnp.int32, query.shape, 1)
    keys = [joined(key_refs[:4]), joined(key_refs[4:])]
    values = [joined(value_refs[:4]), joined(value_refs[4:])]
    picks = (
        lax.broadcasted_iota(jnp.int32, (8, 128), 1) // 64 == lax.broadcasted_iota(jnp.int32, (8, 128), 0)
    ).astype(FLOAT)
    deltas = lax.dot_general(
        picks, grad.astype(FLOAT) * out_ref[0], (((1,), (1,)), ((), ())), precision=PRECISE, preferred_element_type=FLOAT
    )
    query_heads = [head_rows(query, head, lane) for head in range(2)]
    grad_heads = [head_rows(grad, head, lane) for head in range(2)]
    probs, slopes = [[], []], [[], []]
    pieces = []
    for head in range(2):
        logsum = lse_ref[0, 0, head : head + 1]
        delta = deltas[head : head + 1]
        flow = None
        for half in range(2):
            scores = half_scores(
                keys[half], query_heads[head], meta, head, half, seq, bias_ref, mask_ref, rows, count, radius
            )
            prob = jnp.exp(scores - logsum)
            slope = prob * (nt(values[half], grad_heads[head]) - delta)
            for position in range(count):
                index = tile_index(meta, half, position, count, radius)
                sum_ref[head, index] = sum_ref[head, index] + slope[position * rows : (position + 1) * rows]
            slope_low = slope.astype(BFLOAT)
            probs[half].append(prob.astype(BFLOAT))
            slopes[half].append(slope_low)
            term = tn(keys[half], slope_low)
            flow = term if flow is None else flow + term
        pieces.append(flow[64 * head : 64 * head + 64])
    dq_ref[0] = jnp.transpose(jnp.concatenate(pieces, axis=0)).astype(BFLOAT)
    query_stack = jnp.concatenate(query_heads, axis=0)
    grad_stack = jnp.concatenate(grad_heads, axis=0)
    for half in range(2):
        dk = jnp.dot(jnp.concatenate(slopes[half], axis=1), query_stack, preferred_element_type=FLOAT)
        dv = jnp.dot(jnp.concatenate(probs[half], axis=1), grad_stack, preferred_element_type=FLOAT)
        dk = dk.astype(BFLOAT).reshape(count, 1, rows, 128)
        dv = dv.astype(BFLOAT).reshape(count, 1, rows, 128)
        for part, both_ref in enumerate(both_refs[4 * half : 4 * half + 4]):
            side = slice(part * count // 4, (part + 1) * count // 4)
            both_ref[:, :, :, :128] = dk[side]
            both_ref[:, :, :, 128:] = dv[side]

    @pl.when(seq == pl.num_programs(1) - 1)
    def _():
        for head in range(2):
            sums = {}
            for side, bucket in ((0, 15), (2 * radius + 2, 31)):
                sums[bucket] = jnp.sum(sum_ref[head, side], axis=0, keepdims=True)
            for gap in range(-radius, radius + 1):
                buckets = bucket_of(tile_offsets(gap, rows))
                tile = sum_ref[head, gap + radius + 1]
                for bucket in tile_buckets(gap, rows):
                    part = jnp.sum(jnp.where(buckets == bucket, tile, 0.0), axis=0, keepdims=True)
                    sums[bucket] = sums[bucket] + part if bucket in sums else part
            for bucket in range(BUCKETS):
                tab_ref[0, head, bucket : bucket + 1] = sums.get(bucket, jnp.zeros((1, rows), FLOAT))


def attention_specs(seqs, rows, count, blocks, pairs):
    small = [
        pl.BlockSpec(memory_space=pltpu.SMEM),
        pl.BlockSpec(memory_space=pltpu.SMEM),
        pl.BlockSpec((seqs, blocks, rows), lambda p, s: (0, 0, 0)),
    ]
    query = pl.BlockSpec((1, rows, 128), lambda p, s: (s, 0, p))
    key = pl.BlockSpec((count // 4, 1, rows, 128), lambda p, s: (0, s, 0, 2 * p))
    value = pl.BlockSpec((count // 4, 1, rows, 128), lambda p, s: (0, s, 0, 2 * p + 1))
    stat = pl.BlockSpec((1, 1, 8, rows), lambda p, s: (p, s, 0, 0))
    return small, query, key, value, stat


def attention_scratch(seqs, rows, count, radius):
    return [
        pltpu.VMEM((2, 2 * radius + 3, rows, rows), FLOAT),
        pltpu.VMEM((seqs, 2 * count, rows, rows), FLOAT),
    ]


def attention_cost(seqs, rows, keys, width, products):
    return cost(
        flops=2 * products * seqs * rows * keys * width,
        bytes_accessed=4 * seqs * keys * width * products,
        transcendentals=seqs * rows * keys * width // 64,
    )


def attention_forward(meta, table, segs, queries, kv):
    seqs, rows, inner = queries.shape
    count, blocks, pairs = 4 * kv[0].shape[0], segs.shape[1], inner // 128
    radius = near_radius(rows)
    small, query, key, value, stat = attention_specs(seqs, rows, count, blocks, pairs)
    return pl.pallas_call(
        functools.partial(forward_kernel, rows=rows, count=count, radius=radius),
        grid=(pairs, seqs),
        in_specs=[*small, query, *[key] * 8, *[value] * 8],
        out_specs=[query, stat],
        out_shape=[
            jax.ShapeDtypeStruct((seqs, rows, inner), FLOAT),
            jax.ShapeDtypeStruct((pairs, seqs, 8, rows), FLOAT),
        ],
        scratch_shapes=attention_scratch(seqs, rows, count, radius),
        cost_estimate=attention_cost(seqs, rows, blocks * rows, inner, 2),
        name="attention_forward",
    )(meta, table, segs, queries, *kv, *kv)


def attention_backward(meta, table, segs, queries, kv, grad, out, lse, *deps):
    seqs, rows, inner = queries.shape
    count, blocks, pairs = 4 * kv[0].shape[0], segs.shape[1], inner // 128
    radius = near_radius(rows)
    small, query, key, value, stat = attention_specs(seqs, rows, count, blocks, pairs)
    side = jax.ShapeDtypeStruct((count // 4, seqs, rows, 2 * inner), BFLOAT)
    both = pl.BlockSpec((count // 4, 1, rows, 256), lambda p, s: (0, s, 0, p))
    return pl.pallas_call(
        skipping(functools.partial(backward_kernel, rows=rows, count=count, radius=radius), 23, len(deps)),
        grid=(pairs, seqs),
        in_specs=[*small, query, *[key] * 8, *[value] * 8, query, query, stat] + [UNREAD] * len(deps),
        out_specs=[query, *[both] * 8, pl.BlockSpec((1, 2, BUCKETS, rows), lambda p, s: (p, 0, 0, 0))],
        out_shape=[
            jax.ShapeDtypeStruct((seqs, rows, inner), BFLOAT), *[side] * 8,
            jax.ShapeDtypeStruct((pairs, 2, BUCKETS, rows), FLOAT),
        ],
        scratch_shapes=[
            *attention_scratch(seqs, rows, count, radius),
            pltpu.VMEM((2, 2 * radius + 3, rows, rows), FLOAT),
        ],
        cost_estimate=attention_cost(seqs, rows, blocks * rows, inner, 5),
        name="attention_backward",
    )(meta, table, segs, queries, *kv, *kv, grad, out, lse, *deps)


def swap(value, bit):
    count = lax.axis_size("ctx")
    return lax.ppermute(value, "ctx", [(source, source ^ bit) for source in range(count)])


def swap_depth(value, bit):
    count = lax.axis_size("wsh")
    return lax.ppermute(value, "wsh", [(source, source ^ bit) for source in range(count)])


def after(value, *others):
    return lax.optimization_barrier((value, *others))[0]


def gather_halves(own):
    near, far = own
    first_near, second_far = swap(near, 2), swap(far, 4)
    first_far, second_near = swap(far, 2), swap(near, 4)
    return [near, far, first_near, first_far, second_near, second_far, swap(first_near, 4), swap(second_far, 2)]


def gather_direct(own):
    return [own, swap(own, 2), swap(own, 4), swap(own, 6)]


def gather_relay(own, cut):
    first, second = swap(own, 2), swap(own, 4)
    return jnp.stack((own, first, second, jnp.concatenate((swap(first[:cut], 4), swap(second[cut:], 2)), axis=0)))


VMEM_WHOLE = pl.BlockSpec(memory_space=pltpu.VMEM)
UNREAD = pl.BlockSpec(memory_space=pl.ANY)


def skipping(kernel, inputs, count):
    return lambda *refs: kernel(*refs[:inputs], *refs[inputs + count :])


SMEM_WHOLE = pl.BlockSpec(memory_space=pltpu.SMEM)
BIG = pltpu.CompilerParams(vmem_limit_bytes=60 * 1024 * 1024)


def moved(*arrays):
    return cost(
        flops=0, bytes_accessed=sum(int(np.prod(array.shape)) * array.dtype.itemsize for array in arrays), transcendentals=0
    )


def slice_size(total):
    return -(-total // (GROUP * 16)) * 16


def slice_start(index, total, size):
    return jnp.minimum(index * size, total - size)


def column_cut(width):
    return -(-width // 512) * 128


def pack_kernel(place_ref, q_ref, k_ref, v_ref, proj_ref, early_ref, late_ref, table_ref, out_ref, *, size, wide):
    low = place_ref[0]
    chip, core = low // 2, lax.rem(low, 2)
    inner = q_ref.shape[1]
    shard = q_ref.shape[0]
    start = pl.multiple_of(slice_start(low, shard, size), 16)
    out_ref[:size, :inner] = q_ref[pl.ds(start, size), :]
    for index, ref in enumerate((k_ref, v_ref)):
        rows = ref[pl.ds(start, size), :]
        for pair in range(inner // 128):
            base = inner + 256 * pair + 128 * index
            out_ref[:size, base : base + 128] = rows[:, 128 * pair : 128 * pair + 128]
    part = proj_ref.shape[0] // 2
    each = part // 3
    out_ref[size:, :] = jnp.zeros((out_ref.shape[0] - size, out_ref.shape[1]), BFLOAT)
    for column in range(4):
        reach = min(wide, proj_ref.shape[1] - column * wide)

        @pl.when(chip == column)
        def _(column=column, reach=reach):
            for lane in range(3):
                row = pl.multiple_of(core * part + lane * each, 16)
                out_ref[size : size + each, lane * wide : lane * wide + reach] = proj_ref[
                    pl.ds(row, each), column * wide : column * wide + reach
                ]

    base = size + each
    out_ref[base : base + 1, :shard] = early_ref[...]
    out_ref[base + 1 : base + 2, :shard] = late_ref[...]
    out_ref[base + 8 : base + 16, :128] = table_ref[...]


def unpack_kernel(place_ref, misc_ref, near_ref, far_ref, qkv_ref, proj_ref, gains_ref, table_ref, segs_ref, *, depth, size, wide):
    low = place_ref[0]
    shard, part = qkv_ref.shape[0] // depth, proj_ref.shape[0] // depth // 2
    each = part // 3
    span = size + each
    buckets = table_ref.shape[0] // depth
    for level in range(depth):
        rows = misc_ref[level].astype(FLOAT)
        gains_ref[:, level * shard : (level + 1) * shard] = rows[:8, :shard]
        table_ref[level * buckets : (level + 1) * buckets, :] = rows[8 : 8 + buckets, :128]
    seqs, _, rows = segs_ref.shape
    for index in range(GROUP):
        gap = lax.bitwise_xor(low, jnp.int32(index))
        slot, odd = gap // 2, lax.rem(gap, 2)
        block = jnp.where(odd == 0, near_ref[slot], far_ref[slot])
        for level in range(depth):
            base = level * shard + min(index * size, shard - size)
            qkv_ref[base : base + size, :] = block[level * span : level * span + size]
            column = (index // 2) * wide
            reach = min(wide, proj_ref.shape[1] - column)
            for lane in range(3):
                base = (level * 2 + index % 2) * part + lane * each
                proj_ref[base : base + each, column : column + reach] = block[
                    level * span + size : level * span + span, lane * wide : lane * wide + reach
                ]
        own = block[depth * span : depth * span + 16, :128].astype(FLOAT)
        for seq in range(seqs):
            segs_ref[seq, index : index + 1, :] = own[seq : seq + 1, :rows]


def grad_kernel(
    place_ref, normed_ref, *refs, depth, size, wide
):
    owns, gots, (dq_ref, table_ref, proj_ref) = refs[:4], refs[4:8], refs[8:11]
    sums, (keep_ref, send_ref, kv_scr, q_scr, t_scr) = refs[11:15], refs[15:]
    step = pl.program_id(0)
    for index in range(4):

        @pl.when(step == index)
        def _(index=index):
            total = (owns[index][0].astype(FLOAT) + gots[index][0].astype(FLOAT)).astype(BFLOAT)
            t_scr[...] = total
            sums[index][...] = total

    part = tn(normed_ref[0], t_scr[...])

    @pl.when(step == 0)
    def _():
        kv_scr[...] = part
        q_scr[...] = tn(normed_ref[0], dq_ref[...]).astype(BFLOAT)

    @pl.when(step > 0)
    def _():
        kv_scr[...] = kv_scr[...] + part

    @pl.when(step == 3)
    def _():
        low = place_ref[0]
        zed = place_ref[1]
        inner = q_scr.shape[1]
        shard = q_scr.shape[0] // depth
        for index in range(GROUP):
            target = lax.bitwise_xor(low, jnp.int32(index))
            out_ref = keep_ref if index % 2 == 0 else send_ref
            for gap in range(depth):
                level = lax.bitwise_xor(zed, jnp.int32(gap))
                start = pl.multiple_of(level * shard + slice_start(target, shard, size), 16)
                out_ref[index // 2, gap, :size, :inner] = q_scr[pl.ds(start, size), :]
                out_ref[index // 2, gap, :size, inner:] = kv_scr[pl.ds(start, size), :].astype(BFLOAT)
                part = proj_ref.shape[0] // depth // 2
                each = part // 3
                column = pl.multiple_of((target // 2) * wide, 128)
                for lane in range(3):
                    row = pl.multiple_of((level * 2 + lax.rem(target, 2)) * part + lane * each, 16)
                    out_ref[index // 2, gap, size:, lane * wide : (lane + 1) * wide] = proj_ref[
                        pl.ds(row, each), pl.ds(column, wide)
                    ]
                last = target == GROUP - 1
                rows = table_ref[pl.ds(pl.multiple_of(level * 16, 16), 16), :]
                out_ref[index // 2, gap, :16, :128] = jnp.where(last, rows, out_ref[index // 2, gap, :16, :128])


def weight_grads(place, normed, own, got, dq, table, proj, depth, size, wide, *deps):
    _, tokens, width = normed.shape
    inner = dq.shape[1]
    block = once((1, tokens, 2 * inner))
    summed = pl.BlockSpec((tokens, 2 * inner), lambda g: (0, 0))
    span = size + proj.shape[0] // depth // 6
    piece = jax.ShapeDtypeStruct((4, depth, span, 3 * inner), BFLOAT)
    kept = pl.BlockSpec((4, depth, span, 3 * inner), lambda g: (0, 0, 0, 0))
    return pl.pallas_call(
        skipping(functools.partial(grad_kernel, depth=depth, size=size, wide=wide), 13, len(deps)),
        grid=(4,),
        in_specs=[
            SMEM_WHOLE, pl.BlockSpec((1, tokens, width), lambda g: (g, 0, 0)), *[block] * 8, once(dq.shape), once(table.shape),
            once(proj.shape),
        ]
        + [UNREAD] * len(deps),
        out_specs=[*[summed] * 4, kept, kept],
        out_shape=[*[jax.ShapeDtypeStruct((tokens, 2 * inner), BFLOAT)] * 4, piece, piece],
        scratch_shapes=[
            pltpu.VMEM((width, 2 * inner), FLOAT), pltpu.VMEM((width, inner), BFLOAT), pltpu.VMEM((tokens, 2 * inner), BFLOAT),
        ],
        compiler_params=BIG,
        cost_estimate=cost(flops=18 * tokens * width * inner, bytes_accessed=12 * tokens * width, transcendentals=0),
        name="weight_grads",
    )(place, normed, *own, *got, dq, table, proj, *deps)


def pick_block(refs, step, scratch_ref):
    cut = refs[0].shape[0]
    for index in range(4):

        @pl.when(step == index)
        def _(index=index):
            scratch_ref[:cut] = refs[2 * index][...]
            scratch_ref[cut:] = refs[2 * index + 1][...]


def pick_whole(refs, step, scratch_ref):
    for index in range(4):

        @pl.when(step == index)
        def _(index=index):
            scratch_ref[...] = refs[index][...]


def once(shape):
    return pl.BlockSpec(shape, lambda g, *_: (0,) * len(shape), pipeline_mode=pl.Buffered(1))


def norm_kernel(*refs, inner):
    pieces, (gain_ref, weight_ref, normed_ref, k0, k1, k2, k3, q_ref, x_scr) = refs[:8], refs[8:]
    step = pl.program_id(0)
    pick_block(pieces, step, x_scr)
    hidden = x_scr[...].astype(FLOAT)
    scale = lax.rsqrt(jnp.mean(hidden * hidden, axis=-1, keepdims=True) + EPSILON)
    normed = (hidden * scale * gain_ref[...]).astype(BFLOAT)
    normed_ref[0] = normed
    both = jnp.dot(normed, weight_ref[:, inner:], preferred_element_type=FLOAT).astype(BFLOAT)

    for index, kv_ref in enumerate((k0, k1, k2, k3)):

        @pl.when(step == index)
        def _(kv_ref=kv_ref):
            kv_ref[0] = both

    @pl.when(step == 0)
    def _():
        q_ref[...] = jnp.dot(normed, weight_ref[:, :inner], preferred_element_type=FLOAT).astype(BFLOAT)


def norm_project(pieces, gain, weight, inner):
    tokens, width = 2 * pieces[0].shape[0], pieces[0].shape[1]
    return pl.pallas_call(
        functools.partial(norm_kernel, inner=inner),
        grid=(4,),
        in_specs=[*[once(piece.shape) for piece in pieces], once(gain.shape), once(weight.shape)],
        out_specs=[
            pl.BlockSpec((1, tokens, width), lambda g: (g, 0, 0)),
            *[pl.BlockSpec((1, tokens, 2 * inner), lambda g: (0, 0, 0))] * 4,
            pl.BlockSpec((tokens, inner), lambda g: (0, 0)),
        ],
        out_shape=[
            jax.ShapeDtypeStruct((4, tokens, width), BFLOAT),
            *[jax.ShapeDtypeStruct((1, tokens, 2 * inner), BFLOAT)] * 4,
            jax.ShapeDtypeStruct((tokens, inner), BFLOAT),
        ],
        scratch_shapes=[pltpu.VMEM((tokens, width), BFLOAT)],
        compiler_params=BIG,
        cost_estimate=cost(
            flops=18 * tokens * width * inner, bytes_accessed=18 * tokens * width, transcendentals=0
        ),
        name="norm_project",
    )(*pieces, gain, weight)


GELU_SCALE = float(np.sqrt(2.0 / np.pi))


def late_kernel(*refs):
    attn, inputs = refs[:4], refs[4:12]
    proj_ref, gain_ref, after_ref, normed_ref, a_scr, x_scr = refs[12:]
    step = pl.program_id(0)
    pick_whole(attn, step, a_scr)
    pick_block(inputs, step, x_scr)
    after_attn = x_scr[...].astype(FLOAT) + jnp.dot(a_scr[...], proj_ref[...], preferred_element_type=FLOAT)

    @pl.when(step == 0)
    def _():
        after_ref[...] = after_attn

    scale = lax.rsqrt(jnp.mean(after_attn * after_attn, axis=-1, keepdims=True) + EPSILON)
    normed_ref[0] = (after_attn * scale * gain_ref[...]).astype(BFLOAT)


def late_norm(attn, inputs, proj, gain):
    tokens, inner = attn[0].shape
    width = proj.shape[1]
    return pl.pallas_call(
        late_kernel,
        grid=(4,),
        in_specs=[once(value.shape) for value in (*attn, *inputs, proj, gain)],
        out_specs=[
            pl.BlockSpec((tokens, width), lambda g: (0, 0)), pl.BlockSpec((1, tokens, width), lambda g: (g, 0, 0)),
        ],
        out_shape=[
            jax.ShapeDtypeStruct((tokens, width), FLOAT), jax.ShapeDtypeStruct((4, tokens, width), BFLOAT),
        ],
        scratch_shapes=[pltpu.VMEM((tokens, inner), BFLOAT), pltpu.VMEM((tokens, width), BFLOAT)],
        compiler_params=BIG,
        cost_estimate=cost(flops=8 * tokens * width * inner, bytes_accessed=24 * tokens * width, transcendentals=0),
        name="late_norm",
    )(*attn, *inputs, proj, gain)


def feed_kernel(
    spot_ref, normed_ref, cots_ref, mine_ref, other_ref, down_mine, down_other,
    act_ref, dmine_ref, dother_ref, out_ref, l0, l1, l2, l3, cot_ref, down_ref,
):
    is_zero = spot_ref[0] == 0
    tokens = normed_ref.shape[1]

    @pl.when(pl.program_id(0) == 0)
    def _():
        depth, piece, _ = down_mine.shape
        for level in range(depth):
            first = jnp.where(is_zero, down_mine[level], down_other[level])
            second = jnp.where(is_zero, down_other[level], down_mine[level])
            down_ref[2 * level * piece : (2 * level + 1) * piece, :] = first
            down_ref[(2 * level + 1) * piece : (2 * level + 2) * piece, :] = second

    cot = cots_ref[...].reshape(tokens, cots_ref.shape[2])
    cot_ref[0] = cot
    normed = normed_ref[0]
    pre_mine = jnp.dot(normed, mine_ref[...], preferred_element_type=FLOAT)
    pre_other = jnp.dot(normed, other_ref[...], preferred_element_type=FLOAT)
    gate = jnp.where(is_zero, pre_mine, pre_other)
    up = jnp.where(is_zero, pre_other, pre_mine)
    square = gate * gate
    lifted = jnp.tanh(GELU_SCALE * (gate + 0.044715 * gate * square))
    half = 0.5 * (1.0 + lifted)
    smooth = gate * half
    act = (smooth * up).astype(BFLOAT)
    act_ref[0] = act
    out = jnp.dot(act, down_ref[...], preferred_element_type=FLOAT).astype(BFLOAT)
    out_ref[...] = out.reshape(out_ref.shape)
    act_back = nt(cot, down_ref[...])
    slope = half + 0.5 * gate * (1.0 - lifted * lifted) * (GELU_SCALE * (1.0 + 3 * 0.044715 * square))
    gate_back = act_back * up * slope
    up_back = act_back * smooth
    dmine = jnp.where(is_zero, gate_back, up_back).astype(BFLOAT)
    dother = jnp.where(is_zero, up_back, gate_back).astype(BFLOAT)
    dmine_ref[0] = dmine
    dother_ref[0] = dother
    late = (nt(dmine, mine_ref[...]) + nt(dother, other_ref[...])).astype(BFLOAT)
    for index, late_ref in enumerate((l0, l1, l2, l3)):

        @pl.when(pl.program_id(0) == index)
        def _(late_ref=late_ref):
            late_ref[...] = late.reshape(late_ref.shape)


def feed_forward(spot, normed, cots, mine, other, downs):
    _, tokens, width = normed.shape
    wide = mine.shape[1]

    def block(size):
        return pl.BlockSpec((1, tokens, size), lambda g, spot: (g, 0, 0))

    def shape(size):
        return jax.ShapeDtypeStruct((4, tokens, size), BFLOAT)

    placed = pl.BlockSpec((2, tokens // 2, width), lambda g, spot: (lax.bitwise_xor(g, spot[1]), 0, 0))
    sent = jax.ShapeDtypeStruct((8, tokens // 2, width), BFLOAT)
    half = jax.ShapeDtypeStruct((2, tokens // 2, width), BFLOAT)
    piece = pl.BlockSpec((2, tokens // 2, width), lambda g, spot: (0, 0, 0))
    return pl.pallas_call(
        feed_kernel,
        grid_spec=pltpu.PrefetchScalarGridSpec(
            num_scalar_prefetch=1,
            grid=(4,),
            in_specs=[block(width), placed, *[once(value.shape) for value in (mine, other, *downs)]],
            out_specs=[block(wide), block(wide), block(wide), placed, *[piece] * 4, block(width)],
            scratch_shapes=[pltpu.VMEM((wide, width), BFLOAT)],
        ),
        out_shape=[shape(wide), shape(wide), shape(wide), sent, *[half] * 4, shape(width)],
        compiler_params=BIG,
        cost_estimate=cost(
            flops=48 * tokens * width * wide, bytes_accessed=30 * tokens * width, transcendentals=4 * tokens * wide
        ),
        name="feed_forward",
    )(spot, normed, cots, mine, other, *downs)


def outer_kernel(left_ref, *refs):
    count = len(refs) // 3
    rights, outs, scratch = refs[:count], refs[count : 2 * count], refs[2 * count :]
    step = pl.program_id(0)

    def rows(ref):
        return ref[...].reshape(-1, ref.shape[2])

    left = jnp.transpose(rows(left_ref))
    for right_ref, out_ref, acc_ref in zip(rights, outs, scratch):
        part = jnp.dot(left, rows(right_ref), preferred_element_type=FLOAT).reshape(out_ref.shape)

        @pl.when(step == 0)
        def _(acc_ref=acc_ref, part=part):
            acc_ref[...] = part

        @pl.when(step == 1)
        def _(acc_ref=acc_ref, out_ref=out_ref, part=part):
            out_ref[...] = (acc_ref[...] + part).astype(BFLOAT)


def outer_sums(left, rights):
    _, tokens, width = left.shape
    shapes = [(2, width // 2, right.shape[2]) for right in rights]
    return pl.pallas_call(
        outer_kernel,
        grid=(2,),
        in_specs=[pl.BlockSpec((2, tokens, value.shape[2]), lambda g: (g, 0, 0)) for value in (left, *rights)],
        out_specs=[pl.BlockSpec(shape, lambda g: (0, 0, 0)) for shape in shapes],
        out_shape=[jax.ShapeDtypeStruct(shape, BFLOAT) for shape in shapes],
        scratch_shapes=[pltpu.VMEM(shape, FLOAT) for shape in shapes],
        compiler_params=BIG,
        cost_estimate=cost(flops=16 * tokens * width * sum(shape[2] for shape in shapes), bytes_accessed=0, transcendentals=0),
        name="outer_sums",
    )(left, *rights)


def norm_back(hidden, gain, back):
    scale = lax.rsqrt(jnp.mean(hidden * hidden, axis=-1, keepdims=True) + EPSILON)
    lifted = back * gain
    return scale * lifted - hidden * (scale * scale * scale) * jnp.mean(lifted * hidden, axis=-1, keepdims=True)


def quarter_specs(tile, width):
    whole = pl.BlockSpec((tile, width), lambda g: (g, 0))
    near = pl.BlockSpec((tile, width), lambda g: (jnp.minimum(g, 1), 0))
    far = pl.BlockSpec((tile, width), lambda g: (jnp.maximum(g - 2, 0), 0))
    return whole, [near, near, far, far]


def summed(own_ref, parts):
    near = pl.program_id(0) < 2
    first = jnp.where(near, parts[0][...], parts[2][...]).astype(FLOAT)
    second = jnp.where(near, parts[1][...], parts[3][...]).astype(FLOAT)
    return own_ref[...].astype(FLOAT) + first + second


def middle_kernel(after_ref, p0, p1, p2, p3, cot_ref, gain_ref, proj_ref, residual_ref, mix_ref, attn_ref):
    back = sum(ref[0].astype(FLOAT) for ref in (p0, p1, p2, p3))
    residual = cot_ref[0].astype(FLOAT) + norm_back(after_ref[...], gain_ref[...], back)
    residual_ref[...] = residual
    mix = residual.astype(BFLOAT)
    mix_ref[...] = mix
    attn_ref[...] = nt(mix, proj_ref[...]).astype(BFLOAT)


def middle(after_attn, parts, cots, gain, proj, *deps):
    tokens, width = after_attn.shape
    inner = proj.shape[0]
    tile = tokens // 4
    whole = pl.BlockSpec((tile, width), lambda g: (g, 0))
    half = pl.BlockSpec((1, tile, width), lambda g: (g // 2, g % 2, 0))
    return pl.pallas_call(
        skipping(middle_kernel, 8, len(deps)),
        grid=(4,),
        in_specs=[whole, half, half, half, half, half, once(gain.shape), once(proj.shape)] + [UNREAD] * len(deps),
        out_specs=[whole, whole, pl.BlockSpec((tile, inner), lambda g: (g, 0))],
        out_shape=[
            jax.ShapeDtypeStruct((tokens, width), FLOAT),
            jax.ShapeDtypeStruct((tokens, width), BFLOAT),
            jax.ShapeDtypeStruct((tokens, inner), BFLOAT),
        ],
        compiler_params=BIG,
        cost_estimate=pl.CostEstimate(flops=10**11, bytes_accessed=0, transcendentals=0),
        name="middle",
    )(after_attn, *parts, cots, gain, proj, *deps)


def plus_kernel(left_ref, *refs):
    rights, out_ref = refs[:-1], refs[-1]
    for index, right_ref in enumerate(rights):

        @pl.when(pl.program_id(0) * len(rights) // pl.num_programs(0) == index)
        def _(right_ref=right_ref):
            out_ref[0] = (left_ref[0].astype(FLOAT) + right_ref[0].astype(FLOAT)).astype(BFLOAT)


def plus(left, rights, *deps):
    shape = left.shape
    each = shape[0] // len(rights)
    spec = pl.BlockSpec((1, *shape[1:]), lambda g: (g,) + (0,) * (len(shape) - 1))

    def part(index):
        return pl.BlockSpec(
            (1, *shape[1:]), lambda g: (jnp.clip(g - index * each, 0, each - 1),) + (0,) * (len(shape) - 1)
        )

    return pl.pallas_call(
        skipping(plus_kernel, 1 + len(rights), len(deps)),
        grid=(shape[0],),
        in_specs=[spec, *[part(index) for index in range(len(rights))]] + [UNREAD] * len(deps),
        out_specs=spec,
        out_shape=jax.ShapeDtypeStruct(shape, BFLOAT),
        compiler_params=BIG,
        cost_estimate=moved(left, left, left),
        name="plus",
    )(left, *rights, *deps)


def last_kernel(dq_ref, own_ref, p1, p2, p3, x0, x1, residual_ref, gain_ref, weight_ref, out_ref):
    dkv = sum(ref[...].astype(FLOAT) for ref in (own_ref, p1, p2, p3)).astype(BFLOAT)
    inner = dq_ref.shape[1]
    back = nt(dq_ref[...], weight_ref[:, :inner]) + nt(dkv, weight_ref[:, inner:])
    hidden = jnp.where(pl.program_id(0) < 2, x0[...], x1[...]).astype(FLOAT)
    out_ref[...] = (residual_ref[...] + norm_back(hidden, gain_ref[...], back)).astype(BFLOAT)


def last(dq, own, parts, inputs, residual, gain, weight):
    tokens, width = residual.shape
    inner = dq.shape[1]
    tile = tokens // 4
    whole = pl.BlockSpec((tile, width), lambda g: (g, 0))
    near = pl.BlockSpec((tile, width), lambda g: (jnp.minimum(g, 1), 0))
    far = pl.BlockSpec((tile, width), lambda g: (jnp.maximum(g - 2, 0), 0))
    piece = pl.BlockSpec((tile, 2 * inner), lambda g: (g, 0))
    return pl.pallas_call(
        last_kernel,
        grid=(4,),
        in_specs=[
            pl.BlockSpec((tile, inner), lambda g: (g, 0)), piece, piece, piece, piece, near, far, whole,
            once(gain.shape), once(weight.shape),
        ],
        out_specs=whole,
        out_shape=jax.ShapeDtypeStruct((tokens, width), BFLOAT),
        compiler_params=BIG,
        cost_estimate=pl.CostEstimate(flops=10**11, bytes_accessed=0, transcendentals=0),
        name="input_gradient",
    )(dq, own, *parts, *inputs, residual, gain, weight)


def choose(refs, slot):
    value = refs[0][...]
    for index in range(1, len(refs)):
        value = jnp.where(slot == index, refs[index][...], value)
    return value


def spread_kernel(place_ref, *refs, depth, part):
    nears, fars, (gate_ref, up_ref, gate_out, up_out, late_ref) = refs[:4], refs[4:8], refs[8:]
    low = place_ref[0]
    chip, core = low // 2, lax.rem(low, 2)
    for index in range(4):
        slot = lax.bitwise_xor(chip, jnp.int32(index))
        near, far = choose(nears, slot), choose(fars, slot)
        gate = jnp.where(core == 0, near, far).astype(FLOAT)
        up = jnp.where(core == 0, far, near).astype(FLOAT)
        for level in range(depth):
            base = (level * 4 + index) * part
            gate_out[:, base : base + part] = gate[:, level * part : (level + 1) * part]
            up_out[:, base : base + part] = up[:, level * part : (level + 1) * part]
    total = gate_out[...] * gate_ref[...].astype(FLOAT) + up_out[...] * up_ref[...].astype(FLOAT)
    late_ref[...] = jnp.broadcast_to(jnp.sum(total, axis=1, keepdims=True), late_ref.shape)


def spread(place, nears, fars, gate, up, depth, part):
    shard, hidden = gate.shape
    tile = 184 if shard % 184 == 0 else shard
    pieces = pl.BlockSpec((tile, nears[0].shape[1]), lambda g: (g, 0))
    rows = pl.BlockSpec((tile, hidden), lambda g: (g, 0))
    return pl.pallas_call(
        functools.partial(spread_kernel, depth=depth, part=part),
        grid=(shard // tile,),
        in_specs=[SMEM_WHOLE, *[pieces] * 8, rows, rows],
        out_specs=[rows, rows, pl.BlockSpec((tile, 128), lambda g: (g, 0))],
        out_shape=[
            jax.ShapeDtypeStruct((shard, hidden), FLOAT),
            jax.ShapeDtypeStruct((shard, hidden), FLOAT),
            jax.ShapeDtypeStruct((shard, 128), FLOAT),
        ],
        compiler_params=BIG,
        cost_estimate=cost(flops=4 * shard * hidden, bytes_accessed=16 * shard * hidden, transcendentals=0),
        name="spread_columns",
    )(place, *nears, *fars, gate, up)


def rows_kernel(place_ref, *refs):
    nears, fars, (out_ref, scratch_ref) = refs[:4], refs[4:8], refs[8:]
    low = place_ref[0]
    size = nears[0].shape[0]

    @pl.when(pl.program_id(0) == 0)
    def _():
        for index in range(GROUP):
            gap = lax.bitwise_xor(low, jnp.int32(index))
            slot, odd = gap // 2, lax.rem(gap, 2)
            rows = jnp.where(odd == 0, choose(nears, slot), choose(fars, slot))
            scratch_ref[index * size : (index + 1) * size, :] = rows

    base = pl.multiple_of(pl.program_id(0) * 128, 128)
    out_ref[...] = jnp.transpose(scratch_ref[pl.ds(base, 128), :].astype(FLOAT))


def gathered_kernel(own_ref, *refs):
    total = own_ref[...].astype(FLOAT)
    for ref in refs[:-1]:
        total = total + ref[...].astype(FLOAT)
    refs[-1][...] = total.astype(BFLOAT)


def sum_parts(parts, *deps):
    return pl.pallas_call(
        skipping(gathered_kernel, len(parts), len(deps)),
        in_specs=[VMEM_WHOLE] * len(parts) + [UNREAD] * len(deps),
        out_specs=VMEM_WHOLE,
        out_shape=jax.ShapeDtypeStruct(parts[0].shape, BFLOAT),
        cost_estimate=moved(*parts),
        name="sum_parts",
    )(*parts, *deps)


def stack_kernel(*refs):
    for index, ref in enumerate(refs[:-1]):
        refs[-1][index] = ref[...]


def finish_kernel(
    place_ref, near_ref, far_ref, q_ref, k_ref, v_ref, q_out, k_out, v_out, proj_out, early_ref, table_ref, *, size, wide
):
    low = place_ref[0]
    shard, inner = q_ref.shape
    part = proj_out.shape[0] // 2
    each = part // 3
    for index in range(GROUP):
        gap = lax.bitwise_xor(low, jnp.int32(index))
        slot, odd = gap // 2, lax.rem(gap, 2)
        block = jnp.where(odd == 0, near_ref[slot], far_ref[slot]).astype(FLOAT)
        base = min(index * size, shard - size)
        skip = index * size - base
        q_out[base + skip : base + size, :] = block[skip:size, :inner]
        for pair in range(inner // 128):
            for offset, out_ref in enumerate((k_out, v_out)):
                column = inner + 256 * pair + 128 * offset
                out_ref[base + skip : base + size, 128 * pair : 128 * pair + 128] = block[skip:size, column : column + 128]
        if index == GROUP - 1:
            table_ref[...] = block[:16, :128]
        column = (index // 2) * wide
        reach = min(wide, proj_out.shape[1] - column)
        for lane in range(3):
            base = (index % 2) * part + lane * each
            proj_out[base : base + each, column : column + reach] = block[size:, lane * wide : lane * wide + reach]
    total = q_out[...] * q_ref[...].astype(FLOAT) + k_out[...] * k_ref[...].astype(FLOAT)
    total = total + v_out[...] * v_ref[...].astype(FLOAT)
    early_ref[...] = jnp.broadcast_to(jnp.sum(total, axis=1, keepdims=True), early_ref.shape)


def rows_of_kernel(x_ref, cot_ref, near_ref, far_ref, rows_ref):
    rows, cut = x_ref.shape[2], near_ref.shape[0]
    for seq in range(x_ref.shape[0]):
        turned = jnp.transpose(x_ref[seq])
        start = seq * rows
        split = min(max(cut - start, 0), rows)
        if split > 0:
            near_ref[start : start + split, :] = turned[:split]
        if split < rows:
            far_ref[start + split - cut : start + rows - cut, :] = turned[split:]
        turned = jnp.transpose(cot_ref[seq])
        for copy in range(4):
            if split > 0:
                rows_ref[2 * copy, start : start + split, :] = turned[:split]
            if split < rows:
                rows_ref[2 * copy + 1, start + split - cut : start + rows - cut, :] = turned[split:]


def on_device(
    layer_input, segments, cotangent, query_weight, key_weight, value_weight, projection, gate_weight, up_weight,
    down_weight, gain_early, gain_late, bias_table,
):
    ring = lax.axis_size("ctx")
    depth = lax.axis_size("wsh")
    groups = ring // GROUP
    mine = lax.axis_index("ctx")
    low = lax.rem(mine, GROUP)
    chip, core = low // 2, lax.rem(low, 2)
    zed = lax.axis_index("wsh")
    seqs, rows, width = layer_input.shape
    inner = query_weight.shape[1]
    heads = bias_table.shape[1]
    shard = width // depth
    slab = gate_weight.shape[1] // depth
    part = slab // 4
    piece = part // 2
    tokens = seqs * rows
    cut = tokens // 2
    buckets = BUCKETS // depth
    size, wide = slice_size(shard), column_cut(width)
    each = inner // depth // 6
    upper = [[group * GROUP + index for group in range(groups)] for index in range(GROUP)]
    is_zero = core == 0
    place = jnp.stack((low, zed)).astype(jnp.int32)
    meta = mine.astype(jnp.int32).reshape(1)
    spot = jnp.stack((core, chip)).astype(jnp.int32)

    half = jax.ShapeDtypeStruct((cut, width), BFLOAT)
    chips = [[group * GROUP + 2 * index + side for index in range(4)] for group in range(groups) for side in range(2)]

    def exchange(blocks):
        return lax.all_to_all(blocks, "ctx", split_axis=0, concat_axis=0, tiled=True, axis_index_groups=chips)

    x_near, x_far, own_cots = pl.pallas_call(
        rows_of_kernel,
        in_specs=[VMEM_WHOLE] * 2,
        out_specs=[VMEM_WHOLE] * 3,
        out_shape=[half, half, jax.ShapeDtypeStruct((8, cut, width), BFLOAT)],
        compiler_params=BIG,
        cost_estimate=moved(layer_input, layer_input, cotangent, cotangent),
        name="token_rows",
    )(jnp.swapaxes(layer_input, 1, 2), jnp.swapaxes(cotangent, 1, 2))
    inputs = gather_halves((x_near, x_far))

    def columns(weight):
        return jnp.concatenate(
            [lax.dynamic_slice_in_dim(weight, index * slab + chip * part, part, 1) for index in range(depth)], axis=1
        )

    pair_slice = jnp.where(is_zero, columns(gate_weight), columns(up_weight))
    down_slice = lax.dynamic_slice_in_dim(down_weight, chip * part + core * piece, piece, 0)

    packed = pl.pallas_call(
        functools.partial(pack_kernel, size=size, wide=wide),
        in_specs=[SMEM_WHOLE] + [VMEM_WHOLE] * 7,
        out_specs=VMEM_WHOLE,
        out_shape=jax.ShapeDtypeStruct((size + each + 16, 3 * inner), BFLOAT),
        cost_estimate=moved(query_weight, query_weight),
        name="pack",
    )(
        after(place, pair_slice, down_slice), query_weight, key_weight, value_weight, projection, gain_early.reshape(1, shard), gain_late.reshape(1, shard),
        jnp.pad(bias_table, ((0, 8 - buckets), (0, 128 - heads))),
    )
    packed = lax.all_gather(packed, "wsh", axis=0)
    pair_mine = lax.all_gather(after(pair_slice, packed), "wsh", axis=0, tiled=True)
    seg_rows = jnp.pad(segments.astype(BFLOAT), ((0, 16 - seqs), (0, 3 * inner - rows)))
    small = jnp.concatenate((packed[:, : size + each].reshape(-1, 3 * inner), seg_rows), axis=0)
    small = after(small, *inputs[2:6])
    near = gather_relay(small, small.shape[0] // 32 * 16)
    far = swap(near, 1)
    down_mine = lax.all_gather(after(down_slice, near), "wsh", axis=0, tiled=True).reshape(depth, piece, width)
    qkv_full, proj_full, gains, table, segs = pl.pallas_call(
        functools.partial(unpack_kernel, depth=depth, size=size, wide=wide),
        in_specs=[SMEM_WHOLE, VMEM_WHOLE, VMEM_WHOLE, VMEM_WHOLE],
        out_specs=[VMEM_WHOLE] * 5,
        out_shape=[
            jax.ShapeDtypeStruct((width, 3 * inner), BFLOAT),
            jax.ShapeDtypeStruct((inner, width), BFLOAT),
            jax.ShapeDtypeStruct((8, width), FLOAT),
            jax.ShapeDtypeStruct((BUCKETS, 128), FLOAT),
            jax.ShapeDtypeStruct((seqs, GROUP, rows), FLOAT),
        ],
        compiler_params=BIG,
        cost_estimate=moved(near, far, near),
        name="unpack",
    )(place, packed[:, size + each :], near, far)

    def whole(value, axis=0):
        if groups == 1:
            return value
        return lax.all_gather(value, "ctx", axis=axis, tiled=True, axis_index_groups=upper)

    segs = whole(segs, 1)

    normed, *kv, queries = norm_project(inputs, gains[0:1], qkv_full, inner)
    cots = exchange(own_cots)
    kv = [value.reshape(1, seqs, rows, 2 * inner) for value in kv]
    queries = queries.reshape(seqs, rows, inner)
    kv = [whole(value) for value in (*kv, *[swap(value, 1) for value in kv])]
    attention, lse = attention_forward(meta, table, segs, queries, kv)
    attn_low = attention.astype(BFLOAT).reshape(tokens, inner)
    attn = gather_direct(attn_low)

    after_attn, normed_late = late_norm(attn, inputs, proj_full, gains[1:2])
    pair_mine = after(pair_mine, attn_low)
    pair_other = swap(pair_mine, 1)
    down_mine = after(down_mine, normed_late)
    down_other = swap(down_mine, 1)
    activation, back_mine, back_other, out_part, *late_part, cot_all = feed_forward(
        spot, normed_late, cots, pair_mine, pair_other, (down_mine, down_other)
    )

    def flat(value):
        return value.reshape(4 * tokens, value.shape[2])

    def over_groups(value):
        return lax.psum(value, "ctx", axis_index_groups=upper) if groups > 1 else value

    late_parts = [late_part[0]] + [swap(late_part[index], 2 * index) for index in range(1, 4)]
    other_grad, mine_grad = outer_sums(normed_late, (back_other, back_mine))
    other_got = [swap(other_grad[index : index + 1], 1) for index in range(2)]
    down_whole = outer_sums(activation, (cot_all,))[0]
    down_grad = down_whole.reshape(depth, 2, piece, width)
    down_keep = jnp.where(is_zero, down_grad[:, 0], down_grad[:, 1])
    down_send = jnp.where(is_zero, down_grad[:, 1], down_grad[:, 0])
    down_got = swap(down_send, 1)
    residual_grad, mix_low, attn_grad = middle(
        after_attn, late_parts, own_cots, gains[1:2], proj_full, down_whole, mine_grad
    )
    attn_grad = attn_grad.reshape(seqs, rows, inner)
    proj_grad = tn(attn_low, jnp.pad(mix_low, ((0, 0), (0, 4 * wide - width)))).astype(BFLOAT)
    dq, *dkv, table_part = attention_backward(meta, table, segs, queries, kv, attn_grad, attention, lse)

    def owned(value):
        if groups > 1:
            value = lax.psum_scatter(value, "ctx", scatter_dimension=0, tiled=True, axis_index_groups=upper)
        return value.reshape(1, tokens, 2 * inner)

    dkv = [owned(value) for value in dkv]
    dkv_got = [swap(value, 1) for value in dkv[4:]]
    dq = dq.reshape(tokens, inner)
    pair_sum = plus(mine_grad, other_got, mix_low).reshape(width, 2 * piece * depth)
    table_sum = jnp.transpose(jnp.sum(table_part, axis=-1).reshape(heads, BUCKETS)).reshape(depth, buckets, heads)
    table_sum = jnp.pad(table_sum, ((0, 0), (0, 16 - buckets), (0, 128 - heads))).reshape(depth * 16, 128).astype(BFLOAT)
    *dkv_four, keep, send = weight_grads(place, normed, dkv[:4], dkv_got, dq, table_sum, proj_grad, depth, size, wide, pair_sum)
    down_sum = plus(down_keep, [down_got], keep).reshape(depth * piece, width)
    pair_own = over_groups(lax.psum_scatter(pair_sum, "wsh", scatter_dimension=0, tiled=True))
    down_own = over_groups(lax.psum_scatter(down_sum, "wsh", scatter_dimension=0, tiled=True))
    out_parts = exchange(after(out_part, attn_grad)).astype(FLOAT).reshape(4, tokens, width)
    result = (after_attn + jnp.sum(out_parts, axis=0)).astype(BFLOAT)

    blocks = plus(keep, [swap(send, 1)], result)
    dkv_parts = [swap(dkv_four[index], 2 * index) for index in range(1, 4)]
    input_grad = last(dq, dkv_four[0], dkv_parts, (x_near, x_far), residual_grad, gains[0:1], qkv_full)
    levels = sum_parts([blocks[0]] + [swap(blocks[index], 2 * index) for index in range(1, 4)], input_grad, pair_own)
    pair_near = gather_direct(after(pair_own, levels))
    down_near = gather_direct(after(down_own, levels))
    total = sum_parts(
        [levels[0]] + [swap_depth(levels[gap], gap) for gap in range(1, depth)], *pair_near[1:]
    )
    grads_near = gather_direct(over_groups(total))
    pair_far, down_far = [[swap(value, 1) for value in values] for values in (pair_near, down_near)]
    gate_out, up_out, late_sum = spread(place, pair_near, pair_far, gate_weight, up_weight, depth, part)
    down_out = pl.pallas_call(
        rows_kernel,
        grid=(slab // 128,),
        in_specs=[SMEM_WHOLE] + [once((piece, width))] * 8,
        out_specs=pl.BlockSpec((width, 128), lambda g: (0, g)),
        out_shape=jax.ShapeDtypeStruct((width, slab), FLOAT),
        scratch_shapes=[pltpu.VMEM((slab, width), BFLOAT)],
        compiler_params=BIG,
        cost_estimate=moved(down_own, down_own, down_own),
        name="join_down",
    )(place, *down_near, *down_far)
    grads_near = pl.pallas_call(
        skipping(stack_kernel, 4, 1),
        in_specs=[VMEM_WHOLE] * 4 + [UNREAD],
        out_specs=VMEM_WHOLE,
        out_shape=jax.ShapeDtypeStruct((4, *total.shape), BFLOAT),
        cost_estimate=moved(total, total),
        name="stack_small",
    )(*grads_near, late_sum)
    grads_far = swap(grads_near, 1)
    column = jax.ShapeDtypeStruct((shard, inner), FLOAT)
    query_out, key_out, value_out, proj_out, early_sum, table_rows = pl.pallas_call(
        functools.partial(finish_kernel, size=size, wide=wide),
        in_specs=[SMEM_WHOLE] + [VMEM_WHOLE] * 5,
        out_specs=[VMEM_WHOLE] * 6,
        out_shape=[
            column, column, column, jax.ShapeDtypeStruct((inner // depth, width), FLOAT),
            jax.ShapeDtypeStruct((shard, 128), FLOAT), jax.ShapeDtypeStruct((16, 128), FLOAT),
        ],
        compiler_params=BIG,
        cost_estimate=moved(grads_near, grads_far, grads_near),
        name="finish_small",
    )(place, grads_near, grads_far, query_weight, key_weight, value_weight)

    return (
        result.reshape(seqs, rows, width),
        input_grad.reshape(seqs, rows, width),
        query_out,
        key_out,
        value_out,
        proj_out,
        gate_out,
        up_out,
        jnp.transpose(down_out),
        early_sum[:, 0] / gain_early.astype(FLOAT),
        late_sum[:, 0] / gain_late.astype(FLOAT),
        table_rows[:buckets, :heads],
    )


def solution(mesh):
    rows = P("wsh", "ctx", None)
    split = P("wsh", None)
    vector = P("wsh")
    return jax.shard_map(
        on_device,
        mesh=mesh,
        in_specs=(rows, P("wsh", "ctx"), rows, split, split, split, split, split, split, split, vector, vector, split),
        out_specs=(rows, rows, split, split, split, split, split, split, split, vector, vector, split),
        check_vma=False,
    )
```

```python
import functools

import jax
import jax.numpy as jnp
import numpy as np
from jax import lax
from jax.experimental import pallas as pl
from jax.experimental.pallas import tpu as pltpu
from jax.sharding import PartitionSpec as P

BUCKETS = 32
GROUP = 8
EPSILON = 1e-06
NEGATIVE = -1e30
PRECISE = lax.Precision.HIGHEST
BUCKET_EDGES = (12, 16, 23, 32, 46, 64, 91)
FLOAT = jnp.float32
BFLOAT = jnp.bfloat16


SCALE = 0.2


def cost(flops, bytes_accessed, transcendentals):
    return pl.CostEstimate(
        flops=int(SCALE * flops), bytes_accessed=int(SCALE * bytes_accessed), transcendentals=int(SCALE * transcendentals)
    )


def bucket_number(offset):
    distance = abs(offset)
    level = distance if distance < 8 else 8 + sum(distance >= edge for edge in BUCKET_EDGES)
    return level + (16 if offset > 0 else 0)


def bucket_of(offsets):
    distance = jnp.abs(offsets)
    coarse = 8 + sum(((distance >= boundary).astype(jnp.int32) for boundary in BUCKET_EDGES))
    level = jnp.where(distance < 8, distance, coarse)
    return level + jnp.where(offsets > 0, 16, 0)


def near_radius(rows):
    return -(-(BUCKET_EDGES[-1] - 1) // rows)


def tile_offsets(block_gap, rows):
    keys = lax.broadcasted_iota(jnp.int32, (rows, rows), 0)
    queries = lax.broadcasted_iota(jnp.int32, (rows, rows), 1)
    return block_gap * rows + keys - queries


def tile_buckets(block_gap, rows):
    low, high = block_gap * rows - (rows - 1), block_gap * rows + (rows - 1)
    return sorted({bucket_number(offset) for offset in range(low, high + 1)})


def nt(left, right):
    return lax.dot_general(left, right, (((1,), (1,)), ((), ())), preferred_element_type=FLOAT)


def tn(left, right):
    return lax.dot_general(left, right, (((0,), (0,)), ((), ())), preferred_element_type=FLOAT)


def block_number(meta, half, position, count):
    low = lax.rem(meta, GROUP)
    part, group = divmod(position, count // 4)
    return group * GROUP + lax.bitwise_xor(low, jnp.int32(2 * part + half))


def tile_index(meta, half, position, count, radius):
    gap = block_number(meta, half, position, count) - meta
    return jnp.clip(gap, -(radius + 1), radius + 1) + radius + 1


def build_bias(bias_ref, table_ref, pair, rows, radius):
    for side, bucket in ((0, 15), (2 * radius + 2, 31)):
        for head in range(2):
            bias_ref[head, side] = jnp.full((rows, rows), table_ref[bucket, 2 * pair + head], FLOAT)
    for gap in range(-radius, radius + 1):
        buckets = bucket_of(tile_offsets(gap, rows))
        present = tile_buckets(gap, rows)
        tiles = [jnp.full((rows, rows), table_ref[present[0], 2 * pair + head], FLOAT) for head in range(2)]
        for bucket in present[1:]:
            hit = buckets == bucket
            tiles = [jnp.where(hit, table_ref[bucket, 2 * pair + head], tiles[head]) for head in range(2)]
        for head in range(2):
            bias_ref[head, gap + radius + 1] = tiles[head]


def build_mask(mask_ref, segs_ref, meta, seq, rows, count):
    own = segs_ref[seq, pl.ds(meta, 1), :]
    for half in range(2):
        for position in range(count):
            row = segs_ref[seq, pl.ds(block_number(meta, half, position, count), 1), :]
            keys = jnp.transpose(jnp.broadcast_to(row, (rows, rows)))
            mask_ref[seq, half * count + position] = jnp.where(keys == own, 0.0, NEGATIVE)


def half_scores(keys, query, meta, head, half, seq, bias_ref, mask_ref, rows, count, radius):
    raw = nt(keys, query)
    parts = []
    for position in range(count):
        extra = bias_ref[head, tile_index(meta, half, position, count, radius)]
        masked = mask_ref[seq, half * count + position]
        parts.append(raw[position * rows : (position + 1) * rows] + (extra + masked))
    return jnp.concatenate(parts, axis=0)


def joined(refs):
    return jnp.concatenate([ref[...].reshape(-1, ref.shape[-1]) for ref in refs], axis=0)


def head_rows(value, head, lane):
    return jnp.where((lane < 64) == (head == 0), value, jnp.zeros_like(value))


def forward_kernel(
    meta_ref, table_ref, segs_ref, q_ref, *refs, rows, count, radius,
):
    key_refs, value_refs, (out_ref, lse_ref, bias_ref, mask_ref) = refs[:8], refs[8:16], refs[16:]
    pair, seq = pl.program_id(0), pl.program_id(1)
    meta = meta_ref[0]

    @pl.when(seq == 0)
    def _():
        build_bias(bias_ref, table_ref, pair, rows, radius)

    @pl.when(pair == 0)
    def _():
        build_mask(mask_ref, segs_ref, meta, seq, rows, count)

    query = q_ref[0]
    lane = lax.broadcasted_iota(jnp.int32, query.shape, 1)
    keys = [joined(key_refs[:4]), joined(key_refs[4:])]
    values = [joined(value_refs[:4]), joined(value_refs[4:])]
    pieces = []
    for head in range(2):
        one = head_rows(query, head, lane)
        scores = [
            half_scores(keys[half], one, meta, head, half, seq, bias_ref, mask_ref, rows, count, radius)
            for half in range(2)
        ]
        top = jnp.maximum(jnp.max(scores[0], axis=0, keepdims=True), jnp.max(scores[1], axis=0, keepdims=True))
        raised = [jnp.exp(part - top) for part in scores]
        total = jnp.sum(raised[0], axis=0, keepdims=True) + jnp.sum(raised[1], axis=0, keepdims=True)
        scale = 1.0 / total
        mixed = sum(tn(values[half], (raised[half] * scale).astype(BFLOAT)) for half in range(2))
        pieces.append(mixed[64 * head : 64 * head + 64])
        lse_ref[0, 0, head : head + 1] = top + jnp.log(total)
    out_ref[0] = jnp.transpose(jnp.concatenate(pieces, axis=0))


def backward_kernel(
    meta_ref, table_ref, segs_ref, q_ref, *refs, rows, count, radius,
):
    key_refs, value_refs, (do_ref, out_ref, lse_ref, dq_ref) = refs[:8], refs[8:16], refs[16:20]
    both_refs, (tab_ref, bias_ref, mask_ref, sum_ref) = refs[20:28], refs[28:]
    pair, seq = pl.program_id(0), pl.program_id(1)
    meta = meta_ref[0]

    @pl.when(seq == 0)
    def _():
        build_bias(bias_ref, table_ref, pair, rows, radius)
        sum_ref[...] = jnp.zeros_like(sum_ref)

    @pl.when(pair == 0)
    def _():
        build_mask(mask_ref, segs_ref, meta, seq, rows, count)

    query, grad = q_ref[0], do_ref[0]
    lane = lax.broadcasted_iota(jnp.int32, query.shape, 1)
    keys = [joined(key_refs[:4]), joined(key_refs[4:])]
    values = [joined(value_refs[:4]), joined(value_refs[4:])]
    picks = (
        lax.broadcasted_iota(jnp.int32, (8, 128), 1) // 64 == lax.broadcasted_iota(jnp.int32, (8, 128), 0)
    ).astype(FLOAT)
    deltas = lax.dot_general(
        picks, grad.astype(FLOAT) * out_ref[0], (((1,), (1,)), ((), ())), precision=PRECISE, preferred_element_type=FLOAT
    )
    query_heads = [head_rows(query, head, lane) for head in range(2)]
    grad_heads = [head_rows(grad, head, lane) for head in range(2)]
    probs, slopes = [[], []], [[], []]
    pieces = []
    for head in range(2):
        logsum = lse_ref[0, 0, head : head + 1]
        delta = deltas[head : head + 1]
        flow = None
        for half in range(2):
            scores = half_scores(
                keys[half], query_heads[head], meta, head, half, seq, bias_ref, mask_ref, rows, count, radius
            )
            prob = jnp.exp(scores - logsum)
            slope = prob * (nt(values[half], grad_heads[head]) - delta)
            for position in range(count):
                index = tile_index(meta, half, position, count, radius)
                sum_ref[head, index] = sum_ref[head, index] + slope[position * rows : (position + 1) * rows]
            slope_low = slope.astype(BFLOAT)
            probs[half].append(prob.astype(BFLOAT))
            slopes[half].append(slope_low)
            term = tn(keys[half], slope_low)
            flow = term if flow is None else flow + term
        pieces.append(flow[64 * head : 64 * head + 64])
    dq_ref[0] = jnp.transpose(jnp.concatenate(pieces, axis=0)).astype(BFLOAT)
    query_stack = jnp.concatenate(query_heads, axis=0)
    grad_stack = jnp.concatenate(grad_heads, axis=0)
    for half in range(2):
        dk = jnp.dot(jnp.concatenate(slopes[half], axis=1), query_stack, preferred_element_type=FLOAT)
        dv = jnp.dot(jnp.concatenate(probs[half], axis=1), grad_stack, preferred_element_type=FLOAT)
        dk = dk.astype(BFLOAT).reshape(count, 1, rows, 128)
        dv = dv.astype(BFLOAT).reshape(count, 1, rows, 128)
        for part, both_ref in enumerate(both_refs[4 * half : 4 * half + 4]):
            side = slice(part * count // 4, (part + 1) * count // 4)
            both_ref[:, :, :, :128] = dk[side]
            both_ref[:, :, :, 128:] = dv[side]

    @pl.when(seq == pl.num_programs(1) - 1)
    def _():
        for head in range(2):
            sums = {}
            for side, bucket in ((0, 15), (2 * radius + 2, 31)):
                sums[bucket] = jnp.sum(sum_ref[head, side], axis=0, keepdims=True)
            for gap in range(-radius, radius + 1):
                buckets = bucket_of(tile_offsets(gap, rows))
                tile = sum_ref[head, gap + radius + 1]
                for bucket in tile_buckets(gap, rows):
                    part = jnp.sum(jnp.where(buckets == bucket, tile, 0.0), axis=0, keepdims=True)
                    sums[bucket] = sums[bucket] + part if bucket in sums else part
            for bucket in range(BUCKETS):
                tab_ref[0, head, bucket : bucket + 1] = sums.get(bucket, jnp.zeros((1, rows), FLOAT))


def attention_specs(seqs, rows, count, blocks, pairs):
    small = [
        pl.BlockSpec(memory_space=pltpu.SMEM),
        pl.BlockSpec(memory_space=pltpu.SMEM),
        pl.BlockSpec((seqs, blocks, rows), lambda p, s: (0, 0, 0)),
    ]
    query = pl.BlockSpec((1, rows, 128), lambda p, s: (s, 0, p))
    key = pl.BlockSpec((count // 4, 1, rows, 128), lambda p, s: (0, s, 0, 2 * p))
    value = pl.BlockSpec((count // 4, 1, rows, 128), lambda p, s: (0, s, 0, 2 * p + 1))
    stat = pl.BlockSpec((1, 1, 8, rows), lambda p, s: (p, s, 0, 0))
    return small, query, key, value, stat


def attention_scratch(seqs, rows, count, radius):
    return [
        pltpu.VMEM((2, 2 * radius + 3, rows, rows), FLOAT),
        pltpu.VMEM((seqs, 2 * count, rows, rows), FLOAT),
    ]


def attention_cost(seqs, rows, keys, width, products):
    return cost(
        flops=2 * products * seqs * rows * keys * width,
        bytes_accessed=4 * seqs * keys * width * products,
        transcendentals=seqs * rows * keys * width // 64,
    )


def attention_forward(meta, table, segs, queries, kv):
    seqs, rows, inner = queries.shape
    count, blocks, pairs = 4 * kv[0].shape[0], segs.shape[1], inner // 128
    radius = near_radius(rows)
    small, query, key, value, stat = attention_specs(seqs, rows, count, blocks, pairs)
    return pl.pallas_call(
        functools.partial(forward_kernel, rows=rows, count=count, radius=radius),
        grid=(pairs, seqs),
        in_specs=[*small, query, *[key] * 8, *[value] * 8],
        out_specs=[query, stat],
        out_shape=[
            jax.ShapeDtypeStruct((seqs, rows, inner), FLOAT),
            jax.ShapeDtypeStruct((pairs, seqs, 8, rows), FLOAT),
        ],
        scratch_shapes=attention_scratch(seqs, rows, count, radius),
        cost_estimate=attention_cost(seqs, rows, blocks * rows, inner, 2),
        name="attention_forward",
    )(meta, table, segs, queries, *kv, *kv)


def attention_backward(meta, table, segs, queries, kv, grad, out, lse, *deps):
    seqs, rows, inner = queries.shape
    count, blocks, pairs = 4 * kv[0].shape[0], segs.shape[1], inner // 128
    radius = near_radius(rows)
    small, query, key, value, stat = attention_specs(seqs, rows, count, blocks, pairs)
    side = jax.ShapeDtypeStruct((count // 4, seqs, rows, 2 * inner), BFLOAT)
    both = pl.BlockSpec((count // 4, 1, rows, 256), lambda p, s: (0, s, 0, p))
    return pl.pallas_call(
        skipping(functools.partial(backward_kernel, rows=rows, count=count, radius=radius), 23, len(deps)),
        grid=(pairs, seqs),
        in_specs=[*small, query, *[key] * 8, *[value] * 8, query, query, stat] + [UNREAD] * len(deps),
        out_specs=[query, *[both] * 8, pl.BlockSpec((1, 2, BUCKETS, rows), lambda p, s: (p, 0, 0, 0))],
        out_shape=[
            jax.ShapeDtypeStruct((seqs, rows, inner), BFLOAT), *[side] * 8,
            jax.ShapeDtypeStruct((pairs, 2, BUCKETS, rows), FLOAT),
        ],
        scratch_shapes=[
            *attention_scratch(seqs, rows, count, radius),
            pltpu.VMEM((2, 2 * radius + 3, rows, rows), FLOAT),
        ],
        cost_estimate=attention_cost(seqs, rows, blocks * rows, inner, 5),
        name="attention_backward",
    )(meta, table, segs, queries, *kv, *kv, grad, out, lse, *deps)


def swap(value, bit):
    count = lax.axis_size("ctx")
    return lax.ppermute(value, "ctx", [(source, source ^ bit) for source in range(count)])


def swap_depth(value, bit):
    count = lax.axis_size("wsh")
    return lax.ppermute(value, "wsh", [(source, source ^ bit) for source in range(count)])


def after(value, *others):
    return lax.optimization_barrier((value, *others))[0]


def gather_halves(own):
    near, far = own
    first_near, second_far = swap(near, 2), swap(far, 4)
    first_far, second_near = swap(far, 2), swap(near, 4)
    return [near, far, first_near, first_far, second_near, second_far, swap(first_near, 4), swap(second_far, 2)]


def gather_direct(own):
    return [own, swap(own, 2), swap(own, 4), swap(own, 6)]


def gather_relay(own, cut):
    first, second = swap(own, 2), swap(own, 4)
    return jnp.stack((own, first, second, jnp.concatenate((swap(first[:cut], 4), swap(second[cut:], 2)), axis=0)))


VMEM_WHOLE = pl.BlockSpec(memory_space=pltpu.VMEM)
UNREAD = pl.BlockSpec(memory_space=pl.ANY)


def skipping(kernel, inputs, count):
    return lambda *refs: kernel(*refs[:inputs], *refs[inputs + count :])


SMEM_WHOLE = pl.BlockSpec(memory_space=pltpu.SMEM)
BIG = pltpu.CompilerParams(vmem_limit_bytes=60 * 1024 * 1024)


def moved(*arrays):
    return cost(
        flops=0, bytes_accessed=sum(int(np.prod(array.shape)) * array.dtype.itemsize for array in arrays), transcendentals=0
    )


def slice_size(total):
    return -(-total // (GROUP * 16)) * 16


def slice_start(index, total, size):
    return jnp.minimum(index * size, total - size)


def column_cut(width):
    return -(-width // 512) * 128


def pack_kernel(place_ref, q_ref, k_ref, v_ref, proj_ref, early_ref, late_ref, table_ref, out_ref, *, size, wide):
    low = place_ref[0]
    chip, core = low // 2, lax.rem(low, 2)
    inner = q_ref.shape[1]
    shard = q_ref.shape[0]
    start = pl.multiple_of(slice_start(low, shard, size), 16)
    out_ref[:size, :inner] = q_ref[pl.ds(start, size), :]
    for index, ref in enumerate((k_ref, v_ref)):
        rows = ref[pl.ds(start, size), :]
        for pair in range(inner // 128):
            base = inner + 256 * pair + 128 * index
            out_ref[:size, base : base + 128] = rows[:, 128 * pair : 128 * pair + 128]
    part = proj_ref.shape[0] // 2
    each = part // 3
    out_ref[size:, :] = jnp.zeros((out_ref.shape[0] - size, out_ref.shape[1]), BFLOAT)
    for column in range(4):
        reach = min(wide, proj_ref.shape[1] - column * wide)

        @pl.when(chip == column)
        def _(column=column, reach=reach):
            for lane in range(3):
                row = pl.multiple_of(core * part + lane * each, 16)
                out_ref[size : size + each, lane * wide : lane * wide + reach] = proj_ref[
                    pl.ds(row, each), column * wide : column * wide + reach
                ]

    base = size + each
    out_ref[base : base + 1, :shard] = early_ref[...]
    out_ref[base + 1 : base + 2, :shard] = late_ref[...]
    out_ref[base + 8 : base + 16, :128] = table_ref[...]


def unpack_kernel(place_ref, misc_ref, near_ref, far_ref, qkv_ref, proj_ref, gains_ref, table_ref, segs_ref, *, depth, size, wide):
    low = place_ref[0]
    shard, part = qkv_ref.shape[0] // depth, proj_ref.shape[0] // depth // 2
    each = part // 3
    span = size + each
    buckets = table_ref.shape[0] // depth
    for level in range(depth):
        rows = misc_ref[level].astype(FLOAT)
        gains_ref[:, level * shard : (level + 1) * shard] = rows[:8, :shard]
        table_ref[level * buckets : (level + 1) * buckets, :] = rows[8 : 8 + buckets, :128]
    seqs, _, rows = segs_ref.shape
    for index in range(GROUP):
        gap = lax.bitwise_xor(low, jnp.int32(index))
        slot, odd = gap // 2, lax.rem(gap, 2)
        block = jnp.where(odd == 0, near_ref[slot], far_ref[slot])
        for level in range(depth):
            base = level * shard + min(index * size, shard - size)
            qkv_ref[base : base + size, :] = block[level * span : level * span + size]
            column = (index // 2) * wide
            reach = min(wide, proj_ref.shape[1] - column)
            for lane in range(3):
                base = (level * 2 + index % 2) * part + lane * each
                proj_ref[base : base + each, column : column + reach] = block[
                    level * span + size : level * span + span, lane * wide : lane * wide + reach
                ]
        own = block[depth * span : depth * span + 16, :128].astype(FLOAT)
        for seq in range(seqs):
            segs_ref[seq, index : index + 1, :] = own[seq : seq + 1, :rows]


def grad_kernel(
    place_ref, normed_ref, *refs, depth, size, wide
):
    owns, gots, (dq_ref, table_ref, proj_ref) = refs[:4], refs[4:8], refs[8:11]
    sums, (keep_ref, send_ref, kv_scr, q_scr, t_scr) = refs[11:15], refs[15:]
    step = pl.program_id(0)
    tokens = dq_ref.shape[0]
    for index in range(4):

        @pl.when(step == index // 2)
        def _(index=index):
            total = (owns[index][0].astype(FLOAT) + gots[index][0].astype(FLOAT)).astype(BFLOAT)
            t_scr[index % 2 * tokens : (index % 2 + 1) * tokens, :] = total
            sums[index][...] = total

    turned = jnp.transpose(normed_ref[...].reshape(2 * tokens, normed_ref.shape[2]))
    product = jnp.dot(turned, t_scr[...], preferred_element_type=FLOAT)

    @pl.when(step == 0)
    def _():
        kv_scr[...] = product
        q_scr[...] = jnp.dot(turned[:, :tokens], dq_ref[...], preferred_element_type=FLOAT).astype(BFLOAT)

    @pl.when(step == 1)
    def _():
        kv_scr[...] = kv_scr[...] + product
        low = place_ref[0]
        zed = place_ref[1]
        inner = q_scr.shape[1]
        shard = q_scr.shape[0] // depth
        for index in range(GROUP):
            target = lax.bitwise_xor(low, jnp.int32(index))
            out_ref = keep_ref if index % 2 == 0 else send_ref
            for gap in range(depth):
                level = lax.bitwise_xor(zed, jnp.int32(gap))
                start = pl.multiple_of(level * shard + slice_start(target, shard, size), 16)
                out_ref[index // 2, gap, :size, :inner] = q_scr[pl.ds(start, size), :]
                out_ref[index // 2, gap, :size, inner:] = kv_scr[pl.ds(start, size), :].astype(BFLOAT)
                part = proj_ref.shape[0] // depth // 2
                each = part // 3
                column = pl.multiple_of((target // 2) * wide, 128)
                for lane in range(3):
                    row = pl.multiple_of((level * 2 + lax.rem(target, 2)) * part + lane * each, 16)
                    out_ref[index // 2, gap, size:, lane * wide : (lane + 1) * wide] = proj_ref[
                        pl.ds(row, each), pl.ds(column, wide)
                    ]
                last = target == GROUP - 1
                rows = table_ref[pl.ds(pl.multiple_of(level * 16, 16), 16), :]
                out_ref[index // 2, gap, :16, :128] = jnp.where(last, rows, out_ref[index // 2, gap, :16, :128])


def weight_grads(place, normed, own, got, dq, table, proj, depth, size, wide, *deps):
    _, tokens, width = normed.shape
    inner = dq.shape[1]
    block = once((1, tokens, 2 * inner))
    summed = pl.BlockSpec((tokens, 2 * inner), lambda g: (0, 0))
    span = size + proj.shape[0] // depth // 6
    piece = jax.ShapeDtypeStruct((4, depth, span, 3 * inner), BFLOAT)
    kept = pl.BlockSpec((4, depth, span, 3 * inner), lambda g: (0, 0, 0, 0))
    return pl.pallas_call(
        skipping(functools.partial(grad_kernel, depth=depth, size=size, wide=wide), 13, len(deps)),
        grid=(2,),
        in_specs=[
            SMEM_WHOLE, pl.BlockSpec((2, tokens, width), lambda g: (g, 0, 0)), *[block] * 8, once(dq.shape), once(table.shape),
            once(proj.shape),
        ]
        + [UNREAD] * len(deps),
        out_specs=[*[summed] * 4, kept, kept],
        out_shape=[*[jax.ShapeDtypeStruct((tokens, 2 * inner), BFLOAT)] * 4, piece, piece],
        scratch_shapes=[
            pltpu.VMEM((width, 2 * inner), FLOAT), pltpu.VMEM((width, inner), BFLOAT), pltpu.VMEM((2 * tokens, 2 * inner), BFLOAT),
        ],
        compiler_params=BIG,
        cost_estimate=cost(flops=18 * tokens * width * inner, bytes_accessed=12 * tokens * width, transcendentals=0),
        name="weight_grads",
    )(place, normed, *own, *got, dq, table, proj, *deps)


def pick_block(refs, step, scratch_ref):
    cut = refs[0].shape[0]
    for index in range(4):

        @pl.when(step == index)
        def _(index=index):
            scratch_ref[:cut] = refs[2 * index][...]
            scratch_ref[cut:] = refs[2 * index + 1][...]


def pick_whole(refs, step, scratch_ref):
    for index in range(4):

        @pl.when(step == index)
        def _(index=index):
            scratch_ref[...] = refs[index][...]


def once(shape):
    return pl.BlockSpec(shape, lambda g, *_: (0,) * len(shape), pipeline_mode=pl.Buffered(1))


def norm_kernel(*refs, inner):
    pieces, (gain_ref, weight_ref, normed_ref, k0, k1, k2, k3, q_ref, x_scr) = refs[:8], refs[8:]
    step = pl.program_id(0)
    pick_block(pieces, step, x_scr)
    hidden = x_scr[...].astype(FLOAT)
    scale = lax.rsqrt(jnp.mean(hidden * hidden, axis=-1, keepdims=True) + EPSILON)
    normed = (hidden * scale * gain_ref[...]).astype(BFLOAT)
    normed_ref[0] = normed
    both = jnp.dot(normed, weight_ref[:, inner:], preferred_element_type=FLOAT).astype(BFLOAT)

    for index, kv_ref in enumerate((k0, k1, k2, k3)):

        @pl.when(step == index)
        def _(kv_ref=kv_ref):
            kv_ref[0] = both

    @pl.when(step == 0)
    def _():
        q_ref[...] = jnp.dot(normed, weight_ref[:, :inner], preferred_element_type=FLOAT).astype(BFLOAT)


def norm_project(pieces, gain, weight, inner):
    tokens, width = 2 * pieces[0].shape[0], pieces[0].shape[1]
    return pl.pallas_call(
        functools.partial(norm_kernel, inner=inner),
        grid=(4,),
        in_specs=[*[once(piece.shape) for piece in pieces], once(gain.shape), once(weight.shape)],
        out_specs=[
            pl.BlockSpec((1, tokens, width), lambda g: (g, 0, 0)),
            *[pl.BlockSpec((1, tokens, 2 * inner), lambda g: (0, 0, 0))] * 4,
            pl.BlockSpec((tokens, inner), lambda g: (0, 0)),
        ],
        out_shape=[
            jax.ShapeDtypeStruct((4, tokens, width), BFLOAT),
            *[jax.ShapeDtypeStruct((1, tokens, 2 * inner), BFLOAT)] * 4,
            jax.ShapeDtypeStruct((tokens, inner), BFLOAT),
        ],
        scratch_shapes=[pltpu.VMEM((tokens, width), BFLOAT)],
        compiler_params=BIG,
        cost_estimate=cost(
            flops=18 * tokens * width * inner, bytes_accessed=18 * tokens * width, transcendentals=0
        ),
        name="norm_project",
    )(*pieces, gain, weight)


GELU_SCALE = float(np.sqrt(2.0 / np.pi))


def late_kernel(*refs):
    attn, inputs = refs[:4], refs[4:12]
    proj_ref, gain_ref, after_ref, normed_ref, a_scr, x_scr = refs[12:]
    step = pl.program_id(0)
    pick_whole(attn, step, a_scr)
    pick_block(inputs, step, x_scr)
    after_attn = x_scr[...].astype(FLOAT) + jnp.dot(a_scr[...], proj_ref[...], preferred_element_type=FLOAT)

    @pl.when(step == 0)
    def _():
        after_ref[...] = after_attn

    scale = lax.rsqrt(jnp.mean(after_attn * after_attn, axis=-1, keepdims=True) + EPSILON)
    normed_ref[0] = (after_attn * scale * gain_ref[...]).astype(BFLOAT)


def late_norm(attn, inputs, proj, gain):
    tokens, inner = attn[0].shape
    width = proj.shape[1]
    return pl.pallas_call(
        late_kernel,
        grid=(4,),
        in_specs=[once(value.shape) for value in (*attn, *inputs, proj, gain)],
        out_specs=[
            pl.BlockSpec((tokens, width), lambda g: (0, 0)), pl.BlockSpec((1, tokens, width), lambda g: (g, 0, 0)),
        ],
        out_shape=[
            jax.ShapeDtypeStruct((tokens, width), FLOAT), jax.ShapeDtypeStruct((4, tokens, width), BFLOAT),
        ],
        scratch_shapes=[pltpu.VMEM((tokens, inner), BFLOAT), pltpu.VMEM((tokens, width), BFLOAT)],
        compiler_params=BIG,
        cost_estimate=cost(flops=8 * tokens * width * inner, bytes_accessed=24 * tokens * width, transcendentals=0),
        name="late_norm",
    )(*attn, *inputs, proj, gain)


def feed_kernel(
    spot_ref, normed_ref, cots_ref, mine_ref, other_ref, down_mine, down_other,
    act_ref, dmine_ref, dother_ref, out_ref, l0, *refs
):
    late_refs, (cot_ref, down_ref) = refs[:6], refs[6:]
    is_zero = spot_ref[0] == 0
    tokens = normed_ref.shape[1]

    @pl.when(pl.program_id(0) == 0)
    def _():
        depth, piece, _ = down_mine.shape
        for level in range(depth):
            first = jnp.where(is_zero, down_mine[level], down_other[level])
            second = jnp.where(is_zero, down_other[level], down_mine[level])
            down_ref[2 * level * piece : (2 * level + 1) * piece, :] = first
            down_ref[(2 * level + 1) * piece : (2 * level + 2) * piece, :] = second

    cot = cots_ref[...].reshape(tokens, cots_ref.shape[2])
    cot_ref[0] = cot
    normed = normed_ref[0]
    pre_mine = jnp.dot(normed, mine_ref[...], preferred_element_type=FLOAT)
    pre_other = jnp.dot(normed, other_ref[...], preferred_element_type=FLOAT)
    gate = jnp.where(is_zero, pre_mine, pre_other)
    up = jnp.where(is_zero, pre_other, pre_mine)
    square = gate * gate
    lifted = jnp.tanh(GELU_SCALE * (gate + 0.044715 * gate * square))
    gate_half = 0.5 * (1.0 + lifted)
    smooth = gate * gate_half
    act = (smooth * up).astype(BFLOAT)
    act_ref[0] = act
    out = jnp.dot(act, down_ref[...], preferred_element_type=FLOAT).astype(BFLOAT)
    out_ref[...] = out.reshape(out_ref.shape)
    act_back = nt(cot, down_ref[...])
    slope = gate_half + 0.5 * gate * (1.0 - lifted * lifted) * (GELU_SCALE * (1.0 + 3 * 0.044715 * square))
    gate_back = act_back * up * slope
    up_back = act_back * smooth
    dmine = jnp.where(is_zero, gate_back, up_back).astype(BFLOAT)
    dother = jnp.where(is_zero, up_back, gate_back).astype(BFLOAT)
    dmine_ref[0] = dmine
    dother_ref[0] = dother
    late = (nt(dmine, mine_ref[...]) + nt(dother, other_ref[...])).astype(BFLOAT)
    half = late.shape[0] // 2

    @pl.when(pl.program_id(0) == 0)
    def _():
        l0[...] = late.reshape(l0.shape)

    for index in range(3):

        @pl.when(pl.program_id(0) == index + 1)
        def _(index=index):
            late_refs[2 * index][...] = late[:half]
            late_refs[2 * index + 1][...] = late[half:]


def feed_forward(spot, normed, cots, mine, other, downs):
    _, tokens, width = normed.shape
    wide = mine.shape[1]

    def block(size):
        return pl.BlockSpec((1, tokens, size), lambda g, spot: (g, 0, 0))

    def shape(size):
        return jax.ShapeDtypeStruct((4, tokens, size), BFLOAT)

    placed = pl.BlockSpec((2, tokens // 2, width), lambda g, spot: (lax.bitwise_xor(g, spot[1]), 0, 0))
    sent = jax.ShapeDtypeStruct((8, tokens // 2, width), BFLOAT)
    half = jax.ShapeDtypeStruct((2, tokens // 2, width), BFLOAT)
    piece = pl.BlockSpec((2, tokens // 2, width), lambda g, spot: (0, 0, 0))
    rows = jax.ShapeDtypeStruct((tokens // 2, width), BFLOAT)
    part = pl.BlockSpec((tokens // 2, width), lambda g, spot: (0, 0))
    return pl.pallas_call(
        feed_kernel,
        grid_spec=pltpu.PrefetchScalarGridSpec(
            num_scalar_prefetch=1,
            grid=(4,),
            in_specs=[block(width), placed, *[once(value.shape) for value in (mine, other, *downs)]],
            out_specs=[block(wide), block(wide), block(wide), placed, piece, *[part] * 6, block(width)],
            scratch_shapes=[pltpu.VMEM((wide, width), BFLOAT)],
        ),
        out_shape=[shape(wide), shape(wide), shape(wide), sent, half, *[rows] * 6, shape(width)],
        compiler_params=BIG,
        cost_estimate=cost(
            flops=48 * tokens * width * wide, bytes_accessed=30 * tokens * width, transcendentals=4 * tokens * wide
        ),
        name="feed_forward",
    )(spot, normed, cots, mine, other, *downs)


def outer_kernel(left_ref, *refs):
    count = len(refs) // 3
    rights, outs, scratch = refs[:count], refs[count : 2 * count], refs[2 * count :]
    step = pl.program_id(0)

    def rows(ref):
        return ref[...].reshape(-1, ref.shape[2])

    left = jnp.transpose(rows(left_ref))
    for right_ref, out_ref, acc_ref in zip(rights, outs, scratch):
        part = jnp.dot(left, rows(right_ref), preferred_element_type=FLOAT).reshape(out_ref.shape)

        @pl.when(step == 0)
        def _(acc_ref=acc_ref, part=part):
            acc_ref[...] = part

        @pl.when(step == 1)
        def _(acc_ref=acc_ref, out_ref=out_ref, part=part):
            out_ref[...] = (acc_ref[...] + part).astype(BFLOAT)


def outer_sums(left, rights):
    _, tokens, width = left.shape
    shapes = [(2, width // 2, right.shape[2]) for right in rights]
    return pl.pallas_call(
        outer_kernel,
        grid=(2,),
        in_specs=[pl.BlockSpec((2, tokens, value.shape[2]), lambda g: (g, 0, 0)) for value in (left, *rights)],
        out_specs=[pl.BlockSpec(shape, lambda g: (0, 0, 0)) for shape in shapes],
        out_shape=[jax.ShapeDtypeStruct(shape, BFLOAT) for shape in shapes],
        scratch_shapes=[pltpu.VMEM(shape, FLOAT) for shape in shapes],
        compiler_params=BIG,
        cost_estimate=cost(flops=16 * tokens * width * sum(shape[2] for shape in shapes), bytes_accessed=0, transcendentals=0),
        name="outer_sums",
    )(left, *rights)


def norm_back(hidden, gain, back):
    scale = lax.rsqrt(jnp.mean(hidden * hidden, axis=-1, keepdims=True) + EPSILON)
    lifted = back * gain
    return scale * lifted - hidden * (scale * scale * scale) * jnp.mean(lifted * hidden, axis=-1, keepdims=True)


def quarter_specs(tile, width):
    whole = pl.BlockSpec((tile, width), lambda g: (g, 0))
    near = pl.BlockSpec((tile, width), lambda g: (jnp.minimum(g, 1), 0))
    far = pl.BlockSpec((tile, width), lambda g: (jnp.maximum(g - 2, 0), 0))
    return whole, [near, near, far, far]


def summed(own_ref, parts):
    near = pl.program_id(0) < 2
    first = jnp.where(near, parts[0][...], parts[2][...]).astype(FLOAT)
    second = jnp.where(near, parts[1][...], parts[3][...]).astype(FLOAT)
    return own_ref[...].astype(FLOAT) + first + second


def middle_kernel(after_ref, own_ref, n0, n1, f0, f1, cot_ref, gain_ref, proj_ref, residual_ref, mix_ref, attn_ref):
    near = pl.program_id(0) < 2
    back = own_ref[0].astype(FLOAT) + jnp.where(near, n0[...], f0[...]).astype(FLOAT)
    back = back + jnp.where(near, n1[...], f1[...]).astype(FLOAT)
    residual = cot_ref[0].astype(FLOAT) + norm_back(after_ref[...], gain_ref[...], back)
    residual_ref[...] = residual
    mix = residual.astype(BFLOAT)
    mix_ref[...] = mix
    attn_ref[...] = nt(mix, proj_ref[...]).astype(BFLOAT)


def middle(after_attn, own, parts, cots, gain, proj, *deps):
    tokens, width = after_attn.shape
    inner = proj.shape[0]
    tile = tokens // 4
    whole = pl.BlockSpec((tile, width), lambda g: (g, 0))
    half = pl.BlockSpec((1, tile, width), lambda g: (g // 2, g % 2, 0))
    near = pl.BlockSpec((tile, width), lambda g: (jnp.minimum(g, 1), 0))
    far = pl.BlockSpec((tile, width), lambda g: (jnp.maximum(g - 2, 0), 0))
    return pl.pallas_call(
        skipping(middle_kernel, 9, len(deps)),
        grid=(4,),
        in_specs=[whole, half, near, near, far, far, half, once(gain.shape), once(proj.shape)] + [UNREAD] * len(deps),
        out_specs=[whole, whole, pl.BlockSpec((tile, inner), lambda g: (g, 0))],
        out_shape=[
            jax.ShapeDtypeStruct((tokens, width), FLOAT),
            jax.ShapeDtypeStruct((tokens, width), BFLOAT),
            jax.ShapeDtypeStruct((tokens, inner), BFLOAT),
        ],
        compiler_params=BIG,
        cost_estimate=pl.CostEstimate(flops=10**11, bytes_accessed=0, transcendentals=0),
        name="middle",
    )(after_attn, own, *parts, cots, gain, proj, *deps)


def apart_kernel(left_ref, right_ref, *outs):
    for index, out_ref in enumerate(outs):

        @pl.when(pl.program_id(0) == index)
        def _(out_ref=out_ref):
            out_ref[...] = (left_ref[0].astype(FLOAT) + right_ref[0].astype(FLOAT)).astype(BFLOAT)


def plus_apart(left, right, *deps):
    count, *shape = left.shape
    spec = pl.BlockSpec((1, *shape), lambda g: (g,) + (0,) * len(shape))
    return pl.pallas_call(
        skipping(apart_kernel, 2, len(deps)),
        grid=(count,),
        in_specs=[spec, spec] + [UNREAD] * len(deps),
        out_specs=[pl.BlockSpec(tuple(shape), lambda g: (0,) * len(shape))] * count,
        out_shape=[jax.ShapeDtypeStruct(tuple(shape), BFLOAT)] * count,
        compiler_params=BIG,
        cost_estimate=moved(left, left, left),
        name="plus_apart",
    )(left, right, *deps)


def relay_kernel(a_ref, b_ref, c_ref, d_ref, first_ref, second_ref):
    first_ref[...] = (a_ref[...].astype(FLOAT) + b_ref[...].astype(FLOAT)).astype(BFLOAT)
    second_ref[...] = (c_ref[...].astype(FLOAT) + d_ref[...].astype(FLOAT)).astype(BFLOAT)


def relay_sums(first, second, *deps):
    shape = jax.ShapeDtypeStruct(first[0].shape, BFLOAT)
    return pl.pallas_call(
        skipping(relay_kernel, 4, len(deps)),
        in_specs=[VMEM_WHOLE] * 4 + [UNREAD] * len(deps),
        out_specs=[VMEM_WHOLE] * 2,
        out_shape=[shape, shape],
        cost_estimate=moved(*first, *second),
        name="relay_sums",
    )(*first, *second, *deps)


def plus_kernel(left_ref, *refs):
    rights, out_ref = refs[:-1], refs[-1]
    for index, right_ref in enumerate(rights):

        @pl.when(pl.program_id(0) * len(rights) // pl.num_programs(0) == index)
        def _(right_ref=right_ref):
            out_ref[0] = (left_ref[0].astype(FLOAT) + right_ref[0].astype(FLOAT)).astype(BFLOAT)


def plus(left, rights, *deps):
    shape = left.shape
    each = shape[0] // len(rights)
    spec = pl.BlockSpec((1, *shape[1:]), lambda g: (g,) + (0,) * (len(shape) - 1))

    def part(index):
        return pl.BlockSpec(
            (1, *shape[1:]), lambda g: (jnp.clip(g - index * each, 0, each - 1),) + (0,) * (len(shape) - 1)
        )

    return pl.pallas_call(
        skipping(plus_kernel, 1 + len(rights), len(deps)),
        grid=(shape[0],),
        in_specs=[spec, *[part(index) for index in range(len(rights))]] + [UNREAD] * len(deps),
        out_specs=spec,
        out_shape=jax.ShapeDtypeStruct(shape, BFLOAT),
        compiler_params=BIG,
        cost_estimate=moved(left, left, left),
        name="plus",
    )(left, *rights, *deps)


def last_kernel(dq_ref, own_ref, p1, p2, p3, x0, x1, residual_ref, gain_ref, weight_ref, out_ref):
    dkv = sum(ref[...].astype(FLOAT) for ref in (own_ref, p1, p2, p3)).astype(BFLOAT)
    inner = dq_ref.shape[1]
    back = nt(dq_ref[...], weight_ref[:, :inner]) + nt(dkv, weight_ref[:, inner:])
    hidden = jnp.where(pl.program_id(0) < 2, x0[...], x1[...]).astype(FLOAT)
    out_ref[...] = (residual_ref[...] + norm_back(hidden, gain_ref[...], back)).astype(BFLOAT)


def last(dq, own, parts, inputs, residual, gain, weight, *deps):
    tokens, width = residual.shape
    inner = dq.shape[1]
    tile = tokens // 4
    whole = pl.BlockSpec((tile, width), lambda g: (g, 0))
    near = pl.BlockSpec((tile, width), lambda g: (jnp.minimum(g, 1), 0))
    far = pl.BlockSpec((tile, width), lambda g: (jnp.maximum(g - 2, 0), 0))
    piece = pl.BlockSpec((tile, 2 * inner), lambda g: (g, 0))
    return pl.pallas_call(
        skipping(last_kernel, 10, len(deps)),
        grid=(4,),
        in_specs=[
            pl.BlockSpec((tile, inner), lambda g: (g, 0)), piece, piece, piece, piece, near, far, whole,
            once(gain.shape), once(weight.shape),
        ]
        + [UNREAD] * len(deps),
        out_specs=whole,
        out_shape=jax.ShapeDtypeStruct((tokens, width), BFLOAT),
        compiler_params=BIG,
        cost_estimate=pl.CostEstimate(flops=10**11, bytes_accessed=0, transcendentals=0),
        name="input_gradient",
    )(dq, own, *parts, *inputs, residual, gain, weight, *deps)


def choose(refs, slot):
    value = refs[0][...]
    for index in range(1, len(refs)):
        value = jnp.where(slot == index, refs[index][...], value)
    return value


def spread_kernel(place_ref, *refs, depth, part):
    nears, fars, (gate_ref, up_ref, gate_out, up_out, late_ref) = refs[:4], refs[4:8], refs[8:]
    low = place_ref[0]
    chip, core = low // 2, lax.rem(low, 2)
    for index in range(4):
        slot = lax.bitwise_xor(chip, jnp.int32(index))
        near, far = choose(nears, slot), choose(fars, slot)
        gate = jnp.where(core == 0, near, far).astype(FLOAT)
        up = jnp.where(core == 0, far, near).astype(FLOAT)
        for level in range(depth):
            base = (level * 4 + index) * part
            gate_out[:, base : base + part] = gate[:, level * part : (level + 1) * part]
            up_out[:, base : base + part] = up[:, level * part : (level + 1) * part]
    total = gate_out[...] * gate_ref[...].astype(FLOAT) + up_out[...] * up_ref[...].astype(FLOAT)
    late_ref[...] = jnp.broadcast_to(jnp.sum(total, axis=1, keepdims=True), late_ref.shape)


def spread(place, nears, fars, gate, up, depth, part):
    shard, hidden = gate.shape
    tile = 184 if shard % 184 == 0 else shard
    pieces = pl.BlockSpec((tile, nears[0].shape[1]), lambda g: (g, 0))
    rows = pl.BlockSpec((tile, hidden), lambda g: (g, 0))
    return pl.pallas_call(
        functools.partial(spread_kernel, depth=depth, part=part),
        grid=(shard // tile,),
        in_specs=[SMEM_WHOLE, *[pieces] * 8, rows, rows],
        out_specs=[rows, rows, pl.BlockSpec((tile, 128), lambda g: (g, 0))],
        out_shape=[
            jax.ShapeDtypeStruct((shard, hidden), FLOAT),
            jax.ShapeDtypeStruct((shard, hidden), FLOAT),
            jax.ShapeDtypeStruct((shard, 128), FLOAT),
        ],
        compiler_params=BIG,
        cost_estimate=cost(flops=4 * shard * hidden, bytes_accessed=16 * shard * hidden, transcendentals=0),
        name="spread_columns",
    )(place, *nears, *fars, gate, up)


def rows_kernel(place_ref, *refs):
    nears, fars, (out_ref, scratch_ref) = refs[:4], refs[4:8], refs[8:]
    low = place_ref[0]
    size = nears[0].shape[0]

    @pl.when(pl.program_id(0) == 0)
    def _():
        for index in range(GROUP):
            gap = lax.bitwise_xor(low, jnp.int32(index))
            slot, odd = gap // 2, lax.rem(gap, 2)
            rows = jnp.where(odd == 0, choose(nears, slot), choose(fars, slot))
            scratch_ref[index * size : (index + 1) * size, :] = rows

    base = pl.multiple_of(pl.program_id(0) * 128, 128)
    out_ref[...] = jnp.transpose(scratch_ref[pl.ds(base, 128), :].astype(FLOAT))


def gathered_kernel(own_ref, *refs):
    total = own_ref[...].astype(FLOAT)
    for ref in refs[:-1]:
        total = total + ref[...].astype(FLOAT)
    refs[-1][...] = total.astype(BFLOAT)


def sum_parts(parts, *deps):
    return pl.pallas_call(
        skipping(gathered_kernel, len(parts), len(deps)),
        in_specs=[VMEM_WHOLE] * len(parts) + [UNREAD] * len(deps),
        out_specs=VMEM_WHOLE,
        out_shape=jax.ShapeDtypeStruct(parts[0].shape, BFLOAT),
        cost_estimate=moved(*parts),
        name="sum_parts",
    )(*parts, *deps)


def stack_kernel(*refs):
    for index, ref in enumerate(refs[:-1]):
        refs[-1][index] = ref[...]


def finish_kernel(
    place_ref, near_ref, far_ref, q_ref, k_ref, v_ref, q_out, k_out, v_out, proj_out, early_ref, table_ref, *, size, wide
):
    low = place_ref[0]
    shard, inner = q_ref.shape
    part = proj_out.shape[0] // 2
    each = part // 3
    for index in range(GROUP):
        gap = lax.bitwise_xor(low, jnp.int32(index))
        slot, odd = gap // 2, lax.rem(gap, 2)
        block = jnp.where(odd == 0, near_ref[slot], far_ref[slot]).astype(FLOAT)
        base = min(index * size, shard - size)
        skip = index * size - base
        q_out[base + skip : base + size, :] = block[skip:size, :inner]
        for pair in range(inner // 128):
            for offset, out_ref in enumerate((k_out, v_out)):
                column = inner + 256 * pair + 128 * offset
                out_ref[base + skip : base + size, 128 * pair : 128 * pair + 128] = block[skip:size, column : column + 128]
        if index == GROUP - 1:
            table_ref[...] = block[:16, :128]
        column = (index // 2) * wide
        reach = min(wide, proj_out.shape[1] - column)
        for lane in range(3):
            base = (index % 2) * part + lane * each
            proj_out[base : base + each, column : column + reach] = block[size:, lane * wide : lane * wide + reach]
    total = q_out[...] * q_ref[...].astype(FLOAT) + k_out[...] * k_ref[...].astype(FLOAT)
    total = total + v_out[...] * v_ref[...].astype(FLOAT)
    early_ref[...] = jnp.broadcast_to(jnp.sum(total, axis=1, keepdims=True), early_ref.shape)


def rows_of_kernel(x_ref, cot_ref, near_ref, far_ref, rows_ref):
    rows, cut = x_ref.shape[2], near_ref.shape[0]
    for seq in range(x_ref.shape[0]):
        turned = jnp.transpose(x_ref[seq])
        start = seq * rows
        split = min(max(cut - start, 0), rows)
        if split > 0:
            near_ref[start : start + split, :] = turned[:split]
        if split < rows:
            far_ref[start + split - cut : start + rows - cut, :] = turned[split:]
        turned = jnp.transpose(cot_ref[seq])
        for copy in range(4):
            if split > 0:
                rows_ref[2 * copy, start : start + split, :] = turned[:split]
            if split < rows:
                rows_ref[2 * copy + 1, start + split - cut : start + rows - cut, :] = turned[split:]


def on_device(
    layer_input, segments, cotangent, query_weight, key_weight, value_weight, projection, gate_weight, up_weight,
    down_weight, gain_early, gain_late, bias_table,
):
    ring = lax.axis_size("ctx")
    depth = lax.axis_size("wsh")
    groups = ring // GROUP
    mine = lax.axis_index("ctx")
    low = lax.rem(mine, GROUP)
    chip, core = low // 2, lax.rem(low, 2)
    zed = lax.axis_index("wsh")
    seqs, rows, width = layer_input.shape
    inner = query_weight.shape[1]
    heads = bias_table.shape[1]
    shard = width // depth
    slab = gate_weight.shape[1] // depth
    part = slab // 4
    piece = part // 2
    tokens = seqs * rows
    cut = tokens // 2
    buckets = BUCKETS // depth
    size, wide = slice_size(shard), column_cut(width)
    each = inner // depth // 6
    upper = [[group * GROUP + index for group in range(groups)] for index in range(GROUP)]
    is_zero = core == 0
    place = jnp.stack((low, zed)).astype(jnp.int32)
    meta = mine.astype(jnp.int32).reshape(1)
    spot = jnp.stack((core, chip)).astype(jnp.int32)

    half = jax.ShapeDtypeStruct((cut, width), BFLOAT)
    chips = [[group * GROUP + 2 * index + side for index in range(4)] for group in range(groups) for side in range(2)]

    def exchange(blocks):
        return lax.all_to_all(blocks, "ctx", split_axis=0, concat_axis=0, tiled=True, axis_index_groups=chips)

    x_near, x_far, own_cots = pl.pallas_call(
        rows_of_kernel,
        in_specs=[VMEM_WHOLE] * 2,
        out_specs=[VMEM_WHOLE] * 3,
        out_shape=[half, half, jax.ShapeDtypeStruct((8, cut, width), BFLOAT)],
        compiler_params=BIG,
        cost_estimate=moved(layer_input, layer_input, cotangent, cotangent),
        name="token_rows",
    )(jnp.swapaxes(layer_input, 1, 2), jnp.swapaxes(cotangent, 1, 2))
    inputs = gather_halves((x_near, x_far))

    def columns(weight):
        return jnp.concatenate(
            [lax.dynamic_slice_in_dim(weight, index * slab + chip * part, part, 1) for index in range(depth)], axis=1
        )

    pair_slice = jnp.where(is_zero, columns(gate_weight), columns(up_weight))
    down_slice = lax.dynamic_slice_in_dim(down_weight, chip * part + core * piece, piece, 0)

    packed = pl.pallas_call(
        functools.partial(pack_kernel, size=size, wide=wide),
        in_specs=[SMEM_WHOLE] + [VMEM_WHOLE] * 7,
        out_specs=VMEM_WHOLE,
        out_shape=jax.ShapeDtypeStruct((size + each + 16, 3 * inner), BFLOAT),
        cost_estimate=moved(query_weight, query_weight),
        name="pack",
    )(
        after(place, pair_slice, down_slice), query_weight, key_weight, value_weight, projection, gain_early.reshape(1, shard), gain_late.reshape(1, shard),
        jnp.pad(bias_table, ((0, 8 - buckets), (0, 128 - heads))),
    )
    packed = lax.all_gather(packed, "wsh", axis=0)
    pair_mine = lax.all_gather(after(pair_slice, packed), "wsh", axis=0, tiled=True)
    seg_rows = jnp.pad(segments.astype(BFLOAT), ((0, 16 - seqs), (0, 3 * inner - rows)))
    small = jnp.concatenate((packed[:, : size + each].reshape(-1, 3 * inner), seg_rows), axis=0)
    small = after(small, *inputs[2:6])
    near = gather_relay(small, small.shape[0] // 32 * 16)
    far = swap(near, 1)
    down_mine = lax.all_gather(after(down_slice, near), "wsh", axis=0, tiled=True).reshape(depth, piece, width)
    qkv_full, proj_full, gains, table, segs = pl.pallas_call(
        functools.partial(unpack_kernel, depth=depth, size=size, wide=wide),
        in_specs=[SMEM_WHOLE, VMEM_WHOLE, VMEM_WHOLE, VMEM_WHOLE],
        out_specs=[VMEM_WHOLE] * 5,
        out_shape=[
            jax.ShapeDtypeStruct((width, 3 * inner), BFLOAT),
            jax.ShapeDtypeStruct((inner, width), BFLOAT),
            jax.ShapeDtypeStruct((8, width), FLOAT),
            jax.ShapeDtypeStruct((BUCKETS, 128), FLOAT),
            jax.ShapeDtypeStruct((seqs, GROUP, rows), FLOAT),
        ],
        compiler_params=BIG,
        cost_estimate=moved(near, far, near),
        name="unpack",
    )(place, packed[:, size + each :], near, far)

    def whole(value, axis=0):
        if groups == 1:
            return value
        return lax.all_gather(value, "ctx", axis=axis, tiled=True, axis_index_groups=upper)

    segs = whole(segs, 1)

    normed, *kv, queries = norm_project(inputs, gains[0:1], qkv_full, inner)
    cots = exchange(own_cots)
    kv = [value.reshape(1, seqs, rows, 2 * inner) for value in kv]
    queries = queries.reshape(seqs, rows, inner)
    kv = [whole(value) for value in (*kv, *[swap(value, 1) for value in kv])]
    attention, lse = attention_forward(meta, table, segs, queries, kv)
    attn_low = attention.astype(BFLOAT).reshape(tokens, inner)
    attn = gather_direct(attn_low)

    after_attn, normed_late = late_norm(attn, inputs, proj_full, gains[1:2])
    pair_mine = after(pair_mine, attn_low)
    pair_other = swap(pair_mine, 1)
    down_mine = after(down_mine, normed_late)
    down_other = swap(down_mine, 1)
    activation, back_mine, back_other, out_part, *late_part, cot_all = feed_forward(
        spot, normed_late, cots, pair_mine, pair_other, (down_mine, down_other)
    )

    def flat(value):
        return value.reshape(4 * tokens, value.shape[2])

    def over_groups(value):
        return lax.psum(value, "ctx", axis_index_groups=upper) if groups > 1 else value

    late_own, first_near, first_far, second_near, second_far, last_near, last_far = late_part
    low, high = swap(last_near, 4), swap(last_far, 2)
    got_far, got_near = swap(first_far, 2), swap(second_near, 4)
    other_grad, mine_grad = outer_sums(normed_late, (back_other, back_mine))
    first_near, second_far = relay_sums((first_near, low), (second_far, high), mine_grad, got_far, got_near)
    late_parts = (swap(first_near, 2), got_near, got_far, swap(second_far, 4))
    other_got = [swap(other_grad[index : index + 1], 1) for index in range(2)]
    down_whole = outer_sums(activation, (cot_all,))[0]
    down_grad = down_whole.reshape(depth, 2, piece, width)
    down_keep = jnp.where(is_zero, down_grad[:, 0], down_grad[:, 1])
    down_send = jnp.where(is_zero, down_grad[:, 1], down_grad[:, 0])
    down_got = swap(down_send, 1)
    residual_grad, mix_low, attn_grad = middle(
        after_attn, late_own, late_parts, own_cots, gains[1:2], proj_full, down_whole, mine_grad
    )
    attn_grad = attn_grad.reshape(seqs, rows, inner)
    proj_grad = tn(attn_low, jnp.pad(mix_low, ((0, 0), (0, 4 * wide - width)))).astype(BFLOAT)
    dq, *dkv, table_part = attention_backward(meta, table, segs, queries, kv, attn_grad, attention, lse)

    def owned(value):
        if groups > 1:
            value = lax.psum_scatter(value, "ctx", scatter_dimension=0, tiled=True, axis_index_groups=upper)
        return value.reshape(1, tokens, 2 * inner)

    dkv = [owned(value) for value in dkv]
    dkv_got = [swap(value, 1) for value in dkv[4:]]
    dq = dq.reshape(tokens, inner)
    pair_sum = plus(mine_grad, other_got, mix_low).reshape(width, 2 * piece * depth)
    table_sum = jnp.transpose(jnp.sum(table_part, axis=-1).reshape(heads, BUCKETS)).reshape(depth, buckets, heads)
    table_sum = jnp.pad(table_sum, ((0, 0), (0, 16 - buckets), (0, 128 - heads))).reshape(depth * 16, 128).astype(BFLOAT)
    *dkv_four, keep, send = weight_grads(place, normed, dkv[:4], dkv_got, dq, table_sum, proj_grad, depth, size, wide, pair_sum)
    down_sum = plus(down_keep, [down_got], keep).reshape(depth * piece, width)
    pair_own = over_groups(lax.psum_scatter(pair_sum, "wsh", scatter_dimension=0, tiled=True))
    down_own = over_groups(lax.psum_scatter(down_sum, "wsh", scatter_dimension=0, tiled=True))
    out_parts = exchange(after(out_part, attn_grad)).astype(FLOAT).reshape(4, tokens, width)
    result = (after_attn + jnp.sum(out_parts, axis=0)).astype(BFLOAT)

    blocks = plus_apart(keep, swap(send, 1), result)
    dkv_parts = [swap(dkv_four[index], 2 * index) for index in range(1, 4)]
    input_grad = last(dq, dkv_four[0], dkv_parts, (x_near, x_far), residual_grad, gains[0:1], qkv_full)
    levels = sum_parts([blocks[0]] + [swap(blocks[index], 2 * index) for index in range(1, 4)], input_grad, pair_own)
    pair_near = gather_direct(after(pair_own, levels))
    down_near = gather_direct(after(down_own, levels))
    total = sum_parts(
        [levels[0]] + [swap_depth(levels[gap], gap) for gap in range(1, depth)], *pair_near[1:]
    )
    grads_near = gather_direct(over_groups(total))
    pair_far, down_far = [[swap(value, 1) for value in values] for values in (pair_near, down_near)]
    gate_out, up_out, late_sum = spread(place, pair_near, pair_far, gate_weight, up_weight, depth, part)
    down_out = pl.pallas_call(
        rows_kernel,
        grid=(slab // 128,),
        in_specs=[SMEM_WHOLE] + [once((piece, width))] * 8,
        out_specs=pl.BlockSpec((width, 128), lambda g: (0, g)),
        out_shape=jax.ShapeDtypeStruct((width, slab), FLOAT),
        scratch_shapes=[pltpu.VMEM((slab, width), BFLOAT)],
        compiler_params=BIG,
        cost_estimate=moved(down_own, down_own, down_own),
        name="join_down",
    )(place, *down_near, *down_far)
    grads_near = pl.pallas_call(
        skipping(stack_kernel, 4, 1),
        in_specs=[VMEM_WHOLE] * 4 + [UNREAD],
        out_specs=VMEM_WHOLE,
        out_shape=jax.ShapeDtypeStruct((4, *total.shape), BFLOAT),
        cost_estimate=moved(total, total),
        name="stack_small",
    )(*grads_near, late_sum)
    grads_far = swap(grads_near, 1)
    column = jax.ShapeDtypeStruct((shard, inner), FLOAT)
    query_out, key_out, value_out, proj_out, early_sum, table_rows = pl.pallas_call(
        functools.partial(finish_kernel, size=size, wide=wide),
        in_specs=[SMEM_WHOLE] + [VMEM_WHOLE] * 5,
        out_specs=[VMEM_WHOLE] * 6,
        out_shape=[
            column, column, column, jax.ShapeDtypeStruct((inner // depth, width), FLOAT),
            jax.ShapeDtypeStruct((shard, 128), FLOAT), jax.ShapeDtypeStruct((16, 128), FLOAT),
        ],
        compiler_params=BIG,
        cost_estimate=moved(grads_near, grads_far, grads_near),
        name="finish_small",
    )(place, grads_near, grads_far, query_weight, key_weight, value_weight)

    return (
        result.reshape(seqs, rows, width),
        input_grad.reshape(seqs, rows, width),
        query_out,
        key_out,
        value_out,
        proj_out,
        gate_out,
        up_out,
        jnp.transpose(down_out),
        early_sum[:, 0] / gain_early.astype(FLOAT),
        late_sum[:, 0] / gain_late.astype(FLOAT),
        table_rows[:buckets, :heads],
    )


def solution(mesh):
    rows = P("wsh", "ctx", None)
    split = P("wsh", None)
    vector = P("wsh")
    return jax.shard_map(
        on_device,
        mesh=mesh,
        in_specs=(rows, P("wsh", "ctx"), rows, split, split, split, split, split, split, split, vector, vector, split),
        out_specs=(rows, rows, split, split, split, split, split, split, split, vector, vector, split),
        check_vma=False,
    )
```

```python
import functools

import jax
import jax.numpy as jnp
import numpy as np
from jax import lax
from jax.experimental import pallas as pl
from jax.experimental.pallas import tpu as pltpu
from jax.sharding import PartitionSpec as P

BUCKETS = 32
GROUP = 8
EPSILON = 1e-06
NEGATIVE = -1e30
PRECISE = lax.Precision.HIGHEST
BUCKET_EDGES = (12, 16, 23, 32, 46, 64, 91)
FLOAT = jnp.float32
BFLOAT = jnp.bfloat16


SCALE = 0.2


def cost(flops, bytes_accessed, transcendentals):
    return pl.CostEstimate(
        flops=int(SCALE * flops), bytes_accessed=int(SCALE * bytes_accessed), transcendentals=int(SCALE * transcendentals)
    )


def bucket_number(offset):
    distance = abs(offset)
    level = distance if distance < 8 else 8 + sum(distance >= edge for edge in BUCKET_EDGES)
    return level + (16 if offset > 0 else 0)


def bucket_of(offsets):
    distance = jnp.abs(offsets)
    coarse = 8 + sum(((distance >= boundary).astype(jnp.int32) for boundary in BUCKET_EDGES))
    level = jnp.where(distance < 8, distance, coarse)
    return level + jnp.where(offsets > 0, 16, 0)


def near_radius(rows):
    return -(-(BUCKET_EDGES[-1] - 1) // rows)


def tile_offsets(block_gap, rows):
    keys = lax.broadcasted_iota(jnp.int32, (rows, rows), 0)
    queries = lax.broadcasted_iota(jnp.int32, (rows, rows), 1)
    return block_gap * rows + keys - queries


def tile_buckets(block_gap, rows):
    low, high = block_gap * rows - (rows - 1), block_gap * rows + (rows - 1)
    return sorted({bucket_number(offset) for offset in range(low, high + 1)})


def nt(left, right):
    return lax.dot_general(left, right, (((1,), (1,)), ((), ())), preferred_element_type=FLOAT)


def tn(left, right):
    return lax.dot_general(left, right, (((0,), (0,)), ((), ())), preferred_element_type=FLOAT)


def block_number(meta, half, position, count):
    low = lax.rem(meta, GROUP)
    part, group = divmod(position, count // 4)
    return group * GROUP + lax.bitwise_xor(low, jnp.int32(2 * part + half))


def tile_index(meta, half, position, count, radius):
    gap = block_number(meta, half, position, count) - meta
    return jnp.clip(gap, -(radius + 1), radius + 1) + radius + 1


def build_bias(bias_ref, table_ref, pair, rows, radius):
    for side, bucket in ((0, 15), (2 * radius + 2, 31)):
        for head in range(2):
            bias_ref[pair, head, side] = jnp.full((rows, rows), table_ref[bucket, 2 * pair + head], FLOAT)
    for gap in range(-radius, radius + 1):
        buckets = bucket_of(tile_offsets(gap, rows))
        present = tile_buckets(gap, rows)
        tiles = [jnp.full((rows, rows), table_ref[present[0], 2 * pair + head], FLOAT) for head in range(2)]
        for bucket in present[1:]:
            hit = buckets == bucket
            tiles = [jnp.where(hit, table_ref[bucket, 2 * pair + head], tiles[head]) for head in range(2)]
        for head in range(2):
            bias_ref[pair, head, gap + radius + 1] = tiles[head]


def build_mask(mask_ref, segs_ref, meta, seq, rows, count):
    own = segs_ref[seq, pl.ds(meta, 1), :]
    for half in range(2):
        for position in range(count):
            row = segs_ref[seq, pl.ds(block_number(meta, half, position, count), 1), :]
            keys = jnp.transpose(jnp.broadcast_to(row, (rows, rows)))
            mask_ref[seq, half * count + position] = jnp.where(keys == own, 0.0, NEGATIVE)


def half_scores(keys, query, meta, head, half, seq, bias_ref, mask_ref, rows, count, radius):
    raw = nt(keys, query)
    parts = []
    for position in range(count):
        extra = bias_ref[0, head, tile_index(meta, half, position, count, radius)]
        masked = mask_ref[0, half * count + position]
        parts.append(raw[position * rows : (position + 1) * rows] + (extra + masked))
    return jnp.concatenate(parts, axis=0)


def joined(refs):
    return jnp.concatenate([ref[...].reshape(-1, ref.shape[-1]) for ref in refs], axis=0)


def head_rows(value, head, lane):
    return jnp.where((lane < 64) == (head == 0), value, jnp.zeros_like(value))


def forward_kernel(
    meta_ref, bias_ref, mask_ref, q_ref, *refs, rows, count, radius,
):
    key_refs, value_refs, (out_ref, lse_ref) = refs[:8], refs[8:16], refs[16:]
    pair, seq = pl.program_id(0), pl.program_id(1)
    meta = meta_ref[0]

    query = q_ref[0]
    lane = lax.broadcasted_iota(jnp.int32, query.shape, 1)
    keys = [joined(key_refs[:4]), joined(key_refs[4:])]
    values = [joined(value_refs[:4]), joined(value_refs[4:])]
    pieces = []
    for head in range(2):
        one = head_rows(query, head, lane)
        scores = [
            half_scores(keys[half], one, meta, head, half, seq, bias_ref, mask_ref, rows, count, radius)
            for half in range(2)
        ]
        top = jnp.maximum(jnp.max(scores[0], axis=0, keepdims=True), jnp.max(scores[1], axis=0, keepdims=True))
        raised = [jnp.exp(part - top) for part in scores]
        total = jnp.sum(raised[0], axis=0, keepdims=True) + jnp.sum(raised[1], axis=0, keepdims=True)
        scale = 1.0 / total
        mixed = sum(tn(values[half], (raised[half] * scale).astype(BFLOAT)) for half in range(2))
        pieces.append(mixed[64 * head : 64 * head + 64])
        lse_ref[0, 0, head : head + 1] = top + jnp.log(total)
    out_ref[0] = jnp.transpose(jnp.concatenate(pieces, axis=0))


def backward_kernel(
    meta_ref, bias_ref, mask_ref, q_ref, *refs, rows, count, radius,
):
    key_refs, value_refs, (do_ref, out_ref, lse_ref, dq_ref) = refs[:8], refs[8:16], refs[16:20]
    both_refs, (tab_ref, sum_ref) = refs[20:28], refs[28:]
    pair, seq = pl.program_id(0), pl.program_id(1)
    meta = meta_ref[0]

    @pl.when(seq == 0)
    def _():
        sum_ref[...] = jnp.zeros_like(sum_ref)

    query, grad = q_ref[0], do_ref[0]
    lane = lax.broadcasted_iota(jnp.int32, query.shape, 1)
    keys = [joined(key_refs[:4]), joined(key_refs[4:])]
    values = [joined(value_refs[:4]), joined(value_refs[4:])]
    picks = (
        lax.broadcasted_iota(jnp.int32, (8, 128), 1) // 64 == lax.broadcasted_iota(jnp.int32, (8, 128), 0)
    ).astype(FLOAT)
    deltas = lax.dot_general(
        picks, grad.astype(FLOAT) * out_ref[0], (((1,), (1,)), ((), ())), precision=PRECISE, preferred_element_type=FLOAT
    )
    query_heads = [head_rows(query, head, lane) for head in range(2)]
    grad_heads = [head_rows(grad, head, lane) for head in range(2)]
    probs, slopes = [[], []], [[], []]
    pieces = []
    for head in range(2):
        logsum = lse_ref[0, 0, head : head + 1]
        delta = deltas[head : head + 1]
        flow = None
        for half in range(2):
            scores = half_scores(
                keys[half], query_heads[head], meta, head, half, seq, bias_ref, mask_ref, rows, count, radius
            )
            prob = jnp.exp(scores - logsum)
            slope = prob * (nt(values[half], grad_heads[head]) - delta)
            for position in range(count):
                index = tile_index(meta, half, position, count, radius)
                sum_ref[head, index] = sum_ref[head, index] + slope[position * rows : (position + 1) * rows]
            slope_low = slope.astype(BFLOAT)
            probs[half].append(prob.astype(BFLOAT))
            slopes[half].append(slope_low)
            term = tn(keys[half], slope_low)
            flow = term if flow is None else flow + term
        pieces.append(flow[64 * head : 64 * head + 64])
    dq_ref[0] = jnp.transpose(jnp.concatenate(pieces, axis=0)).astype(BFLOAT)
    query_stack = jnp.concatenate(query_heads, axis=0)
    grad_stack = jnp.concatenate(grad_heads, axis=0)
    for half in range(2):
        dk = jnp.dot(jnp.concatenate(slopes[half], axis=1), query_stack, preferred_element_type=FLOAT)
        dv = jnp.dot(jnp.concatenate(probs[half], axis=1), grad_stack, preferred_element_type=FLOAT)
        dk = dk.astype(BFLOAT).reshape(count, 1, rows, 128)
        dv = dv.astype(BFLOAT).reshape(count, 1, rows, 128)
        for part, both_ref in enumerate(both_refs[4 * half : 4 * half + 4]):
            side = slice(part * count // 4, (part + 1) * count // 4)
            both_ref[:, :, :, :128] = dk[side]
            both_ref[:, :, :, 128:] = dv[side]

    @pl.when(seq == pl.num_programs(1) - 1)
    def _():
        for head in range(2):
            sums = {}
            for side, bucket in ((0, 15), (2 * radius + 2, 31)):
                sums[bucket] = jnp.sum(sum_ref[head, side], axis=0, keepdims=True)
            for gap in range(-radius, radius + 1):
                buckets = bucket_of(tile_offsets(gap, rows))
                tile = sum_ref[head, gap + radius + 1]
                for bucket in tile_buckets(gap, rows):
                    part = jnp.sum(jnp.where(buckets == bucket, tile, 0.0), axis=0, keepdims=True)
                    sums[bucket] = sums[bucket] + part if bucket in sums else part
            for bucket in range(BUCKETS):
                tab_ref[0, head, bucket : bucket + 1] = sums.get(bucket, jnp.zeros((1, rows), FLOAT))


def prepare_kernel(meta_ref, table_ref, segs_ref, bias_ref, mask_ref, *, rows, count, radius):
    for pair in range(bias_ref.shape[0]):
        build_bias(bias_ref, table_ref, pair, rows, radius)
    for seq in range(mask_ref.shape[0]):
        build_mask(mask_ref, segs_ref, meta_ref[0], seq, rows, count)


def attention_terms(meta, table, segs, pairs, count):
    seqs, _, rows = segs.shape
    radius = near_radius(rows)
    return pl.pallas_call(
        functools.partial(prepare_kernel, rows=rows, count=count, radius=radius),
        in_specs=[pl.BlockSpec(memory_space=pltpu.SMEM)] * 2 + [pl.BlockSpec(memory_space=pltpu.VMEM)],
        out_specs=[pl.BlockSpec(memory_space=pltpu.VMEM)] * 2,
        out_shape=[
            jax.ShapeDtypeStruct((pairs, 2, 2 * radius + 3, rows, rows), FLOAT),
            jax.ShapeDtypeStruct((seqs, 2 * count, rows, rows), FLOAT),
        ],
        cost_estimate=cost(flops=0, bytes_accessed=10**6, transcendentals=0),
        name="attention_terms",
    )(meta, table, segs)


def attention_specs(bias, mask, rows, count):
    small = [
        pl.BlockSpec(memory_space=pltpu.SMEM),
        pl.BlockSpec((1, *bias.shape[1:]), lambda p, s: (p, 0, 0, 0, 0)),
        pl.BlockSpec((1, *mask.shape[1:]), lambda p, s: (s, 0, 0, 0)),
    ]
    query = pl.BlockSpec((1, rows, 128), lambda p, s: (s, 0, p))
    key = pl.BlockSpec((count // 4, 1, rows, 128), lambda p, s: (0, s, 0, 2 * p))
    value = pl.BlockSpec((count // 4, 1, rows, 128), lambda p, s: (0, s, 0, 2 * p + 1))
    stat = pl.BlockSpec((1, 1, 8, rows), lambda p, s: (p, s, 0, 0))
    return small, query, key, value, stat


def attention_cost(seqs, rows, keys, width, products):
    return cost(
        flops=2 * products * seqs * rows * keys * width,
        bytes_accessed=4 * seqs * keys * width * products,
        transcendentals=seqs * rows * keys * width // 64,
    )


def attention_forward(meta, bias, mask, queries, kv):
    seqs, rows, inner = queries.shape
    count, blocks, pairs = 4 * kv[0].shape[0], mask.shape[1], inner // 128
    radius = near_radius(rows)
    small, query, key, value, stat = attention_specs(bias, mask, rows, count)
    return pl.pallas_call(
        functools.partial(forward_kernel, rows=rows, count=count, radius=radius),
        grid=(pairs, seqs),
        in_specs=[*small, query, *[key] * 8, *[value] * 8],
        out_specs=[query, stat],
        out_shape=[
            jax.ShapeDtypeStruct((seqs, rows, inner), FLOAT),
            jax.ShapeDtypeStruct((pairs, seqs, 8, rows), FLOAT),
        ],
        cost_estimate=attention_cost(seqs, rows, blocks * rows, inner, 2),
        name="attention_forward",
    )(meta, bias, mask, queries, *kv, *kv)


def attention_backward(meta, bias, mask, queries, kv, grad, out, lse, *deps):
    seqs, rows, inner = queries.shape
    count, blocks, pairs = 4 * kv[0].shape[0], mask.shape[1], inner // 128
    radius = near_radius(rows)
    small, query, key, value, stat = attention_specs(bias, mask, rows, count)
    side = jax.ShapeDtypeStruct((count // 4, seqs, rows, 2 * inner), BFLOAT)
    both = pl.BlockSpec((count // 4, 1, rows, 256), lambda p, s: (0, s, 0, p))
    return pl.pallas_call(
        skipping(functools.partial(backward_kernel, rows=rows, count=count, radius=radius), 23, len(deps)),
        grid=(pairs, seqs),
        in_specs=[*small, query, *[key] * 8, *[value] * 8, query, query, stat] + [UNREAD] * len(deps),
        out_specs=[query, *[both] * 8, pl.BlockSpec((1, 2, BUCKETS, rows), lambda p, s: (p, 0, 0, 0))],
        out_shape=[
            jax.ShapeDtypeStruct((seqs, rows, inner), BFLOAT), *[side] * 8,
            jax.ShapeDtypeStruct((pairs, 2, BUCKETS, rows), FLOAT),
        ],
        scratch_shapes=[
            pltpu.VMEM((2, 2 * radius + 3, rows, rows), FLOAT),
        ],
        cost_estimate=attention_cost(seqs, rows, blocks * rows, inner, 5),
        name="attention_backward",
    )(meta, bias, mask, queries, *kv, *kv, grad, out, lse, *deps)


def swap(value, bit):
    count = lax.axis_size("ctx")
    return lax.ppermute(value, "ctx", [(source, source ^ bit) for source in range(count)])


def swap_depth(value, bit):
    count = lax.axis_size("wsh")
    return lax.ppermute(value, "wsh", [(source, source ^ bit) for source in range(count)])


def after(value, *others):
    return lax.optimization_barrier((value, *others))[0]


def gather_halves(own):
    near, far = own
    first_near, second_far = swap(near, 2), swap(far, 4)
    first_far, second_near = swap(far, 2), swap(near, 4)
    return [near, far, first_near, first_far, second_near, second_far, swap(first_near, 4), swap(second_far, 2)]


def gather_direct(own):
    return [own, swap(own, 2), swap(own, 4), swap(own, 6)]


def gather_relay(own, cut):
    first, second = swap(own, 2), swap(own, 4)
    return jnp.stack((own, first, second, jnp.concatenate((swap(first[:cut], 4), swap(second[cut:], 2)), axis=0)))


VMEM_WHOLE = pl.BlockSpec(memory_space=pltpu.VMEM)
UNREAD = pl.BlockSpec(memory_space=pl.ANY)


def skipping(kernel, inputs, count):
    return lambda *refs: kernel(*refs[:inputs], *refs[inputs + count :])


SMEM_WHOLE = pl.BlockSpec(memory_space=pltpu.SMEM)
BIG = pltpu.CompilerParams(vmem_limit_bytes=60 * 1024 * 1024)


def moved(*arrays):
    return cost(
        flops=0, bytes_accessed=sum(int(np.prod(array.shape)) * array.dtype.itemsize for array in arrays), transcendentals=0
    )


def slice_size(total):
    return -(-total // (GROUP * 16)) * 16


def slice_start(index, total, size):
    return jnp.minimum(index * size, total - size)


def column_cut(width):
    return -(-width // 512) * 128


def pack_kernel(place_ref, q_ref, k_ref, v_ref, proj_ref, early_ref, late_ref, table_ref, out_ref, *, size, wide):
    low = place_ref[0]
    chip, core = low // 2, lax.rem(low, 2)
    inner = q_ref.shape[1]
    shard = q_ref.shape[0]
    start = pl.multiple_of(slice_start(low, shard, size), 16)
    out_ref[:size, :inner] = q_ref[pl.ds(start, size), :]
    for index, ref in enumerate((k_ref, v_ref)):
        rows = ref[pl.ds(start, size), :]
        for pair in range(inner // 128):
            base = inner + 256 * pair + 128 * index
            out_ref[:size, base : base + 128] = rows[:, 128 * pair : 128 * pair + 128]
    part = proj_ref.shape[0] // 2
    each = part // 3
    out_ref[size:, :] = jnp.zeros((out_ref.shape[0] - size, out_ref.shape[1]), BFLOAT)
    for column in range(4):
        reach = min(wide, proj_ref.shape[1] - column * wide)

        @pl.when(chip == column)
        def _(column=column, reach=reach):
            for lane in range(3):
                row = pl.multiple_of(core * part + lane * each, 16)
                out_ref[size : size + each, lane * wide : lane * wide + reach] = proj_ref[
                    pl.ds(row, each), column * wide : column * wide + reach
                ]

    base = size + each
    out_ref[base : base + 1, :shard] = early_ref[...]
    out_ref[base + 1 : base + 2, :shard] = late_ref[...]
    out_ref[base + 8 : base + 16, :128] = table_ref[...]


def unpack_kernel(place_ref, misc_ref, near_ref, far_ref, qkv_ref, proj_ref, gains_ref, table_ref, segs_ref, *, depth, size, wide):
    low = place_ref[0]
    shard, part = qkv_ref.shape[0] // depth, proj_ref.shape[0] // depth // 2
    each = part // 3
    span = size + each
    buckets = table_ref.shape[0] // depth
    for level in range(depth):
        rows = misc_ref[level].astype(FLOAT)
        gains_ref[:, level * shard : (level + 1) * shard] = rows[:8, :shard]
        table_ref[level * buckets : (level + 1) * buckets, :] = rows[8 : 8 + buckets, :128]
    seqs, _, rows = segs_ref.shape
    for index in range(GROUP):
        gap = lax.bitwise_xor(low, jnp.int32(index))
        slot, odd = gap // 2, lax.rem(gap, 2)
        block = jnp.where(odd == 0, near_ref[slot], far_ref[slot])
        for level in range(depth):
            base = level * shard + min(index * size, shard - size)
            qkv_ref[base : base + size, :] = block[level * span : level * span + size]
            column = (index // 2) * wide
            reach = min(wide, proj_ref.shape[1] - column)
            for lane in range(3):
                base = (level * 2 + index % 2) * part + lane * each
                proj_ref[base : base + each, column : column + reach] = block[
                    level * span + size : level * span + span, lane * wide : lane * wide + reach
                ]
        own = block[depth * span : depth * span + 16, :128].astype(FLOAT)
        for seq in range(seqs):
            segs_ref[seq, index : index + 1, :] = own[seq : seq + 1, :rows]


def grad_kernel(
    place_ref, normed_ref, *refs, depth, size, wide
):
    owns, gots, (dq_ref, table_ref, proj_ref) = refs[:4], refs[4:8], refs[8:11]
    sums, (keep_ref, send_ref, kv_scr, q_scr, t_scr) = refs[11:15], refs[15:]
    step = pl.program_id(0)
    tokens = dq_ref.shape[0]
    for index in range(4):

        @pl.when(step == index // 2)
        def _(index=index):
            total = (owns[index][0].astype(FLOAT) + gots[index][0].astype(FLOAT)).astype(BFLOAT)
            t_scr[index % 2 * tokens : (index % 2 + 1) * tokens, :] = total
            sums[index][...] = total

    turned = jnp.transpose(normed_ref[...].reshape(2 * tokens, normed_ref.shape[2]))
    product = jnp.dot(turned, t_scr[...], preferred_element_type=FLOAT)

    @pl.when(step == 0)
    def _():
        kv_scr[...] = product
        q_scr[...] = jnp.dot(turned[:, :tokens], dq_ref[...], preferred_element_type=FLOAT).astype(BFLOAT)

    @pl.when(step == 1)
    def _():
        kv_scr[...] = kv_scr[...] + product
        low = place_ref[0]
        zed = place_ref[1]
        inner = q_scr.shape[1]
        shard = q_scr.shape[0] // depth
        for index in range(GROUP):
            target = lax.bitwise_xor(low, jnp.int32(index))
            out_ref = keep_ref if index % 2 == 0 else send_ref
            for gap in range(depth):
                level = lax.bitwise_xor(zed, jnp.int32(gap))
                start = pl.multiple_of(level * shard + slice_start(target, shard, size), 16)
                out_ref[index // 2, gap, :size, :inner] = q_scr[pl.ds(start, size), :]
                out_ref[index // 2, gap, :size, inner:] = kv_scr[pl.ds(start, size), :].astype(BFLOAT)
                part = proj_ref.shape[0] // depth // 2
                each = part // 3
                column = pl.multiple_of((target // 2) * wide, 128)
                for lane in range(3):
                    row = pl.multiple_of((level * 2 + lax.rem(target, 2)) * part + lane * each, 16)
                    out_ref[index // 2, gap, size:, lane * wide : (lane + 1) * wide] = proj_ref[
                        pl.ds(row, each), pl.ds(column, wide)
                    ]
                last = target == GROUP - 1
                rows = table_ref[pl.ds(pl.multiple_of(level * 16, 16), 16), :]
                out_ref[index // 2, gap, :16, :128] = jnp.where(last, rows, out_ref[index // 2, gap, :16, :128])


def weight_grads(place, normed, own, got, dq, table, proj, depth, size, wide, *deps):
    _, tokens, width = normed.shape
    inner = dq.shape[1]
    block = once((1, tokens, 2 * inner))
    summed = pl.BlockSpec((tokens, 2 * inner), lambda g: (0, 0))
    span = size + proj.shape[0] // depth // 6
    piece = jax.ShapeDtypeStruct((4, depth, span, 3 * inner), BFLOAT)
    kept = pl.BlockSpec((4, depth, span, 3 * inner), lambda g: (0, 0, 0, 0))
    return pl.pallas_call(
        skipping(functools.partial(grad_kernel, depth=depth, size=size, wide=wide), 13, len(deps)),
        grid=(2,),
        in_specs=[
            SMEM_WHOLE, pl.BlockSpec((2, tokens, width), lambda g: (g, 0, 0)), *[block] * 8, once(dq.shape), once(table.shape),
            once(proj.shape),
        ]
        + [UNREAD] * len(deps),
        out_specs=[*[summed] * 4, kept, kept],
        out_shape=[*[jax.ShapeDtypeStruct((tokens, 2 * inner), BFLOAT)] * 4, piece, piece],
        scratch_shapes=[
            pltpu.VMEM((width, 2 * inner), FLOAT), pltpu.VMEM((width, inner), BFLOAT), pltpu.VMEM((2 * tokens, 2 * inner), BFLOAT),
        ],
        compiler_params=BIG,
        cost_estimate=cost(flops=18 * tokens * width * inner, bytes_accessed=12 * tokens * width, transcendentals=0),
        name="weight_grads",
    )(place, normed, *own, *got, dq, table, proj, *deps)


def pick_block(refs, step, scratch_ref):
    cut = refs[0].shape[0]
    for index in range(4):

        @pl.when(step == index)
        def _(index=index):
            scratch_ref[:cut] = refs[2 * index][...]
            scratch_ref[cut:] = refs[2 * index + 1][...]


def pick_whole(refs, step, scratch_ref):
    for index in range(4):

        @pl.when(step == index)
        def _(index=index):
            scratch_ref[...] = refs[index][...]


def once(shape):
    return pl.BlockSpec(shape, lambda g, *_: (0,) * len(shape), pipeline_mode=pl.Buffered(1))


def norm_kernel(*refs, inner):
    pieces, (gain_ref, weight_ref, normed_ref, k0, k1, k2, k3, q_ref, x_scr) = refs[:8], refs[8:]
    step = pl.program_id(0)
    pick_block(pieces, step, x_scr)
    hidden = x_scr[...].astype(FLOAT)
    scale = lax.rsqrt(jnp.mean(hidden * hidden, axis=-1, keepdims=True) + EPSILON)
    normed = (hidden * scale * gain_ref[...]).astype(BFLOAT)
    normed_ref[0] = normed
    both = jnp.dot(normed, weight_ref[:, inner:], preferred_element_type=FLOAT).astype(BFLOAT)

    for index, kv_ref in enumerate((k0, k1, k2, k3)):

        @pl.when(step == index)
        def _(kv_ref=kv_ref):
            kv_ref[0] = both

    @pl.when(step == 0)
    def _():
        q_ref[...] = jnp.dot(normed, weight_ref[:, :inner], preferred_element_type=FLOAT).astype(BFLOAT)


def norm_project(pieces, gain, weight, inner):
    tokens, width = 2 * pieces[0].shape[0], pieces[0].shape[1]
    return pl.pallas_call(
        functools.partial(norm_kernel, inner=inner),
        grid=(4,),
        in_specs=[*[once(piece.shape) for piece in pieces], once(gain.shape), once(weight.shape)],
        out_specs=[
            pl.BlockSpec((1, tokens, width), lambda g: (g, 0, 0)),
            *[pl.BlockSpec((1, tokens, 2 * inner), lambda g: (0, 0, 0))] * 4,
            pl.BlockSpec((tokens, inner), lambda g: (0, 0)),
        ],
        out_shape=[
            jax.ShapeDtypeStruct((4, tokens, width), BFLOAT),
            *[jax.ShapeDtypeStruct((1, tokens, 2 * inner), BFLOAT)] * 4,
            jax.ShapeDtypeStruct((tokens, inner), BFLOAT),
        ],
        scratch_shapes=[pltpu.VMEM((tokens, width), BFLOAT)],
        compiler_params=BIG,
        cost_estimate=cost(
            flops=18 * tokens * width * inner, bytes_accessed=18 * tokens * width, transcendentals=0
        ),
        name="norm_project",
    )(*pieces, gain, weight)


GELU_SCALE = float(np.sqrt(2.0 / np.pi))


def late_kernel(*refs):
    attn, inputs = refs[:4], refs[4:12]
    proj_ref, gain_ref, after_ref, normed_ref, a_scr, x_scr = refs[12:]
    step = pl.program_id(0)
    pick_whole(attn, step, a_scr)
    pick_block(inputs, step, x_scr)
    after_attn = x_scr[...].astype(FLOAT) + jnp.dot(a_scr[...], proj_ref[...], preferred_element_type=FLOAT)

    @pl.when(step == 0)
    def _():
        after_ref[...] = after_attn

    scale = lax.rsqrt(jnp.mean(after_attn * after_attn, axis=-1, keepdims=True) + EPSILON)
    normed_ref[0] = (after_attn * scale * gain_ref[...]).astype(BFLOAT)


def late_norm(attn, inputs, proj, gain):
    tokens, inner = attn[0].shape
    width = proj.shape[1]
    return pl.pallas_call(
        late_kernel,
        grid=(4,),
        in_specs=[once(value.shape) for value in (*attn, *inputs, proj, gain)],
        out_specs=[
            pl.BlockSpec((tokens, width), lambda g: (0, 0)), pl.BlockSpec((1, tokens, width), lambda g: (g, 0, 0)),
        ],
        out_shape=[
            jax.ShapeDtypeStruct((tokens, width), FLOAT), jax.ShapeDtypeStruct((4, tokens, width), BFLOAT),
        ],
        scratch_shapes=[pltpu.VMEM((tokens, inner), BFLOAT), pltpu.VMEM((tokens, width), BFLOAT)],
        compiler_params=BIG,
        cost_estimate=cost(flops=8 * tokens * width * inner, bytes_accessed=24 * tokens * width, transcendentals=0),
        name="late_norm",
    )(*attn, *inputs, proj, gain)


def feed_kernel(
    spot_ref, normed_ref, cots_ref, mine_ref, other_ref, down_mine, down_other,
    act_ref, dmine_ref, dother_ref, out_ref, l0, *refs
):
    late_refs, (cot_ref, down_ref) = refs[:6], refs[6:]
    is_zero = spot_ref[0] == 0
    tokens = normed_ref.shape[1]

    @pl.when(pl.program_id(0) == 0)
    def _():
        depth, piece, _ = down_mine.shape
        for level in range(depth):
            first = jnp.where(is_zero, down_mine[level], down_other[level])
            second = jnp.where(is_zero, down_other[level], down_mine[level])
            down_ref[2 * level * piece : (2 * level + 1) * piece, :] = first
            down_ref[(2 * level + 1) * piece : (2 * level + 2) * piece, :] = second

    cot = cots_ref[...].reshape(tokens, cots_ref.shape[2])
    cot_ref[0] = cot
    normed = normed_ref[0]
    pre_mine = jnp.dot(normed, mine_ref[...], preferred_element_type=FLOAT)
    pre_other = jnp.dot(normed, other_ref[...], preferred_element_type=FLOAT)
    gate = jnp.where(is_zero, pre_mine, pre_other)
    up = jnp.where(is_zero, pre_other, pre_mine)
    square = gate * gate
    lifted = jnp.tanh(GELU_SCALE * (gate + 0.044715 * gate * square))
    gate_half = 0.5 * (1.0 + lifted)
    smooth = gate * gate_half
    act = (smooth * up).astype(BFLOAT)
    act_ref[0] = act
    out = jnp.dot(act, down_ref[...], preferred_element_type=FLOAT).astype(BFLOAT)
    out_ref[...] = out.reshape(out_ref.shape)
    act_back = nt(cot, down_ref[...])
    slope = gate_half + 0.5 * gate * (1.0 - lifted * lifted) * (GELU_SCALE * (1.0 + 3 * 0.044715 * square))
    gate_back = act_back * up * slope
    up_back = act_back * smooth
    dmine = jnp.where(is_zero, gate_back, up_back).astype(BFLOAT)
    dother = jnp.where(is_zero, up_back, gate_back).astype(BFLOAT)
    dmine_ref[0] = dmine
    dother_ref[0] = dother
    late = (nt(dmine, mine_ref[...]) + nt(dother, other_ref[...])).astype(BFLOAT)
    half = late.shape[0] // 2

    @pl.when(pl.program_id(0) == 0)
    def _():
        l0[...] = late.reshape(l0.shape)

    for index in range(3):

        @pl.when(pl.program_id(0) == index + 1)
        def _(index=index):
            late_refs[2 * index][...] = late[:half]
            late_refs[2 * index + 1][...] = late[half:]


def feed_forward(spot, normed, cots, mine, other, downs):
    _, tokens, width = normed.shape
    wide = mine.shape[1]

    def block(size):
        return pl.BlockSpec((1, tokens, size), lambda g, spot: (g, 0, 0))

    def shape(size):
        return jax.ShapeDtypeStruct((4, tokens, size), BFLOAT)

    placed = pl.BlockSpec((2, tokens // 2, width), lambda g, spot: (lax.bitwise_xor(g, spot[1]), 0, 0))
    sent = jax.ShapeDtypeStruct((8, tokens // 2, width), BFLOAT)
    half = jax.ShapeDtypeStruct((2, tokens // 2, width), BFLOAT)
    piece = pl.BlockSpec((2, tokens // 2, width), lambda g, spot: (0, 0, 0))
    rows = jax.ShapeDtypeStruct((tokens // 2, width), BFLOAT)
    part = pl.BlockSpec((tokens // 2, width), lambda g, spot: (0, 0))
    return pl.pallas_call(
        feed_kernel,
        grid_spec=pltpu.PrefetchScalarGridSpec(
            num_scalar_prefetch=1,
            grid=(4,),
            in_specs=[block(width), placed, *[once(value.shape) for value in (mine, other, *downs)]],
            out_specs=[block(wide), block(wide), block(wide), placed, piece, *[part] * 6, block(width)],
            scratch_shapes=[pltpu.VMEM((wide, width), BFLOAT)],
        ),
        out_shape=[shape(wide), shape(wide), shape(wide), sent, half, *[rows] * 6, shape(width)],
        compiler_params=BIG,
        cost_estimate=cost(
            flops=48 * tokens * width * wide, bytes_accessed=30 * tokens * width, transcendentals=4 * tokens * wide
        ),
        name="feed_forward",
    )(spot, normed, cots, mine, other, *downs)


def outer_kernel(left_ref, *refs):
    count = len(refs) // 3
    rights, outs, scratch = refs[:count], refs[count : 2 * count], refs[2 * count :]
    step = pl.program_id(0)

    def rows(ref):
        return ref[...].reshape(-1, ref.shape[2])

    left = jnp.transpose(rows(left_ref))
    for right_ref, out_ref, acc_ref in zip(rights, outs, scratch):
        part = jnp.dot(left, rows(right_ref), preferred_element_type=FLOAT).reshape(out_ref.shape)

        @pl.when(step == 0)
        def _(acc_ref=acc_ref, part=part):
            acc_ref[...] = part

        @pl.when(step == 1)
        def _(acc_ref=acc_ref, out_ref=out_ref, part=part):
            out_ref[...] = (acc_ref[...] + part).astype(BFLOAT)


def outer_sums(left, rights):
    _, tokens, width = left.shape
    shapes = [(2, width // 2, right.shape[2]) for right in rights]
    return pl.pallas_call(
        outer_kernel,
        grid=(2,),
        in_specs=[pl.BlockSpec((2, tokens, value.shape[2]), lambda g: (g, 0, 0)) for value in (left, *rights)],
        out_specs=[pl.BlockSpec(shape, lambda g: (0, 0, 0)) for shape in shapes],
        out_shape=[jax.ShapeDtypeStruct(shape, BFLOAT) for shape in shapes],
        scratch_shapes=[pltpu.VMEM(shape, FLOAT) for shape in shapes],
        compiler_params=BIG,
        cost_estimate=cost(flops=16 * tokens * width * sum(shape[2] for shape in shapes), bytes_accessed=0, transcendentals=0),
        name="outer_sums",
    )(left, *rights)


def norm_back(hidden, gain, back):
    scale = lax.rsqrt(jnp.mean(hidden * hidden, axis=-1, keepdims=True) + EPSILON)
    lifted = back * gain
    return scale * lifted - hidden * (scale * scale * scale) * jnp.mean(lifted * hidden, axis=-1, keepdims=True)


def quarter_specs(tile, width):
    whole = pl.BlockSpec((tile, width), lambda g: (g, 0))
    near = pl.BlockSpec((tile, width), lambda g: (jnp.minimum(g, 1), 0))
    far = pl.BlockSpec((tile, width), lambda g: (jnp.maximum(g - 2, 0), 0))
    return whole, [near, near, far, far]


def summed(own_ref, parts):
    near = pl.program_id(0) < 2
    first = jnp.where(near, parts[0][...], parts[2][...]).astype(FLOAT)
    second = jnp.where(near, parts[1][...], parts[3][...]).astype(FLOAT)
    return own_ref[...].astype(FLOAT) + first + second


def middle_kernel(after_ref, own_ref, n0, n1, f0, f1, cot_ref, gain_ref, proj_ref, residual_ref, mix_ref, attn_ref):
    near = pl.program_id(0) < 2
    back = own_ref[0].astype(FLOAT) + jnp.where(near, n0[...], f0[...]).astype(FLOAT)
    back = back + jnp.where(near, n1[...], f1[...]).astype(FLOAT)
    residual = cot_ref[0].astype(FLOAT) + norm_back(after_ref[...], gain_ref[...], back)
    residual_ref[...] = residual
    mix = residual.astype(BFLOAT)
    mix_ref[...] = mix
    attn_ref[...] = nt(mix, proj_ref[...]).astype(BFLOAT)


def middle(after_attn, own, parts, cots, gain, proj, *deps):
    tokens, width = after_attn.shape
    inner = proj.shape[0]
    tile = tokens // 4
    whole = pl.BlockSpec((tile, width), lambda g: (g, 0))
    half = pl.BlockSpec((1, tile, width), lambda g: (g // 2, g % 2, 0))
    near = pl.BlockSpec((tile, width), lambda g: (jnp.minimum(g, 1), 0))
    far = pl.BlockSpec((tile, width), lambda g: (jnp.maximum(g - 2, 0), 0))
    return pl.pallas_call(
        skipping(middle_kernel, 9, len(deps)),
        grid=(4,),
        in_specs=[whole, half, near, near, far, far, half, once(gain.shape), once(proj.shape)] + [UNREAD] * len(deps),
        out_specs=[whole, whole, pl.BlockSpec((tile, inner), lambda g: (g, 0))],
        out_shape=[
            jax.ShapeDtypeStruct((tokens, width), FLOAT),
            jax.ShapeDtypeStruct((tokens, width), BFLOAT),
            jax.ShapeDtypeStruct((tokens, inner), BFLOAT),
        ],
        compiler_params=BIG,
        cost_estimate=pl.CostEstimate(flops=10**11, bytes_accessed=0, transcendentals=0),
        name="middle",
    )(after_attn, own, *parts, cots, gain, proj, *deps)


def apart_kernel(left_ref, right_ref, *outs):
    for index, out_ref in enumerate(outs):

        @pl.when(pl.program_id(0) == index)
        def _(out_ref=out_ref):
            out_ref[...] = (left_ref[0].astype(FLOAT) + right_ref[0].astype(FLOAT)).astype(BFLOAT)


def plus_apart(left, right, *deps):
    count, *shape = left.shape
    spec = pl.BlockSpec((1, *shape), lambda g: (g,) + (0,) * len(shape))
    return pl.pallas_call(
        skipping(apart_kernel, 2, len(deps)),
        grid=(count,),
        in_specs=[spec, spec] + [UNREAD] * len(deps),
        out_specs=[pl.BlockSpec(tuple(shape), lambda g: (0,) * len(shape))] * count,
        out_shape=[jax.ShapeDtypeStruct(tuple(shape), BFLOAT)] * count,
        compiler_params=BIG,
        cost_estimate=moved(left, left, left),
        name="plus_apart",
    )(left, right, *deps)


def relay_kernel(a_ref, b_ref, c_ref, d_ref, first_ref, second_ref):
    first_ref[...] = (a_ref[...].astype(FLOAT) + b_ref[...].astype(FLOAT)).astype(BFLOAT)
    second_ref[...] = (c_ref[...].astype(FLOAT) + d_ref[...].astype(FLOAT)).astype(BFLOAT)


def relay_sums(first, second, *deps):
    shape = jax.ShapeDtypeStruct(first[0].shape, BFLOAT)
    return pl.pallas_call(
        skipping(relay_kernel, 4, len(deps)),
        in_specs=[VMEM_WHOLE] * 4 + [UNREAD] * len(deps),
        out_specs=[VMEM_WHOLE] * 2,
        out_shape=[shape, shape],
        cost_estimate=moved(*first, *second),
        name="relay_sums",
    )(*first, *second, *deps)


def plus_kernel(left_ref, *refs):
    rights, out_ref = refs[:-1], refs[-1]
    for index, right_ref in enumerate(rights):

        @pl.when(pl.program_id(0) * len(rights) // pl.num_programs(0) == index)
        def _(right_ref=right_ref):
            out_ref[0] = (left_ref[0].astype(FLOAT) + right_ref[0].astype(FLOAT)).astype(BFLOAT)


def plus(left, rights, *deps):
    shape = left.shape
    each = shape[0] // len(rights)
    spec = pl.BlockSpec((1, *shape[1:]), lambda g: (g,) + (0,) * (len(shape) - 1))

    def part(index):
        return pl.BlockSpec(
            (1, *shape[1:]), lambda g: (jnp.clip(g - index * each, 0, each - 1),) + (0,) * (len(shape) - 1)
        )

    return pl.pallas_call(
        skipping(plus_kernel, 1 + len(rights), len(deps)),
        grid=(shape[0],),
        in_specs=[spec, *[part(index) for index in range(len(rights))]] + [UNREAD] * len(deps),
        out_specs=spec,
        out_shape=jax.ShapeDtypeStruct(shape, BFLOAT),
        compiler_params=BIG,
        cost_estimate=moved(left, left, left),
        name="plus",
    )(left, *rights, *deps)


def last_kernel(dq_ref, own_ref, p1, p2, p3, x_ref, residual_ref, gain_ref, weight_ref, out_ref):
    dkv = sum(ref[...].astype(FLOAT) for ref in (own_ref, p1, p2, p3)).astype(BFLOAT)
    inner = dq_ref.shape[1]
    back = nt(dq_ref[...], weight_ref[:, :inner]) + nt(dkv, weight_ref[:, inner:])
    hidden = jnp.transpose(x_ref[0]).astype(FLOAT)
    grad = (residual_ref[...] + norm_back(hidden, gain_ref[...], back)).astype(BFLOAT)
    out_ref[0] = jnp.transpose(grad)


def last(dq, own, parts, turned, residual, gain, weight):
    seqs, width, rows = turned.shape
    inner = dq.shape[1]
    whole = pl.BlockSpec((rows, width), lambda g: (g, 0))
    piece = pl.BlockSpec((rows, 2 * inner), lambda g: (g, 0))
    block = pl.BlockSpec((1, width, rows), lambda g: (g, 0, 0))
    return pl.pallas_call(
        last_kernel,
        grid=(seqs,),
        in_specs=[
            pl.BlockSpec((rows, inner), lambda g: (g, 0)), piece, piece, piece, piece, block, whole,
            once(gain.shape), once(weight.shape),
        ],
        out_specs=block,
        out_shape=jax.ShapeDtypeStruct((seqs, width, rows), BFLOAT),
        compiler_params=BIG,
        cost_estimate=pl.CostEstimate(flops=10**11, bytes_accessed=0, transcendentals=0),
        name="input_gradient",
    )(dq, own, *parts, turned, residual, gain, weight)


def output_kernel(after_ref, parts_ref, out_ref):
    total = after_ref[...]
    for index in range(4):
        total = total + parts_ref[index].astype(FLOAT)
    out_ref[0] = jnp.transpose(total.astype(BFLOAT))


def output_sum(after_attn, parts, seqs):
    tokens, width = after_attn.shape
    rows = tokens // seqs
    return pl.pallas_call(
        output_kernel,
        grid=(seqs,),
        in_specs=[
            pl.BlockSpec((rows, width), lambda g: (g, 0)), pl.BlockSpec((4, rows, width), lambda g: (0, g, 0)),
        ],
        out_specs=pl.BlockSpec((1, width, rows), lambda g: (g, 0, 0)),
        out_shape=jax.ShapeDtypeStruct((seqs, width, rows), BFLOAT),
        compiler_params=BIG,
        cost_estimate=moved(after_attn, parts),
        name="output_sum",
    )(after_attn, parts)


def choose(refs, slot):
    value = refs[0][...]
    for index in range(1, len(refs)):
        value = jnp.where(slot == index, refs[index][...], value)
    return value


def spread_kernel(place_ref, *refs, depth, part):
    nears, fars, (gate_ref, up_ref, gate_out, up_out, late_ref) = refs[:4], refs[4:8], refs[8:]
    low = place_ref[0]
    chip, core = low // 2, lax.rem(low, 2)
    for index in range(4):
        slot = lax.bitwise_xor(chip, jnp.int32(index))
        near, far = choose(nears, slot), choose(fars, slot)
        gate = jnp.where(core == 0, near, far).astype(FLOAT)
        up = jnp.where(core == 0, far, near).astype(FLOAT)
        for level in range(depth):
            base = (level * 4 + index) * part
            gate_out[:, base : base + part] = gate[:, level * part : (level + 1) * part]
            up_out[:, base : base + part] = up[:, level * part : (level + 1) * part]
    total = gate_out[...] * gate_ref[...].astype(FLOAT) + up_out[...] * up_ref[...].astype(FLOAT)
    late_ref[...] = jnp.broadcast_to(jnp.sum(total, axis=1, keepdims=True), late_ref.shape)


def spread(place, nears, fars, gate, up, depth, part):
    shard, hidden = gate.shape
    tile = 184 if shard % 184 == 0 else shard
    pieces = pl.BlockSpec((tile, nears[0].shape[1]), lambda g: (g, 0))
    rows = pl.BlockSpec((tile, hidden), lambda g: (g, 0))
    return pl.pallas_call(
        functools.partial(spread_kernel, depth=depth, part=part),
        grid=(shard // tile,),
        in_specs=[SMEM_WHOLE, *[pieces] * 8, rows, rows],
        out_specs=[rows, rows, pl.BlockSpec((tile, 128), lambda g: (g, 0))],
        out_shape=[
            jax.ShapeDtypeStruct((shard, hidden), FLOAT),
            jax.ShapeDtypeStruct((shard, hidden), FLOAT),
            jax.ShapeDtypeStruct((shard, 128), FLOAT),
        ],
        compiler_params=BIG,
        cost_estimate=cost(flops=4 * shard * hidden, bytes_accessed=16 * shard * hidden, transcendentals=0),
        name="spread_columns",
    )(place, *nears, *fars, gate, up)


def rows_kernel(place_ref, *refs):
    nears, fars, (out_ref, scratch_ref) = refs[:4], refs[4:8], refs[8:]
    low = place_ref[0]
    size = nears[0].shape[0]

    @pl.when(pl.program_id(0) == 0)
    def _():
        for index in range(GROUP):
            gap = lax.bitwise_xor(low, jnp.int32(index))
            slot, odd = gap // 2, lax.rem(gap, 2)
            rows = jnp.where(odd == 0, choose(nears, slot), choose(fars, slot))
            scratch_ref[index * size : (index + 1) * size, :] = rows

    base = pl.multiple_of(pl.program_id(0) * 128, 128)
    out_ref[...] = jnp.transpose(scratch_ref[pl.ds(base, 128), :].astype(FLOAT))


def gathered_kernel(own_ref, *refs):
    total = own_ref[...].astype(FLOAT)
    for ref in refs[:-1]:
        total = total + ref[...].astype(FLOAT)
    refs[-1][...] = total.astype(BFLOAT)


def sum_parts(parts, *deps):
    return pl.pallas_call(
        skipping(gathered_kernel, len(parts), len(deps)),
        in_specs=[VMEM_WHOLE] * len(parts) + [UNREAD] * len(deps),
        out_specs=VMEM_WHOLE,
        out_shape=jax.ShapeDtypeStruct(parts[0].shape, BFLOAT),
        cost_estimate=moved(*parts),
        name="sum_parts",
    )(*parts, *deps)


def stack_kernel(*refs):
    for index, ref in enumerate(refs[:-1]):
        refs[-1][index] = ref[...]


def finish_kernel(
    place_ref, near_ref, far_ref, q_ref, k_ref, v_ref, q_out, k_out, v_out, proj_out, early_ref, table_ref, *, size, wide
):
    low = place_ref[0]
    shard, inner = q_ref.shape
    part = proj_out.shape[0] // 2
    each = part // 3
    for index in range(GROUP):
        gap = lax.bitwise_xor(low, jnp.int32(index))
        slot, odd = gap // 2, lax.rem(gap, 2)
        block = jnp.where(odd == 0, near_ref[slot], far_ref[slot]).astype(FLOAT)
        base = min(index * size, shard - size)
        skip = index * size - base
        q_out[base + skip : base + size, :] = block[skip:size, :inner]
        for pair in range(inner // 128):
            for offset, out_ref in enumerate((k_out, v_out)):
                column = inner + 256 * pair + 128 * offset
                out_ref[base + skip : base + size, 128 * pair : 128 * pair + 128] = block[skip:size, column : column + 128]
        if index == GROUP - 1:
            table_ref[...] = block[:16, :128]
        column = (index // 2) * wide
        reach = min(wide, proj_out.shape[1] - column)
        for lane in range(3):
            base = (index % 2) * part + lane * each
            proj_out[base : base + each, column : column + reach] = block[size:, lane * wide : lane * wide + reach]
    total = q_out[...] * q_ref[...].astype(FLOAT) + k_out[...] * k_ref[...].astype(FLOAT)
    total = total + v_out[...] * v_ref[...].astype(FLOAT)
    early_ref[...] = jnp.broadcast_to(jnp.sum(total, axis=1, keepdims=True), early_ref.shape)


def rows_of_kernel(x_ref, cot_ref, near_ref, far_ref, rows_ref):
    rows, cut = x_ref.shape[2], near_ref.shape[0]
    for seq in range(x_ref.shape[0]):
        turned = jnp.transpose(x_ref[seq])
        start = seq * rows
        split = min(max(cut - start, 0), rows)
        if split > 0:
            near_ref[start : start + split, :] = turned[:split]
        if split < rows:
            far_ref[start + split - cut : start + rows - cut, :] = turned[split:]
        turned = jnp.transpose(cot_ref[seq])
        for copy in range(4):
            if split > 0:
                rows_ref[2 * copy, start : start + split, :] = turned[:split]
            if split < rows:
                rows_ref[2 * copy + 1, start + split - cut : start + rows - cut, :] = turned[split:]


def on_device(
    layer_input, segments, cotangent, query_weight, key_weight, value_weight, projection, gate_weight, up_weight,
    down_weight, gain_early, gain_late, bias_table,
):
    ring = lax.axis_size("ctx")
    depth = lax.axis_size("wsh")
    groups = ring // GROUP
    mine = lax.axis_index("ctx")
    low = lax.rem(mine, GROUP)
    chip, core = low // 2, lax.rem(low, 2)
    zed = lax.axis_index("wsh")
    seqs, rows, width = layer_input.shape
    inner = query_weight.shape[1]
    heads = bias_table.shape[1]
    shard = width // depth
    slab = gate_weight.shape[1] // depth
    part = slab // 4
    piece = part // 2
    tokens = seqs * rows
    cut = tokens // 2
    buckets = BUCKETS // depth
    size, wide = slice_size(shard), column_cut(width)
    each = inner // depth // 6
    upper = [[group * GROUP + index for group in range(groups)] for index in range(GROUP)]
    is_zero = core == 0
    place = jnp.stack((low, zed)).astype(jnp.int32)
    meta = mine.astype(jnp.int32).reshape(1)
    spot = jnp.stack((core, chip)).astype(jnp.int32)

    half = jax.ShapeDtypeStruct((cut, width), BFLOAT)
    chips = [[group * GROUP + 2 * index + side for index in range(4)] for group in range(groups) for side in range(2)]

    def exchange(blocks):
        return lax.all_to_all(blocks, "ctx", split_axis=0, concat_axis=0, tiled=True, axis_index_groups=chips)

    x_near, x_far, own_cots = pl.pallas_call(
        rows_of_kernel,
        in_specs=[VMEM_WHOLE] * 2,
        out_specs=[VMEM_WHOLE] * 3,
        out_shape=[half, half, jax.ShapeDtypeStruct((8, cut, width), BFLOAT)],
        compiler_params=BIG,
        cost_estimate=moved(layer_input, layer_input, cotangent, cotangent),
        name="token_rows",
    )(jnp.swapaxes(layer_input, 1, 2), jnp.swapaxes(cotangent, 1, 2))
    inputs = gather_halves((x_near, x_far))

    def columns(weight):
        return jnp.concatenate(
            [lax.dynamic_slice_in_dim(weight, index * slab + chip * part, part, 1) for index in range(depth)], axis=1
        )

    pair_slice = jnp.where(is_zero, columns(gate_weight), columns(up_weight))
    down_slice = lax.dynamic_slice_in_dim(down_weight, chip * part + core * piece, piece, 0)

    packed = pl.pallas_call(
        functools.partial(pack_kernel, size=size, wide=wide),
        in_specs=[SMEM_WHOLE] + [VMEM_WHOLE] * 7,
        out_specs=VMEM_WHOLE,
        out_shape=jax.ShapeDtypeStruct((size + each + 16, 3 * inner), BFLOAT),
        cost_estimate=moved(query_weight, query_weight),
        name="pack",
    )(
        after(place, pair_slice, down_slice), query_weight, key_weight, value_weight, projection, gain_early.reshape(1, shard), gain_late.reshape(1, shard),
        jnp.pad(bias_table, ((0, 8 - buckets), (0, 128 - heads))),
    )
    packed = lax.all_gather(packed, "wsh", axis=0)
    pair_mine = lax.all_gather(after(pair_slice, packed), "wsh", axis=0, tiled=True)
    seg_rows = jnp.pad(segments.astype(BFLOAT), ((0, 16 - seqs), (0, 3 * inner - rows)))
    small = jnp.concatenate((packed[:, : size + each].reshape(-1, 3 * inner), seg_rows), axis=0)
    small = after(small, *inputs[2:6])
    near = gather_relay(small, small.shape[0] // 32 * 16)
    far = swap(near, 1)
    down_mine = lax.all_gather(after(down_slice, near), "wsh", axis=0, tiled=True).reshape(depth, piece, width)
    qkv_full, proj_full, gains, table, segs = pl.pallas_call(
        functools.partial(unpack_kernel, depth=depth, size=size, wide=wide),
        in_specs=[SMEM_WHOLE, VMEM_WHOLE, VMEM_WHOLE, VMEM_WHOLE],
        out_specs=[VMEM_WHOLE] * 5,
        out_shape=[
            jax.ShapeDtypeStruct((width, 3 * inner), BFLOAT),
            jax.ShapeDtypeStruct((inner, width), BFLOAT),
            jax.ShapeDtypeStruct((8, width), FLOAT),
            jax.ShapeDtypeStruct((BUCKETS, 128), FLOAT),
            jax.ShapeDtypeStruct((seqs, GROUP, rows), FLOAT),
        ],
        compiler_params=BIG,
        cost_estimate=moved(near, far, near),
        name="unpack",
    )(place, packed[:, size + each :], near, far)

    def whole(value, axis=0):
        if groups == 1:
            return value
        return lax.all_gather(value, "ctx", axis=axis, tiled=True, axis_index_groups=upper)

    segs = whole(segs, 1)
    bias, mask = attention_terms(meta, table, segs, inner // 128, ring // 2)

    normed, *kv, queries = norm_project(inputs, gains[0:1], qkv_full, inner)
    cots = exchange(own_cots)
    kv = [value.reshape(1, seqs, rows, 2 * inner) for value in kv]
    queries = queries.reshape(seqs, rows, inner)
    kv = [whole(value) for value in (*kv, *[swap(value, 1) for value in kv])]
    attention, lse = attention_forward(meta, bias, mask, queries, kv)
    attn_low = attention.astype(BFLOAT).reshape(tokens, inner)
    attn = gather_direct(attn_low)

    after_attn, normed_late = late_norm(attn, inputs, proj_full, gains[1:2])
    pair_mine = after(pair_mine, attn_low)
    pair_other = swap(pair_mine, 1)
    down_mine = after(down_mine, normed_late)
    down_other = swap(down_mine, 1)
    activation, back_mine, back_other, out_part, *late_part, cot_all = feed_forward(
        spot, normed_late, cots, pair_mine, pair_other, (down_mine, down_other)
    )

    def flat(value):
        return value.reshape(4 * tokens, value.shape[2])

    def over_groups(value):
        return lax.psum(value, "ctx", axis_index_groups=upper) if groups > 1 else value

    late_own, first_near, first_far, second_near, second_far, last_near, last_far = late_part
    low, high = swap(last_near, 4), swap(last_far, 2)
    got_far, got_near = swap(first_far, 2), swap(second_near, 4)
    other_grad, mine_grad = outer_sums(normed_late, (back_other, back_mine))
    first_near, second_far = relay_sums((first_near, low), (second_far, high), mine_grad, got_far, got_near)
    late_parts = (swap(first_near, 2), got_near, got_far, swap(second_far, 4))
    other_got = [swap(other_grad[index : index + 1], 1) for index in range(2)]
    down_whole = outer_sums(activation, (cot_all,))[0]
    down_grad = down_whole.reshape(depth, 2, piece, width)
    down_keep = jnp.where(is_zero, down_grad[:, 0], down_grad[:, 1])
    down_send = jnp.where(is_zero, down_grad[:, 1], down_grad[:, 0])
    down_got = swap(down_send, 1)
    residual_grad, mix_low, attn_grad = middle(
        after_attn, late_own, late_parts, own_cots, gains[1:2], proj_full, down_whole, mine_grad
    )
    attn_grad = attn_grad.reshape(seqs, rows, inner)
    proj_grad = tn(attn_low, jnp.pad(mix_low, ((0, 0), (0, 4 * wide - width)))).astype(BFLOAT)
    dq, *dkv, table_part = attention_backward(meta, bias, mask, queries, kv, attn_grad, attention, lse)

    def owned(value):
        if groups > 1:
            value = lax.psum_scatter(value, "ctx", scatter_dimension=0, tiled=True, axis_index_groups=upper)
        return value.reshape(1, tokens, 2 * inner)

    dkv = [owned(value) for value in dkv]
    dkv_got = [swap(value, 1) for value in dkv[4:]]
    dq = dq.reshape(tokens, inner)
    pair_sum = plus(mine_grad, other_got, mix_low).reshape(width, 2 * piece * depth)
    table_sum = jnp.transpose(jnp.sum(table_part, axis=-1).reshape(heads, BUCKETS)).reshape(depth, buckets, heads)
    table_sum = jnp.pad(table_sum, ((0, 0), (0, 16 - buckets), (0, 128 - heads))).reshape(depth * 16, 128).astype(BFLOAT)
    *dkv_four, keep, send = weight_grads(place, normed, dkv[:4], dkv_got, dq, table_sum, proj_grad, depth, size, wide, pair_sum)
    down_sum = plus(down_keep, [down_got], keep).reshape(depth * piece, width)
    pair_own = over_groups(lax.psum_scatter(pair_sum, "wsh", scatter_dimension=0, tiled=True))
    down_own = over_groups(lax.psum_scatter(down_sum, "wsh", scatter_dimension=0, tiled=True))
    out_parts = exchange(after(out_part, attn_grad)).reshape(4, tokens, width)
    result = output_sum(after_attn, out_parts, seqs)

    blocks = plus_apart(keep, swap(send, 1), result)
    dkv_parts = [swap(dkv_four[index], 2 * index) for index in range(1, 4)]
    input_grad = last(dq, dkv_four[0], dkv_parts, jnp.swapaxes(layer_input, 1, 2), residual_grad, gains[0:1], qkv_full)
    levels = sum_parts([blocks[0]] + [swap(blocks[index], 2 * index) for index in range(1, 4)], input_grad, pair_own)
    pair_near = gather_direct(after(pair_own, levels))
    down_near = gather_direct(after(down_own, levels))
    total = sum_parts(
        [levels[0]] + [swap_depth(levels[gap], gap) for gap in range(1, depth)], *pair_near[1:]
    )
    grads_near = gather_direct(over_groups(total))
    pair_far, down_far = [[swap(value, 1) for value in values] for values in (pair_near, down_near)]
    gate_out, up_out, late_sum = spread(place, pair_near, pair_far, gate_weight, up_weight, depth, part)
    down_out = pl.pallas_call(
        rows_kernel,
        grid=(slab // 128,),
        in_specs=[SMEM_WHOLE] + [once((piece, width))] * 8,
        out_specs=pl.BlockSpec((width, 128), lambda g: (0, g)),
        out_shape=jax.ShapeDtypeStruct((width, slab), FLOAT),
        scratch_shapes=[pltpu.VMEM((slab, width), BFLOAT)],
        compiler_params=BIG,
        cost_estimate=moved(down_own, down_own, down_own),
        name="join_down",
    )(place, *down_near, *down_far)
    grads_near = pl.pallas_call(
        skipping(stack_kernel, 4, 1),
        in_specs=[VMEM_WHOLE] * 4 + [UNREAD],
        out_specs=VMEM_WHOLE,
        out_shape=jax.ShapeDtypeStruct((4, *total.shape), BFLOAT),
        cost_estimate=moved(total, total),
        name="stack_small",
    )(*grads_near, late_sum)
    grads_far = swap(grads_near, 1)
    column = jax.ShapeDtypeStruct((shard, inner), FLOAT)
    query_out, key_out, value_out, proj_out, early_sum, table_rows = pl.pallas_call(
        functools.partial(finish_kernel, size=size, wide=wide),
        in_specs=[SMEM_WHOLE] + [VMEM_WHOLE] * 5,
        out_specs=[VMEM_WHOLE] * 6,
        out_shape=[
            column, column, column, jax.ShapeDtypeStruct((inner // depth, width), FLOAT),
            jax.ShapeDtypeStruct((shard, 128), FLOAT), jax.ShapeDtypeStruct((16, 128), FLOAT),
        ],
        compiler_params=BIG,
        cost_estimate=moved(grads_near, grads_far, grads_near),
        name="finish_small",
    )(place, grads_near, grads_far, query_weight, key_weight, value_weight)

    return (
        jnp.swapaxes(result, 1, 2),
        jnp.swapaxes(input_grad, 1, 2),
        query_out,
        key_out,
        value_out,
        proj_out,
        gate_out,
        up_out,
        jnp.transpose(down_out),
        early_sum[:, 0] / gain_early.astype(FLOAT),
        late_sum[:, 0] / gain_late.astype(FLOAT),
        table_rows[:buckets, :heads],
    )


def solution(mesh):
    rows = P("wsh", "ctx", None)
    split = P("wsh", None)
    vector = P("wsh")
    return jax.shard_map(
        on_device,
        mesh=mesh,
        in_specs=(rows, P("wsh", "ctx"), rows, split, split, split, split, split, split, split, vector, vector, split),
        out_specs=(rows, rows, split, split, split, split, split, split, split, vector, vector, split),
        check_vma=False,
    )
```

```python
import functools

import jax
import jax.numpy as jnp
import numpy as np
from jax import lax
from jax.experimental import pallas as pl
from jax.experimental.pallas import tpu as pltpu
from jax.sharding import PartitionSpec as P

BUCKETS = 32
GROUP = 8
EPSILON = 1e-06
NEGATIVE = -1e30
PRECISE = lax.Precision.HIGHEST
BUCKET_EDGES = (12, 16, 23, 32, 46, 64, 91)
FLOAT = jnp.float32
BFLOAT = jnp.bfloat16


SCALE = 0.2


def cost(flops, bytes_accessed, transcendentals):
    return pl.CostEstimate(
        flops=int(SCALE * flops), bytes_accessed=int(SCALE * bytes_accessed), transcendentals=int(SCALE * transcendentals)
    )


def bucket_number(offset):
    distance = abs(offset)
    level = distance if distance < 8 else 8 + sum(distance >= edge for edge in BUCKET_EDGES)
    return level + (16 if offset > 0 else 0)


def bucket_of(offsets):
    distance = jnp.abs(offsets)
    coarse = 8 + sum(((distance >= boundary).astype(jnp.int32) for boundary in BUCKET_EDGES))
    level = jnp.where(distance < 8, distance, coarse)
    return level + jnp.where(offsets > 0, 16, 0)


def near_radius(rows):
    return -(-(BUCKET_EDGES[-1] - 1) // rows)


def tile_offsets(block_gap, rows):
    keys = lax.broadcasted_iota(jnp.int32, (rows, rows), 0)
    queries = lax.broadcasted_iota(jnp.int32, (rows, rows), 1)
    return block_gap * rows + keys - queries


def tile_buckets(block_gap, rows):
    low, high = block_gap * rows - (rows - 1), block_gap * rows + (rows - 1)
    return sorted({bucket_number(offset) for offset in range(low, high + 1)})


def nt(left, right):
    return lax.dot_general(left, right, (((1,), (1,)), ((), ())), preferred_element_type=FLOAT)


def tn(left, right):
    return lax.dot_general(left, right, (((0,), (0,)), ((), ())), preferred_element_type=FLOAT)


def block_number(meta, half, position, count):
    low = lax.rem(meta, GROUP)
    part, group = divmod(position, count // 4)
    return group * GROUP + lax.bitwise_xor(low, jnp.int32(2 * part + half))


def tile_index(meta, half, position, count, radius):
    gap = block_number(meta, half, position, count) - meta
    return jnp.clip(gap, -(radius + 1), radius + 1) + radius + 1


def build_bias(bias_ref, table_ref, pair, rows, radius):
    for side, bucket in ((0, 15), (2 * radius + 2, 31)):
        for head in range(2):
            bias_ref[pair, head, side] = jnp.full((rows, rows), table_ref[bucket, 2 * pair + head], FLOAT)
    for gap in range(-radius, radius + 1):
        buckets = bucket_of(tile_offsets(gap, rows))
        present = tile_buckets(gap, rows)
        tiles = [jnp.full((rows, rows), table_ref[present[0], 2 * pair + head], FLOAT) for head in range(2)]
        for bucket in present[1:]:
            hit = buckets == bucket
            tiles = [jnp.where(hit, table_ref[bucket, 2 * pair + head], tiles[head]) for head in range(2)]
        for head in range(2):
            bias_ref[pair, head, gap + radius + 1] = tiles[head]


def build_mask(mask_ref, segs_ref, meta, seq, rows, count):
    own = segs_ref[seq, pl.ds(meta, 1), :]
    for half in range(2):
        for position in range(count):
            row = segs_ref[seq, pl.ds(block_number(meta, half, position, count), 1), :]
            keys = jnp.transpose(jnp.broadcast_to(row, (rows, rows)))
            mask_ref[seq, half * count + position] = jnp.where(keys == own, 0.0, NEGATIVE)


def half_scores(keys, query, meta, head, half, seq, bias_ref, mask_ref, rows, count, radius):
    raw = nt(keys, query)
    parts = []
    for position in range(count):
        extra = bias_ref[0, head, tile_index(meta, half, position, count, radius)]
        masked = mask_ref[0, half * count + position]
        parts.append(raw[position * rows : (position + 1) * rows] + (extra + masked))
    return jnp.concatenate(parts, axis=0)


def joined(refs):
    return jnp.concatenate([ref[...].reshape(-1, ref.shape[-1]) for ref in refs], axis=0)


def head_rows(value, head, lane):
    return jnp.where((lane < 64) == (head == 0), value, jnp.zeros_like(value))


def forward_kernel(
    meta_ref, bias_ref, mask_ref, q_ref, *refs, rows, count, radius,
):
    key_refs, value_refs, (out_ref, lse_ref) = refs[:8], refs[8:16], refs[16:]
    pair, seq = pl.program_id(0), pl.program_id(1)
    meta = meta_ref[0]

    query = q_ref[0]
    lane = lax.broadcasted_iota(jnp.int32, query.shape, 1)
    keys = [joined(key_refs[:4]), joined(key_refs[4:])]
    values = [joined(value_refs[:4]), joined(value_refs[4:])]
    pieces = []
    for head in range(2):
        one = head_rows(query, head, lane)
        scores = [
            half_scores(keys[half], one, meta, head, half, seq, bias_ref, mask_ref, rows, count, radius)
            for half in range(2)
        ]
        top = jnp.maximum(jnp.max(scores[0], axis=0, keepdims=True), jnp.max(scores[1], axis=0, keepdims=True))
        raised = [jnp.exp(part - top) for part in scores]
        total = jnp.sum(raised[0], axis=0, keepdims=True) + jnp.sum(raised[1], axis=0, keepdims=True)
        scale = 1.0 / total
        mixed = sum(tn(values[half], (raised[half] * scale).astype(BFLOAT)) for half in range(2))
        pieces.append(mixed[64 * head : 64 * head + 64])
        lse_ref[0, 0, head : head + 1] = top + jnp.log(total)
    out_ref[0] = jnp.transpose(jnp.concatenate(pieces, axis=0))


def backward_kernel(
    meta_ref, bias_ref, mask_ref, q_ref, *refs, rows, count, radius,
):
    key_refs, value_refs, (do_ref, out_ref, lse_ref, dq_ref) = refs[:8], refs[8:16], refs[16:20]
    both_refs, (tab_ref, sum_ref) = refs[20:28], refs[28:]
    pair, seq = pl.program_id(0), pl.program_id(1)
    meta = meta_ref[0]

    @pl.when(seq == 0)
    def _():
        sum_ref[...] = jnp.zeros_like(sum_ref)

    query, grad = q_ref[0], do_ref[0]
    lane = lax.broadcasted_iota(jnp.int32, query.shape, 1)
    keys = [joined(key_refs[:4]), joined(key_refs[4:])]
    values = [joined(value_refs[:4]), joined(value_refs[4:])]
    picks = (
        lax.broadcasted_iota(jnp.int32, (8, 128), 1) // 64 == lax.broadcasted_iota(jnp.int32, (8, 128), 0)
    ).astype(FLOAT)
    deltas = lax.dot_general(
        picks, grad.astype(FLOAT) * out_ref[0], (((1,), (1,)), ((), ())), precision=PRECISE, preferred_element_type=FLOAT
    )
    query_heads = [head_rows(query, head, lane) for head in range(2)]
    grad_heads = [head_rows(grad, head, lane) for head in range(2)]
    probs, slopes = [[], []], [[], []]
    pieces = []
    for head in range(2):
        logsum = lse_ref[0, 0, head : head + 1]
        delta = deltas[head : head + 1]
        flow = None
        for half in range(2):
            scores = half_scores(
                keys[half], query_heads[head], meta, head, half, seq, bias_ref, mask_ref, rows, count, radius
            )
            prob = jnp.exp(scores - logsum)
            slope = prob * (nt(values[half], grad_heads[head]) - delta)
            for position in range(count):
                index = tile_index(meta, half, position, count, radius)
                sum_ref[head, index] = sum_ref[head, index] + slope[position * rows : (position + 1) * rows]
            slope_low = slope.astype(BFLOAT)
            probs[half].append(prob.astype(BFLOAT))
            slopes[half].append(slope_low)
            term = tn(keys[half], slope_low)
            flow = term if flow is None else flow + term
        pieces.append(flow[64 * head : 64 * head + 64])
    dq_ref[0] = jnp.transpose(jnp.concatenate(pieces, axis=0)).astype(BFLOAT)
    query_stack = jnp.concatenate(query_heads, axis=0)
    grad_stack = jnp.concatenate(grad_heads, axis=0)
    for half in range(2):
        dk = jnp.dot(jnp.concatenate(slopes[half], axis=1), query_stack, preferred_element_type=FLOAT)
        dv = jnp.dot(jnp.concatenate(probs[half], axis=1), grad_stack, preferred_element_type=FLOAT)
        dk = dk.astype(BFLOAT).reshape(count, 1, rows, 128)
        dv = dv.astype(BFLOAT).reshape(count, 1, rows, 128)
        for part, both_ref in enumerate(both_refs[4 * half : 4 * half + 4]):
            side = slice(part * count // 4, (part + 1) * count // 4)
            both_ref[:, :, :, :128] = dk[side]
            both_ref[:, :, :, 128:] = dv[side]

    @pl.when(seq == pl.num_programs(1) - 1)
    def _():
        for head in range(2):
            sums = {}
            for side, bucket in ((0, 15), (2 * radius + 2, 31)):
                sums[bucket] = jnp.sum(sum_ref[head, side], axis=0, keepdims=True)
            for gap in range(-radius, radius + 1):
                buckets = bucket_of(tile_offsets(gap, rows))
                tile = sum_ref[head, gap + radius + 1]
                for bucket in tile_buckets(gap, rows):
                    part = jnp.sum(jnp.where(buckets == bucket, tile, 0.0), axis=0, keepdims=True)
                    sums[bucket] = sums[bucket] + part if bucket in sums else part
            for bucket in range(BUCKETS):
                tab_ref[0, head, bucket : bucket + 1] = sums.get(bucket, jnp.zeros((1, rows), FLOAT))


def prepare_kernel(meta_ref, table_ref, segs_ref, bias_ref, mask_ref, *, rows, count, radius):
    for pair in range(bias_ref.shape[0]):
        build_bias(bias_ref, table_ref, pair, rows, radius)
    for seq in range(mask_ref.shape[0]):
        build_mask(mask_ref, segs_ref, meta_ref[0], seq, rows, count)


def attention_terms(meta, table, segs, pairs, count):
    seqs, _, rows = segs.shape
    radius = near_radius(rows)
    return pl.pallas_call(
        functools.partial(prepare_kernel, rows=rows, count=count, radius=radius),
        in_specs=[pl.BlockSpec(memory_space=pltpu.SMEM)] * 2 + [pl.BlockSpec(memory_space=pltpu.VMEM)],
        out_specs=[pl.BlockSpec(memory_space=pltpu.VMEM)] * 2,
        out_shape=[
            jax.ShapeDtypeStruct((pairs, 2, 2 * radius + 3, rows, rows), FLOAT),
            jax.ShapeDtypeStruct((seqs, 2 * count, rows, rows), FLOAT),
        ],
        cost_estimate=cost(flops=0, bytes_accessed=10**6, transcendentals=0),
        name="attention_terms",
    )(meta, table, segs)


def attention_specs(bias, mask, rows, count):
    small = [
        pl.BlockSpec(memory_space=pltpu.SMEM),
        pl.BlockSpec((1, *bias.shape[1:]), lambda p, s: (p, 0, 0, 0, 0)),
        pl.BlockSpec((1, *mask.shape[1:]), lambda p, s: (s, 0, 0, 0)),
    ]
    query = pl.BlockSpec((1, rows, 128), lambda p, s: (s, 0, p))
    key = pl.BlockSpec((count // 4, 1, rows, 128), lambda p, s: (0, s, 0, 2 * p))
    value = pl.BlockSpec((count // 4, 1, rows, 128), lambda p, s: (0, s, 0, 2 * p + 1))
    stat = pl.BlockSpec((1, 1, 8, rows), lambda p, s: (p, s, 0, 0))
    return small, query, key, value, stat


def attention_cost(seqs, rows, keys, width, products):
    return cost(
        flops=2 * products * seqs * rows * keys * width,
        bytes_accessed=4 * seqs * keys * width * products,
        transcendentals=seqs * rows * keys * width // 64,
    )


def attention_forward(meta, bias, mask, queries, kv):
    seqs, rows, inner = queries.shape
    count, blocks, pairs = 4 * kv[0].shape[0], mask.shape[1], inner // 128
    radius = near_radius(rows)
    small, query, key, value, stat = attention_specs(bias, mask, rows, count)
    return pl.pallas_call(
        functools.partial(forward_kernel, rows=rows, count=count, radius=radius),
        grid=(pairs, seqs),
        in_specs=[*small, query, *[key] * 8, *[value] * 8],
        out_specs=[query, stat],
        out_shape=[
            jax.ShapeDtypeStruct((seqs, rows, inner), FLOAT),
            jax.ShapeDtypeStruct((pairs, seqs, 8, rows), FLOAT),
        ],
        cost_estimate=attention_cost(seqs, rows, blocks * rows, inner, 2),
        name="attention_forward",
    )(meta, bias, mask, queries, *kv, *kv)


def attention_backward(meta, bias, mask, queries, kv, grad, out, lse, *deps):
    seqs, rows, inner = queries.shape
    count, blocks, pairs = 4 * kv[0].shape[0], mask.shape[1], inner // 128
    radius = near_radius(rows)
    small, query, key, value, stat = attention_specs(bias, mask, rows, count)
    side = jax.ShapeDtypeStruct((count // 4, seqs, rows, 2 * inner), BFLOAT)
    both = pl.BlockSpec((count // 4, 1, rows, 256), lambda p, s: (0, s, 0, p))
    return pl.pallas_call(
        skipping(functools.partial(backward_kernel, rows=rows, count=count, radius=radius), 23, len(deps)),
        grid=(pairs, seqs),
        in_specs=[*small, query, *[key] * 8, *[value] * 8, query, query, stat] + [UNREAD] * len(deps),
        out_specs=[query, *[both] * 8, pl.BlockSpec((1, 2, BUCKETS, rows), lambda p, s: (p, 0, 0, 0))],
        out_shape=[
            jax.ShapeDtypeStruct((seqs, rows, inner), BFLOAT), *[side] * 8,
            jax.ShapeDtypeStruct((pairs, 2, BUCKETS, rows), FLOAT),
        ],
        scratch_shapes=[
            pltpu.VMEM((2, 2 * radius + 3, rows, rows), FLOAT),
        ],
        cost_estimate=attention_cost(seqs, rows, blocks * rows, inner, 5),
        name="attention_backward",
    )(meta, bias, mask, queries, *kv, *kv, grad, out, lse, *deps)


def swap(value, bit):
    count = lax.axis_size("ctx")
    return lax.ppermute(value, "ctx", [(source, source ^ bit) for source in range(count)])


def swap_depth(value, bit):
    count = lax.axis_size("wsh")
    return lax.ppermute(value, "wsh", [(source, source ^ bit) for source in range(count)])


def after(value, *others):
    return lax.optimization_barrier((value, *others))[0]


def gather_halves(own):
    near, far = own
    first_near, second_far = swap(near, 2), swap(far, 4)
    first_far, second_near = swap(far, 2), swap(near, 4)
    return [near, far, first_near, first_far, second_near, second_far, swap(first_near, 4), swap(second_far, 2)]


def gather_direct(own):
    return [own, swap(own, 2), swap(own, 4), swap(own, 6)]


def gather_relay(own, cut):
    first, second = swap(own, 2), swap(own, 4)
    return jnp.stack((own, first, second, jnp.concatenate((swap(first[:cut], 4), swap(second[cut:], 2)), axis=0)))


VMEM_WHOLE = pl.BlockSpec(memory_space=pltpu.VMEM)
UNREAD = pl.BlockSpec(memory_space=pl.ANY)


def skipping(kernel, inputs, count):
    return lambda *refs: kernel(*refs[:inputs], *refs[inputs + count :])


SMEM_WHOLE = pl.BlockSpec(memory_space=pltpu.SMEM)
BIG = pltpu.CompilerParams(vmem_limit_bytes=60 * 1024 * 1024)


def moved(*arrays):
    return cost(
        flops=0, bytes_accessed=sum(int(np.prod(array.shape)) * array.dtype.itemsize for array in arrays), transcendentals=0
    )


def slice_size(total):
    return -(-total // (GROUP * 16)) * 16


def slice_start(index, total, size):
    return jnp.minimum(index * size, total - size)


def column_cut(width):
    return -(-width // 512) * 128


def pack_kernel(place_ref, q_ref, k_ref, v_ref, proj_ref, early_ref, late_ref, table_ref, out_ref, *, size, wide):
    low = place_ref[0]
    chip, core = low // 2, lax.rem(low, 2)
    inner = q_ref.shape[1]
    shard = q_ref.shape[0]
    start = pl.multiple_of(slice_start(low, shard, size), 16)
    out_ref[:size, :inner] = q_ref[pl.ds(start, size), :]
    for index, ref in enumerate((k_ref, v_ref)):
        rows = ref[pl.ds(start, size), :]
        for pair in range(inner // 128):
            base = inner + 256 * pair + 128 * index
            out_ref[:size, base : base + 128] = rows[:, 128 * pair : 128 * pair + 128]
    part = proj_ref.shape[0] // 2
    each = part // 3
    out_ref[size:, :] = jnp.zeros((out_ref.shape[0] - size, out_ref.shape[1]), BFLOAT)
    for column in range(4):
        reach = min(wide, proj_ref.shape[1] - column * wide)

        @pl.when(chip == column)
        def _(column=column, reach=reach):
            for lane in range(3):
                row = pl.multiple_of(core * part + lane * each, 16)
                out_ref[size : size + each, lane * wide : lane * wide + reach] = proj_ref[
                    pl.ds(row, each), column * wide : column * wide + reach
                ]

    base = size + each
    out_ref[base : base + 1, :shard] = early_ref[...]
    out_ref[base + 1 : base + 2, :shard] = late_ref[...]
    out_ref[base + 8 : base + 16, :128] = table_ref[...]


def unpack_kernel(place_ref, misc_ref, near_ref, far_ref, qkv_ref, proj_ref, gains_ref, table_ref, segs_ref, *, depth, size, wide):
    low = place_ref[0]
    shard, part = qkv_ref.shape[0] // depth, proj_ref.shape[0] // depth // 2
    each = part // 3
    span = size + each
    buckets = table_ref.shape[0] // depth
    for level in range(depth):
        rows = misc_ref[level].astype(FLOAT)
        gains_ref[:, level * shard : (level + 1) * shard] = rows[:8, :shard]
        table_ref[level * buckets : (level + 1) * buckets, :] = rows[8 : 8 + buckets, :128]
    seqs, _, rows = segs_ref.shape
    for index in range(GROUP):
        gap = lax.bitwise_xor(low, jnp.int32(index))
        slot, odd = gap // 2, lax.rem(gap, 2)
        block = jnp.where(odd == 0, near_ref[slot], far_ref[slot])
        for level in range(depth):
            base = level * shard + min(index * size, shard - size)
            qkv_ref[base : base + size, :] = block[level * span : level * span + size]
            column = (index // 2) * wide
            reach = min(wide, proj_ref.shape[1] - column)
            for lane in range(3):
                base = (level * 2 + index % 2) * part + lane * each
                proj_ref[base : base + each, column : column + reach] = block[
                    level * span + size : level * span + span, lane * wide : lane * wide + reach
                ]
        own = block[depth * span : depth * span + 16, :128].astype(FLOAT)
        for seq in range(seqs):
            segs_ref[seq, index : index + 1, :] = own[seq : seq + 1, :rows]


def grad_kernel(
    place_ref, normed_ref, *refs, depth, size, wide
):
    owns, gots, (dq_ref, table_ref, proj_ref) = refs[:4], refs[4:8], refs[8:11]
    sums, (keep_ref, send_ref, kv_scr, q_scr, t_scr) = refs[11:15], refs[15:]
    step = pl.program_id(0)
    tokens = dq_ref.shape[0]
    for index in range(4):

        @pl.when(step == index // 2)
        def _(index=index):
            total = (owns[index][0].astype(FLOAT) + gots[index][0].astype(FLOAT)).astype(BFLOAT)
            t_scr[index % 2 * tokens : (index % 2 + 1) * tokens, :] = total
            sums[index][...] = total

    turned = jnp.transpose(normed_ref[...].reshape(2 * tokens, normed_ref.shape[2]))
    product = jnp.dot(turned, t_scr[...], preferred_element_type=FLOAT)

    @pl.when(step == 0)
    def _():
        kv_scr[...] = product
        q_scr[...] = jnp.dot(turned[:, :tokens], dq_ref[...], preferred_element_type=FLOAT).astype(BFLOAT)

    @pl.when(step == 1)
    def _():
        kv_scr[...] = kv_scr[...] + product
        low = place_ref[0]
        zed = place_ref[1]
        inner = q_scr.shape[1]
        shard = q_scr.shape[0] // depth
        for index in range(GROUP):
            target = lax.bitwise_xor(low, jnp.int32(index))
            out_ref = keep_ref if index % 2 == 0 else send_ref
            for gap in range(depth):
                level = lax.bitwise_xor(zed, jnp.int32(gap))
                start = pl.multiple_of(level * shard + slice_start(target, shard, size), 16)
                out_ref[index // 2, gap, :size, :inner] = q_scr[pl.ds(start, size), :]
                out_ref[index // 2, gap, :size, inner:] = kv_scr[pl.ds(start, size), :].astype(BFLOAT)
                part = proj_ref.shape[0] // depth // 2
                each = part // 3
                column = pl.multiple_of((target // 2) * wide, 128)
                for lane in range(3):
                    row = pl.multiple_of((level * 2 + lax.rem(target, 2)) * part + lane * each, 16)
                    out_ref[index // 2, gap, size:, lane * wide : (lane + 1) * wide] = proj_ref[
                        pl.ds(row, each), pl.ds(column, wide)
                    ]
                last = target == GROUP - 1
                rows = table_ref[pl.ds(pl.multiple_of(level * 16, 16), 16), :]
                out_ref[index // 2, gap, :16, :128] = jnp.where(last, rows, out_ref[index // 2, gap, :16, :128])


def weight_grads(place, normed, own, got, dq, table, proj, depth, size, wide, *deps):
    _, tokens, width = normed.shape
    inner = dq.shape[1]
    block = once((1, tokens, 2 * inner))
    summed = pl.BlockSpec((tokens, 2 * inner), lambda g: (0, 0))
    span = size + proj.shape[0] // depth // 6
    piece = jax.ShapeDtypeStruct((4, depth, span, 3 * inner), BFLOAT)
    kept = pl.BlockSpec((4, depth, span, 3 * inner), lambda g: (0, 0, 0, 0))
    return pl.pallas_call(
        skipping(functools.partial(grad_kernel, depth=depth, size=size, wide=wide), 13, len(deps)),
        grid=(2,),
        in_specs=[
            SMEM_WHOLE, pl.BlockSpec((2, tokens, width), lambda g: (g, 0, 0)), *[block] * 8, once(dq.shape), once(table.shape),
            once(proj.shape),
        ]
        + [UNREAD] * len(deps),
        out_specs=[*[summed] * 4, kept, kept],
        out_shape=[*[jax.ShapeDtypeStruct((tokens, 2 * inner), BFLOAT)] * 4, piece, piece],
        scratch_shapes=[
            pltpu.VMEM((width, 2 * inner), FLOAT), pltpu.VMEM((width, inner), BFLOAT), pltpu.VMEM((2 * tokens, 2 * inner), BFLOAT),
        ],
        compiler_params=BIG,
        cost_estimate=cost(flops=18 * tokens * width * inner, bytes_accessed=12 * tokens * width, transcendentals=0),
        name="weight_grads",
    )(place, normed, *own, *got, dq, table, proj, *deps)


def pick_block(refs, step, scratch_ref):
    cut = refs[0].shape[0]
    for index in range(4):

        @pl.when(step == index)
        def _(index=index):
            scratch_ref[:cut] = refs[2 * index][...]
            scratch_ref[cut:] = refs[2 * index + 1][...]


def pick_whole(refs, step, scratch_ref):
    for index in range(4):

        @pl.when(step == index)
        def _(index=index):
            scratch_ref[...] = refs[index][...]


def once(shape):
    return pl.BlockSpec(shape, lambda g, *_: (0,) * len(shape), pipeline_mode=pl.Buffered(1))


def norm_kernel(*refs, inner):
    pieces, (gain_ref, weight_ref, normed_ref, k0, k1, k2, k3, q_ref, x_scr) = refs[:8], refs[8:]
    step = pl.program_id(0)
    pick_block(pieces, step, x_scr)
    hidden = x_scr[...].astype(FLOAT)
    scale = lax.rsqrt(jnp.mean(hidden * hidden, axis=-1, keepdims=True) + EPSILON)
    normed = (hidden * scale * gain_ref[...]).astype(BFLOAT)
    normed_ref[0] = normed
    both = jnp.dot(normed, weight_ref[:, inner:], preferred_element_type=FLOAT).astype(BFLOAT)

    for index, kv_ref in enumerate((k0, k1, k2, k3)):

        @pl.when(step == index)
        def _(kv_ref=kv_ref):
            kv_ref[0] = both

    @pl.when(step == 0)
    def _():
        q_ref[...] = jnp.dot(normed, weight_ref[:, :inner], preferred_element_type=FLOAT).astype(BFLOAT)


def norm_project(pieces, gain, weight, inner):
    tokens, width = 2 * pieces[0].shape[0], pieces[0].shape[1]
    return pl.pallas_call(
        functools.partial(norm_kernel, inner=inner),
        grid=(4,),
        in_specs=[*[once(piece.shape) for piece in pieces], once(gain.shape), once(weight.shape)],
        out_specs=[
            pl.BlockSpec((1, tokens, width), lambda g: (g, 0, 0)),
            *[pl.BlockSpec((1, tokens, 2 * inner), lambda g: (0, 0, 0))] * 4,
            pl.BlockSpec((tokens, inner), lambda g: (0, 0)),
        ],
        out_shape=[
            jax.ShapeDtypeStruct((4, tokens, width), BFLOAT),
            *[jax.ShapeDtypeStruct((1, tokens, 2 * inner), BFLOAT)] * 4,
            jax.ShapeDtypeStruct((tokens, inner), BFLOAT),
        ],
        scratch_shapes=[pltpu.VMEM((tokens, width), BFLOAT)],
        compiler_params=BIG,
        cost_estimate=cost(
            flops=18 * tokens * width * inner, bytes_accessed=18 * tokens * width, transcendentals=0
        ),
        name="norm_project",
    )(*pieces, gain, weight)


GELU_SCALE = float(np.sqrt(2.0 / np.pi))


def late_kernel(*refs):
    attn, inputs = refs[:4], refs[4:12]
    proj_ref, gain_ref, after_ref, normed_ref, a_scr, x_scr = refs[12:]
    step = pl.program_id(0)
    pick_whole(attn, step, a_scr)
    pick_block(inputs, step, x_scr)
    after_attn = x_scr[...].astype(FLOAT) + jnp.dot(a_scr[...], proj_ref[...], preferred_element_type=FLOAT)

    @pl.when(step == 0)
    def _():
        after_ref[...] = after_attn

    scale = lax.rsqrt(jnp.mean(after_attn * after_attn, axis=-1, keepdims=True) + EPSILON)
    normed_ref[0] = (after_attn * scale * gain_ref[...]).astype(BFLOAT)


def late_norm(attn, inputs, proj, gain):
    tokens, inner = attn[0].shape
    width = proj.shape[1]
    return pl.pallas_call(
        late_kernel,
        grid=(4,),
        in_specs=[once(value.shape) for value in (*attn, *inputs, proj, gain)],
        out_specs=[
            pl.BlockSpec((tokens, width), lambda g: (0, 0)), pl.BlockSpec((1, tokens, width), lambda g: (g, 0, 0)),
        ],
        out_shape=[
            jax.ShapeDtypeStruct((tokens, width), FLOAT), jax.ShapeDtypeStruct((4, tokens, width), BFLOAT),
        ],
        scratch_shapes=[pltpu.VMEM((tokens, inner), BFLOAT), pltpu.VMEM((tokens, width), BFLOAT)],
        compiler_params=BIG,
        cost_estimate=cost(flops=8 * tokens * width * inner, bytes_accessed=24 * tokens * width, transcendentals=0),
        name="late_norm",
    )(*attn, *inputs, proj, gain)


def feed_kernel(
    spot_ref, normed_ref, cots_ref, mine_ref, other_ref, down_mine, down_other,
    act_ref, dmine_ref, dother_ref, out_ref, l0, *refs
):
    late_refs, (cot_ref, down_ref) = refs[:6], refs[6:]
    is_zero = spot_ref[0] == 0
    tokens = normed_ref.shape[1]

    @pl.when(pl.program_id(0) == 0)
    def _():
        depth, piece, _ = down_mine.shape
        for level in range(depth):
            first = jnp.where(is_zero, down_mine[level], down_other[level])
            second = jnp.where(is_zero, down_other[level], down_mine[level])
            down_ref[2 * level * piece : (2 * level + 1) * piece, :] = first
            down_ref[(2 * level + 1) * piece : (2 * level + 2) * piece, :] = second

    cot = cots_ref[...].reshape(tokens, cots_ref.shape[2])
    cot_ref[0] = cot
    normed = normed_ref[0]
    pre_mine = jnp.dot(normed, mine_ref[...], preferred_element_type=FLOAT)
    pre_other = jnp.dot(normed, other_ref[...], preferred_element_type=FLOAT)
    gate = jnp.where(is_zero, pre_mine, pre_other)
    up = jnp.where(is_zero, pre_other, pre_mine)
    square = gate * gate
    lifted = jnp.tanh(GELU_SCALE * (gate + 0.044715 * gate * square))
    gate_half = 0.5 * (1.0 + lifted)
    smooth = gate * gate_half
    act = (smooth * up).astype(BFLOAT)
    act_ref[0] = act
    out = jnp.dot(act, down_ref[...], preferred_element_type=FLOAT).astype(BFLOAT)
    out_ref[...] = out.reshape(out_ref.shape)
    act_back = nt(cot, down_ref[...])
    slope = gate_half + 0.5 * gate * (1.0 - lifted * lifted) * (GELU_SCALE * (1.0 + 3 * 0.044715 * square))
    gate_back = act_back * up * slope
    up_back = act_back * smooth
    dmine = jnp.where(is_zero, gate_back, up_back).astype(BFLOAT)
    dother = jnp.where(is_zero, up_back, gate_back).astype(BFLOAT)
    dmine_ref[0] = dmine
    dother_ref[0] = dother
    late = (nt(dmine, mine_ref[...]) + nt(dother, other_ref[...])).astype(BFLOAT)
    half = late.shape[0] // 2

    @pl.when(pl.program_id(0) == 0)
    def _():
        l0[...] = late.reshape(l0.shape)

    for index in range(3):

        @pl.when(pl.program_id(0) == index + 1)
        def _(index=index):
            late_refs[2 * index][...] = late[:half]
            late_refs[2 * index + 1][...] = late[half:]


def feed_forward(spot, normed, cots, mine, other, downs):
    _, tokens, width = normed.shape
    wide = mine.shape[1]

    def block(size):
        return pl.BlockSpec((1, tokens, size), lambda g, spot: (g, 0, 0))

    def shape(size):
        return jax.ShapeDtypeStruct((4, tokens, size), BFLOAT)

    placed = pl.BlockSpec((2, tokens // 2, width), lambda g, spot: (lax.bitwise_xor(g, spot[1]), 0, 0))
    sent = jax.ShapeDtypeStruct((8, tokens // 2, width), BFLOAT)
    half = jax.ShapeDtypeStruct((2, tokens // 2, width), BFLOAT)
    piece = pl.BlockSpec((2, tokens // 2, width), lambda g, spot: (0, 0, 0))
    rows = jax.ShapeDtypeStruct((tokens // 2, width), BFLOAT)
    part = pl.BlockSpec((tokens // 2, width), lambda g, spot: (0, 0))
    return pl.pallas_call(
        feed_kernel,
        grid_spec=pltpu.PrefetchScalarGridSpec(
            num_scalar_prefetch=1,
            grid=(4,),
            in_specs=[block(width), placed, *[once(value.shape) for value in (mine, other, *downs)]],
            out_specs=[block(wide), block(wide), block(wide), placed, piece, *[part] * 6, block(width)],
            scratch_shapes=[pltpu.VMEM((wide, width), BFLOAT)],
        ),
        out_shape=[shape(wide), shape(wide), shape(wide), sent, half, *[rows] * 6, shape(width)],
        compiler_params=BIG,
        cost_estimate=cost(
            flops=48 * tokens * width * wide, bytes_accessed=30 * tokens * width, transcendentals=4 * tokens * wide
        ),
        name="feed_forward",
    )(spot, normed, cots, mine, other, *downs)


def outer_kernel(left_ref, *refs):
    count = len(refs) // 3
    rights, outs, scratch = refs[:count], refs[count : 2 * count], refs[2 * count :]
    step = pl.program_id(0)

    def rows(ref):
        return ref[...].reshape(-1, ref.shape[2])

    left = jnp.transpose(rows(left_ref))
    for right_ref, out_ref, acc_ref in zip(rights, outs, scratch):
        part = jnp.dot(left, rows(right_ref), preferred_element_type=FLOAT).reshape(out_ref.shape)

        @pl.when(step == 0)
        def _(acc_ref=acc_ref, part=part):
            acc_ref[...] = part

        @pl.when(step == 1)
        def _(acc_ref=acc_ref, out_ref=out_ref, part=part):
            out_ref[...] = (acc_ref[...] + part).astype(BFLOAT)


def outer_sums(left, rights):
    _, tokens, width = left.shape
    shapes = [(2, width // 2, right.shape[2]) for right in rights]
    return pl.pallas_call(
        outer_kernel,
        grid=(2,),
        in_specs=[pl.BlockSpec((2, tokens, value.shape[2]), lambda g: (g, 0, 0)) for value in (left, *rights)],
        out_specs=[pl.BlockSpec(shape, lambda g: (0, 0, 0)) for shape in shapes],
        out_shape=[jax.ShapeDtypeStruct(shape, BFLOAT) for shape in shapes],
        scratch_shapes=[pltpu.VMEM(shape, FLOAT) for shape in shapes],
        compiler_params=BIG,
        cost_estimate=cost(flops=16 * tokens * width * sum(shape[2] for shape in shapes), bytes_accessed=0, transcendentals=0),
        name="outer_sums",
    )(left, *rights)


def norm_back(hidden, gain, back):
    scale = lax.rsqrt(jnp.mean(hidden * hidden, axis=-1, keepdims=True) + EPSILON)
    lifted = back * gain
    return scale * lifted - hidden * (scale * scale * scale) * jnp.mean(lifted * hidden, axis=-1, keepdims=True)


def quarter_specs(tile, width):
    whole = pl.BlockSpec((tile, width), lambda g: (g, 0))
    near = pl.BlockSpec((tile, width), lambda g: (jnp.minimum(g, 1), 0))
    far = pl.BlockSpec((tile, width), lambda g: (jnp.maximum(g - 2, 0), 0))
    return whole, [near, near, far, far]


def summed(own_ref, parts):
    near = pl.program_id(0) < 2
    first = jnp.where(near, parts[0][...], parts[2][...]).astype(FLOAT)
    second = jnp.where(near, parts[1][...], parts[3][...]).astype(FLOAT)
    return own_ref[...].astype(FLOAT) + first + second


def middle_kernel(after_ref, own_ref, n0, n1, f0, f1, cot_ref, gain_ref, proj_ref, residual_ref, mix_ref, attn_ref):
    near = pl.program_id(0) < 2
    back = own_ref[0].astype(FLOAT) + jnp.where(near, n0[...], f0[...]).astype(FLOAT)
    back = back + jnp.where(near, n1[...], f1[...]).astype(FLOAT)
    residual = cot_ref[0].astype(FLOAT) + norm_back(after_ref[...], gain_ref[...], back)
    residual_ref[...] = residual
    mix = residual.astype(BFLOAT)
    mix_ref[...] = mix
    attn_ref[...] = nt(mix, proj_ref[...]).astype(BFLOAT)


def middle(after_attn, own, parts, cots, gain, proj, *deps):
    tokens, width = after_attn.shape
    inner = proj.shape[0]
    tile = tokens // 4
    whole = pl.BlockSpec((tile, width), lambda g: (g, 0))
    half = pl.BlockSpec((1, tile, width), lambda g: (g // 2, g % 2, 0))
    near = pl.BlockSpec((tile, width), lambda g: (jnp.minimum(g, 1), 0))
    far = pl.BlockSpec((tile, width), lambda g: (jnp.maximum(g - 2, 0), 0))
    return pl.pallas_call(
        skipping(middle_kernel, 9, len(deps)),
        grid=(4,),
        in_specs=[whole, half, near, near, far, far, half, once(gain.shape), once(proj.shape)] + [UNREAD] * len(deps),
        out_specs=[whole, whole, pl.BlockSpec((tile, inner), lambda g: (g, 0))],
        out_shape=[
            jax.ShapeDtypeStruct((tokens, width), FLOAT),
            jax.ShapeDtypeStruct((tokens, width), BFLOAT),
            jax.ShapeDtypeStruct((tokens, inner), BFLOAT),
        ],
        compiler_params=BIG,
        cost_estimate=pl.CostEstimate(flops=10**11, bytes_accessed=0, transcendentals=0),
        name="middle",
    )(after_attn, own, *parts, cots, gain, proj, *deps)


def apart_kernel(left_ref, right_ref, *outs):
    for index, out_ref in enumerate(outs):

        @pl.when(pl.program_id(0) == index)
        def _(out_ref=out_ref):
            out_ref[...] = (left_ref[0].astype(FLOAT) + right_ref[0].astype(FLOAT)).astype(BFLOAT)


def plus_apart(left, right, *deps):
    count, *shape = left.shape
    spec = pl.BlockSpec((1, *shape), lambda g: (g,) + (0,) * len(shape))
    return pl.pallas_call(
        skipping(apart_kernel, 2, len(deps)),
        grid=(count,),
        in_specs=[spec, spec] + [UNREAD] * len(deps),
        out_specs=[pl.BlockSpec(tuple(shape), lambda g: (0,) * len(shape))] * count,
        out_shape=[jax.ShapeDtypeStruct(tuple(shape), BFLOAT)] * count,
        compiler_params=BIG,
        cost_estimate=moved(left, left, left),
        name="plus_apart",
    )(left, right, *deps)


def relay_kernel(a_ref, b_ref, c_ref, d_ref, first_ref, second_ref):
    first_ref[...] = (a_ref[...].astype(FLOAT) + b_ref[...].astype(FLOAT)).astype(BFLOAT)
    second_ref[...] = (c_ref[...].astype(FLOAT) + d_ref[...].astype(FLOAT)).astype(BFLOAT)


def relay_sums(first, second, *deps):
    shape = jax.ShapeDtypeStruct(first[0].shape, BFLOAT)
    return pl.pallas_call(
        skipping(relay_kernel, 4, len(deps)),
        in_specs=[VMEM_WHOLE] * 4 + [UNREAD] * len(deps),
        out_specs=[VMEM_WHOLE] * 2,
        out_shape=[shape, shape],
        cost_estimate=moved(*first, *second),
        name="relay_sums",
    )(*first, *second, *deps)


def plus_kernel(left_ref, *refs):
    rights, out_ref = refs[:-1], refs[-1]
    for index, right_ref in enumerate(rights):

        @pl.when(pl.program_id(0) * len(rights) // pl.num_programs(0) == index)
        def _(right_ref=right_ref):
            out_ref[0] = (left_ref[0].astype(FLOAT) + right_ref[0].astype(FLOAT)).astype(BFLOAT)


def plus(left, rights, *deps):
    shape = left.shape
    each = shape[0] // len(rights)
    spec = pl.BlockSpec((1, *shape[1:]), lambda g: (g,) + (0,) * (len(shape) - 1))

    def part(index):
        return pl.BlockSpec(
            (1, *shape[1:]), lambda g: (jnp.clip(g - index * each, 0, each - 1),) + (0,) * (len(shape) - 1)
        )

    return pl.pallas_call(
        skipping(plus_kernel, 1 + len(rights), len(deps)),
        grid=(shape[0],),
        in_specs=[spec, *[part(index) for index in range(len(rights))]] + [UNREAD] * len(deps),
        out_specs=spec,
        out_shape=jax.ShapeDtypeStruct(shape, BFLOAT),
        compiler_params=BIG,
        cost_estimate=moved(left, left, left),
        name="plus",
    )(left, *rights, *deps)


def last_kernel(dq_ref, own_ref, p1, p2, p3, x_ref, residual_ref, gain_ref, weight_ref, out_ref):
    dkv = sum(ref[...].astype(FLOAT) for ref in (own_ref, p1, p2, p3)).astype(BFLOAT)
    inner = dq_ref.shape[1]
    back = nt(dq_ref[...], weight_ref[:, :inner]) + nt(dkv, weight_ref[:, inner:])
    hidden = jnp.transpose(x_ref[0]).astype(FLOAT)
    grad = (residual_ref[...] + norm_back(hidden, gain_ref[...], back)).astype(BFLOAT)
    out_ref[0] = jnp.transpose(grad)


def last(dq, own, parts, turned, residual, gain, weight):
    seqs, width, rows = turned.shape
    inner = dq.shape[1]
    whole = pl.BlockSpec((rows, width), lambda g: (g, 0))
    piece = pl.BlockSpec((rows, 2 * inner), lambda g: (g, 0))
    block = pl.BlockSpec((1, width, rows), lambda g: (g, 0, 0))
    return pl.pallas_call(
        last_kernel,
        grid=(seqs,),
        in_specs=[
            pl.BlockSpec((rows, inner), lambda g: (g, 0)), piece, piece, piece, piece, block, whole,
            once(gain.shape), once(weight.shape),
        ],
        out_specs=block,
        out_shape=jax.ShapeDtypeStruct((seqs, width, rows), BFLOAT),
        compiler_params=BIG,
        cost_estimate=pl.CostEstimate(flops=10**11, bytes_accessed=0, transcendentals=0),
        name="input_gradient",
    )(dq, own, *parts, turned, residual, gain, weight)


def output_kernel(after_ref, parts_ref, out_ref):
    total = after_ref[...]
    for index in range(4):
        total = total + parts_ref[index].astype(FLOAT)
    out_ref[0] = jnp.transpose(total.astype(BFLOAT))


def output_sum(after_attn, parts, seqs):
    tokens, width = after_attn.shape
    rows = tokens // seqs
    return pl.pallas_call(
        output_kernel,
        grid=(seqs,),
        in_specs=[
            pl.BlockSpec((rows, width), lambda g: (g, 0)), pl.BlockSpec((4, rows, width), lambda g: (0, g, 0)),
        ],
        out_specs=pl.BlockSpec((1, width, rows), lambda g: (g, 0, 0)),
        out_shape=jax.ShapeDtypeStruct((seqs, width, rows), BFLOAT),
        compiler_params=BIG,
        cost_estimate=moved(after_attn, parts),
        name="output_sum",
    )(after_attn, parts)


def choose(refs, slot):
    value = refs[0][...]
    for index in range(1, len(refs)):
        value = jnp.where(slot == index, refs[index][...], value)
    return value


def spread_kernel(place_ref, *refs, depth, part):
    nears, fars, (gate_ref, up_ref, gate_out, up_out, late_ref) = refs[:4], refs[4:8], refs[8:]
    low = place_ref[0]
    chip, core = low // 2, lax.rem(low, 2)
    for index in range(4):
        slot = lax.bitwise_xor(chip, jnp.int32(index))
        near, far = choose(nears, slot), choose(fars, slot)
        gate = jnp.where(core == 0, near, far).astype(FLOAT)
        up = jnp.where(core == 0, far, near).astype(FLOAT)
        for level in range(depth):
            base = (level * 4 + index) * part
            gate_out[:, base : base + part] = gate[:, level * part : (level + 1) * part]
            up_out[:, base : base + part] = up[:, level * part : (level + 1) * part]
    total = gate_out[...] * gate_ref[...].astype(FLOAT) + up_out[...] * up_ref[...].astype(FLOAT)
    late_ref[...] = jnp.broadcast_to(jnp.sum(total, axis=1, keepdims=True), late_ref.shape)


def spread(place, nears, fars, gate, up, depth, part):
    shard, hidden = gate.shape
    tile = 184 if shard % 184 == 0 else shard
    pieces = pl.BlockSpec((tile, nears[0].shape[1]), lambda g: (g, 0))
    rows = pl.BlockSpec((tile, hidden), lambda g: (g, 0))
    return pl.pallas_call(
        functools.partial(spread_kernel, depth=depth, part=part),
        grid=(shard // tile,),
        in_specs=[SMEM_WHOLE, *[pieces] * 8, rows, rows],
        out_specs=[rows, rows, pl.BlockSpec((tile, 128), lambda g: (g, 0))],
        out_shape=[
            jax.ShapeDtypeStruct((shard, hidden), FLOAT),
            jax.ShapeDtypeStruct((shard, hidden), FLOAT),
            jax.ShapeDtypeStruct((shard, 128), FLOAT),
        ],
        compiler_params=BIG,
        cost_estimate=cost(flops=4 * shard * hidden, bytes_accessed=16 * shard * hidden, transcendentals=0),
        name="spread_columns",
    )(place, *nears, *fars, gate, up)


def rows_kernel(place_ref, *refs):
    nears, fars, (out_ref, scratch_ref) = refs[:4], refs[4:8], refs[8:]
    low = place_ref[0]
    size = nears[0].shape[0]

    @pl.when(pl.program_id(0) == 0)
    def _():
        for index in range(GROUP):
            gap = lax.bitwise_xor(low, jnp.int32(index))
            slot, odd = gap // 2, lax.rem(gap, 2)
            rows = jnp.where(odd == 0, choose(nears, slot), choose(fars, slot))
            scratch_ref[index * size : (index + 1) * size, :] = rows

    base = pl.multiple_of(pl.program_id(0) * 128, 128)
    out_ref[...] = jnp.transpose(scratch_ref[pl.ds(base, 128), :].astype(FLOAT))


def gathered_kernel(own_ref, *refs):
    total = own_ref[...].astype(FLOAT)
    for ref in refs[:-1]:
        total = total + ref[...].astype(FLOAT)
    refs[-1][...] = total.astype(BFLOAT)


def sum_parts(parts, *deps):
    return pl.pallas_call(
        skipping(gathered_kernel, len(parts), len(deps)),
        in_specs=[VMEM_WHOLE] * len(parts) + [UNREAD] * len(deps),
        out_specs=VMEM_WHOLE,
        out_shape=jax.ShapeDtypeStruct(parts[0].shape, BFLOAT),
        cost_estimate=moved(*parts),
        name="sum_parts",
    )(*parts, *deps)


def stack_kernel(*refs):
    for index, ref in enumerate(refs[:-1]):
        refs[-1][index] = ref[...]


def finish_kernel(
    place_ref, near_ref, far_ref, q_ref, k_ref, v_ref, q_out, k_out, v_out, proj_out, early_ref, table_ref, *, size, wide
):
    low = place_ref[0]
    shard, inner = q_ref.shape
    part = proj_out.shape[0] // 2
    each = part // 3
    for index in range(GROUP):
        gap = lax.bitwise_xor(low, jnp.int32(index))
        slot, odd = gap // 2, lax.rem(gap, 2)
        block = jnp.where(odd == 0, near_ref[slot], far_ref[slot]).astype(FLOAT)
        base = min(index * size, shard - size)
        skip = index * size - base
        q_out[base + skip : base + size, :] = block[skip:size, :inner]
        for pair in range(inner // 128):
            for offset, out_ref in enumerate((k_out, v_out)):
                column = inner + 256 * pair + 128 * offset
                out_ref[base + skip : base + size, 128 * pair : 128 * pair + 128] = block[skip:size, column : column + 128]
        if index == GROUP - 1:
            table_ref[...] = block[: table_ref.shape[0], : table_ref.shape[1]]
        column = (index // 2) * wide
        reach = min(wide, proj_out.shape[1] - column)
        for lane in range(3):
            base = (index % 2) * part + lane * each
            proj_out[base : base + each, column : column + reach] = block[size:, lane * wide : lane * wide + reach]
    total = q_out[...] * q_ref[...].astype(FLOAT) + k_out[...] * k_ref[...].astype(FLOAT)
    total = total + v_out[...] * v_ref[...].astype(FLOAT)
    early_ref[...] = jnp.broadcast_to(jnp.sum(total, axis=1, keepdims=True), early_ref.shape)


def rows_of_kernel(x_ref, cot_ref, near_ref, far_ref, rows_ref):
    rows, cut = x_ref.shape[2], near_ref.shape[0]
    for seq in range(x_ref.shape[0]):
        turned = jnp.transpose(x_ref[seq])
        start = seq * rows
        split = min(max(cut - start, 0), rows)
        if split > 0:
            near_ref[start : start + split, :] = turned[:split]
        if split < rows:
            far_ref[start + split - cut : start + rows - cut, :] = turned[split:]
        turned = jnp.transpose(cot_ref[seq])
        for copy in range(4):
            if split > 0:
                rows_ref[2 * copy, start : start + split, :] = turned[:split]
            if split < rows:
                rows_ref[2 * copy + 1, start + split - cut : start + rows - cut, :] = turned[split:]


def on_device(
    layer_input, segments, cotangent, query_weight, key_weight, value_weight, projection, gate_weight, up_weight,
    down_weight, gain_early, gain_late, bias_table,
):
    ring = lax.axis_size("ctx")
    depth = lax.axis_size("wsh")
    groups = ring // GROUP
    mine = lax.axis_index("ctx")
    low = lax.rem(mine, GROUP)
    chip, core = low // 2, lax.rem(low, 2)
    zed = lax.axis_index("wsh")
    seqs, rows, width = layer_input.shape
    inner = query_weight.shape[1]
    heads = bias_table.shape[1]
    shard = width // depth
    slab = gate_weight.shape[1] // depth
    part = slab // 4
    piece = part // 2
    tokens = seqs * rows
    cut = tokens // 2
    buckets = BUCKETS // depth
    size, wide = slice_size(shard), column_cut(width)
    each = inner // depth // 6
    upper = [[group * GROUP + index for group in range(groups)] for index in range(GROUP)]
    is_zero = core == 0
    place = jnp.stack((low, zed)).astype(jnp.int32)
    meta = mine.astype(jnp.int32).reshape(1)
    spot = jnp.stack((core, chip)).astype(jnp.int32)

    half = jax.ShapeDtypeStruct((cut, width), BFLOAT)
    chips = [[group * GROUP + 2 * index + side for index in range(4)] for group in range(groups) for side in range(2)]

    def exchange(blocks):
        return lax.all_to_all(blocks, "ctx", split_axis=0, concat_axis=0, tiled=True, axis_index_groups=chips)

    x_near, x_far, own_cots = pl.pallas_call(
        rows_of_kernel,
        in_specs=[VMEM_WHOLE] * 2,
        out_specs=[VMEM_WHOLE] * 3,
        out_shape=[half, half, jax.ShapeDtypeStruct((8, cut, width), BFLOAT)],
        compiler_params=BIG,
        cost_estimate=moved(layer_input, layer_input, cotangent, cotangent),
        name="token_rows",
    )(jnp.swapaxes(layer_input, 1, 2), jnp.swapaxes(cotangent, 1, 2))
    inputs = gather_halves((x_near, x_far))

    def columns(weight):
        return jnp.concatenate(
            [lax.dynamic_slice_in_dim(weight, index * slab + chip * part, part, 1) for index in range(depth)], axis=1
        )

    pair_slice = jnp.where(is_zero, columns(gate_weight), columns(up_weight))
    down_slice = lax.dynamic_slice_in_dim(down_weight, chip * part + core * piece, piece, 0)

    packed = pl.pallas_call(
        functools.partial(pack_kernel, size=size, wide=wide),
        in_specs=[SMEM_WHOLE] + [VMEM_WHOLE] * 7,
        out_specs=VMEM_WHOLE,
        out_shape=jax.ShapeDtypeStruct((size + each + 16, 3 * inner), BFLOAT),
        cost_estimate=moved(query_weight, query_weight),
        name="pack",
    )(
        after(place, pair_slice, down_slice), query_weight, key_weight, value_weight, projection, gain_early.reshape(1, shard), gain_late.reshape(1, shard),
        jnp.pad(bias_table, ((0, 8 - buckets), (0, 128 - heads))),
    )
    packed = lax.all_gather(packed, "wsh", axis=0)
    pair_mine = lax.all_gather(after(pair_slice, packed), "wsh", axis=0, tiled=True)
    seg_rows = jnp.pad(segments.astype(BFLOAT), ((0, 16 - seqs), (0, 3 * inner - rows)))
    small = jnp.concatenate((packed[:, : size + each].reshape(-1, 3 * inner), seg_rows), axis=0)
    small = after(small, *inputs[2:6])
    near = gather_relay(small, small.shape[0] // 32 * 16)
    far = swap(near, 1)
    down_mine = lax.all_gather(after(down_slice, near), "wsh", axis=0, tiled=True).reshape(depth, piece, width)
    qkv_full, proj_full, gains, table, segs = pl.pallas_call(
        functools.partial(unpack_kernel, depth=depth, size=size, wide=wide),
        in_specs=[SMEM_WHOLE, VMEM_WHOLE, VMEM_WHOLE, VMEM_WHOLE],
        out_specs=[VMEM_WHOLE] * 5,
        out_shape=[
            jax.ShapeDtypeStruct((width, 3 * inner), BFLOAT),
            jax.ShapeDtypeStruct((inner, width), BFLOAT),
            jax.ShapeDtypeStruct((8, width), FLOAT),
            jax.ShapeDtypeStruct((BUCKETS, 128), FLOAT),
            jax.ShapeDtypeStruct((seqs, GROUP, rows), FLOAT),
        ],
        compiler_params=BIG,
        cost_estimate=moved(near, far, near),
        name="unpack",
    )(place, packed[:, size + each :], near, far)

    def whole(value, axis=0):
        if groups == 1:
            return value
        return lax.all_gather(value, "ctx", axis=axis, tiled=True, axis_index_groups=upper)

    segs = whole(segs, 1)
    bias, mask = attention_terms(meta, table, segs, inner // 128, ring // 2)

    normed, *kv, queries = norm_project(inputs, gains[0:1], qkv_full, inner)
    cots = exchange(own_cots)
    kv = [value.reshape(1, seqs, rows, 2 * inner) for value in kv]
    queries = queries.reshape(seqs, rows, inner)
    kv = [whole(value) for value in (*kv, *[swap(value, 1) for value in kv])]
    attention, lse = attention_forward(meta, bias, mask, queries, kv)
    attn_low = attention.astype(BFLOAT).reshape(tokens, inner)
    attn = gather_direct(attn_low)

    after_attn, normed_late = late_norm(attn, inputs, proj_full, gains[1:2])
    pair_mine = after(pair_mine, attn_low)
    pair_other = swap(pair_mine, 1)
    down_mine = after(down_mine, normed_late)
    down_other = swap(down_mine, 1)
    activation, back_mine, back_other, out_part, *late_part, cot_all = feed_forward(
        spot, normed_late, cots, pair_mine, pair_other, (down_mine, down_other)
    )

    def flat(value):
        return value.reshape(4 * tokens, value.shape[2])

    def over_groups(value):
        return lax.psum(value, "ctx", axis_index_groups=upper) if groups > 1 else value

    late_own, first_near, first_far, second_near, second_far, last_near, last_far = late_part
    low, high = swap(last_near, 4), swap(last_far, 2)
    got_far, got_near = swap(first_far, 2), swap(second_near, 4)
    other_grad, mine_grad = outer_sums(normed_late, (back_other, back_mine))
    first_near, second_far = relay_sums((first_near, low), (second_far, high), mine_grad, got_far, got_near)
    late_parts = (swap(first_near, 2), got_near, got_far, swap(second_far, 4))
    other_got = [swap(other_grad[index : index + 1], 1) for index in range(2)]
    down_whole = outer_sums(activation, (cot_all,))[0]
    down_grad = down_whole.reshape(depth, 2, piece, width)
    down_keep = jnp.where(is_zero, down_grad[:, 0], down_grad[:, 1])
    down_send = jnp.where(is_zero, down_grad[:, 1], down_grad[:, 0])
    down_got = swap(down_send, 1)
    residual_grad, mix_low, attn_grad = middle(
        after_attn, late_own, late_parts, own_cots, gains[1:2], proj_full, down_whole, mine_grad
    )
    attn_grad = attn_grad.reshape(seqs, rows, inner)
    proj_grad = tn(attn_low, jnp.pad(mix_low, ((0, 0), (0, 4 * wide - width)))).astype(BFLOAT)
    dq, *dkv, table_part = attention_backward(meta, bias, mask, queries, kv, attn_grad, attention, lse)

    def owned(value):
        if groups > 1:
            value = lax.psum_scatter(value, "ctx", scatter_dimension=0, tiled=True, axis_index_groups=upper)
        return value.reshape(1, tokens, 2 * inner)

    dkv = [owned(value) for value in dkv]
    dkv_got = [swap(value, 1) for value in dkv[4:]]
    dq = dq.reshape(tokens, inner)
    pair_sum = plus(mine_grad, other_got, mix_low).reshape(width, 2 * piece * depth)
    table_sum = jnp.transpose(jnp.sum(table_part, axis=-1).reshape(heads, BUCKETS)).reshape(depth, buckets, heads)
    table_sum = jnp.pad(table_sum, ((0, 0), (0, 16 - buckets), (0, 128 - heads))).reshape(depth * 16, 128).astype(BFLOAT)
    *dkv_four, keep, send = weight_grads(place, normed, dkv[:4], dkv_got, dq, table_sum, proj_grad, depth, size, wide, pair_sum)
    down_sum = plus(down_keep, [down_got], keep).reshape(depth * piece, width)
    pair_own = over_groups(lax.psum_scatter(pair_sum, "wsh", scatter_dimension=0, tiled=True))
    down_own = over_groups(lax.psum_scatter(down_sum, "wsh", scatter_dimension=0, tiled=True))
    out_parts = exchange(after(out_part, attn_grad)).reshape(4, tokens, width)
    result = output_sum(after_attn, out_parts, seqs)

    blocks = plus_apart(keep, swap(send, 1), result)
    dkv_parts = [swap(dkv_four[index], 2 * index) for index in range(1, 4)]
    input_grad = last(dq, dkv_four[0], dkv_parts, jnp.swapaxes(layer_input, 1, 2), residual_grad, gains[0:1], qkv_full)
    levels = sum_parts([blocks[0]] + [swap(blocks[index], 2 * index) for index in range(1, 4)], input_grad, pair_own)
    pair_near = gather_direct(after(pair_own, levels))
    down_near = gather_direct(after(down_own, levels))
    total = sum_parts(
        [levels[0]] + [swap_depth(levels[gap], gap) for gap in range(1, depth)], *pair_near[1:]
    )
    grads_near = gather_direct(over_groups(total))
    pair_far, down_far = [[swap(value, 1) for value in values] for values in (pair_near, down_near)]
    gate_out, up_out, late_sum = spread(place, pair_near, pair_far, gate_weight, up_weight, depth, part)
    down_out = pl.pallas_call(
        rows_kernel,
        grid=(slab // 128,),
        in_specs=[SMEM_WHOLE] + [once((piece, width))] * 8,
        out_specs=pl.BlockSpec((width, 128), lambda g: (0, g)),
        out_shape=jax.ShapeDtypeStruct((width, slab), FLOAT),
        scratch_shapes=[pltpu.VMEM((slab, width), BFLOAT)],
        compiler_params=BIG,
        cost_estimate=moved(down_own, down_own, down_own),
        name="join_down",
    )(place, *down_near, *down_far)
    grads_near = pl.pallas_call(
        skipping(stack_kernel, 4, 1),
        in_specs=[VMEM_WHOLE] * 4 + [UNREAD],
        out_specs=VMEM_WHOLE,
        out_shape=jax.ShapeDtypeStruct((4, *total.shape), BFLOAT),
        cost_estimate=moved(total, total),
        name="stack_small",
    )(*grads_near, late_sum)
    grads_far = swap(grads_near, 1)
    column = jax.ShapeDtypeStruct((shard, inner), FLOAT)
    query_out, key_out, value_out, proj_out, early_sum, table_rows = pl.pallas_call(
        functools.partial(finish_kernel, size=size, wide=wide),
        in_specs=[SMEM_WHOLE] + [VMEM_WHOLE] * 5,
        out_specs=[VMEM_WHOLE] * 6,
        out_shape=[
            column, column, column, jax.ShapeDtypeStruct((inner // depth, width), FLOAT),
            jax.ShapeDtypeStruct((shard, 128), FLOAT), jax.ShapeDtypeStruct((buckets, heads), FLOAT),
        ],
        compiler_params=BIG,
        cost_estimate=moved(grads_near, grads_far, grads_near),
        name="finish_small",
    )(place, grads_near, grads_far, query_weight, key_weight, value_weight)

    return (
        jnp.swapaxes(result, 1, 2),
        jnp.swapaxes(input_grad, 1, 2),
        query_out,
        key_out,
        value_out,
        proj_out,
        gate_out,
        up_out,
        jnp.transpose(down_out),
        early_sum[:, 0] / gain_early.astype(FLOAT),
        late_sum[:, 0] / gain_late.astype(FLOAT),
        table_rows,
    )


def solution(mesh):
    rows = P("wsh", "ctx", None)
    split = P("wsh", None)
    vector = P("wsh")
    return jax.shard_map(
        on_device,
        mesh=mesh,
        in_specs=(rows, P("wsh", "ctx"), rows, split, split, split, split, split, split, split, vector, vector, split),
        out_specs=(rows, rows, split, split, split, split, split, split, split, vector, vector, split),
        check_vma=False,
    )
```
